512 devices in a mesh: gz: 32 (over z_hi, x, core), gy: 16 (over z_lo, y).
Axes of the slice: x: 4, y: 8, z: 8 (z_hi: 4, z_lo: 2; z = z_hi * 2 + z_lo), core: 2. Of those that a mesh axis runs over, the one named last changes fastest.
Arguments:
- filtered: bfloat16 [16, 256, 4096], P(None, 'gz', 'gy'), may hold values from -6 to 6
- angle_index: int32 [16], replicated, may hold values from 0 to 3599
- band_offset: int32 [16, 32], P(None, 'gz'), may hold values from 0 to 12, as said below
- band_length: int32 [16, 32], P(None, 'gz'), may hold values from 4 to 12
- foot_block: int32 [16, 64, 64], P(None, 'gy'), may hold values from 0 to 62, as said below
Outputs:
- denoised: float32 [64, 256, 4096], P('gy', 'gz')
The draws below stay inside these ranges and needn't reach their ends.
Inputs may be any that keep to these rules, and one draw needn't show every extreme that they name: band_offset + band_length <= 16 for every projection and group. foot_block[p, y, b] is b plus a shift of -2 to 2 that depends only on p and y, clipped to the range.
All inputs are finite; a program needn't handle non-finite values.
Results may differ from the reference program's by a relative error of at most 0.0041.
Values may be sent and summed in bfloat16 or wider, within the bound.
A program may use at most 64 MiB of HBM per device.

```python
import math
import jax
import jax.numpy as jnp
from jax import lax

X = 4096
U = 4096
Z_DEV = 8
P_SIZE = 16
NANG = 3600
BLOCK = 64
ITERS = 2
YTOT = 64
ZTOT = 256
V = 256
GROUPS = 32
XB = 64


def band_pair(key):
    folded = jax.random.fold_in(key, 11)
    key_length, key_offset = jax.random.split(folded)
    shortest = Z_DEV // 2
    longest = 3 * Z_DEV // 2
    lengths = jax.random.randint(key_length, (P_SIZE, GROUPS), shortest, longest + 1)
    lengths = lengths.at[0, 0].set(longest).at[0, 1].set(shortest)
    random_bits = jax.random.randint(key_offset, (P_SIZE, GROUPS), 0, 1048576)
    offsets = random_bits % (2 * Z_DEV - lengths + 1)
    offsets = offsets.at[0, 0].set(0).at[0, 1].set(2 * Z_DEV - shortest)
    return (offsets.astype(jnp.int32), lengths.astype(jnp.int32))


def draw_band_offset(key, part):
    return band_pair(key)[0]


def draw_band_length(key, part):
    return band_pair(key)[1]


def draw_foot_block(key, part):
    folded = jax.random.fold_in(key, 23)
    shifts = jax.random.randint(folded, (P_SIZE, YTOT), -2, 3)
    shifts = shifts.at[0, 0].set(0)
    blocks = jnp.arange(XB, dtype=jnp.int32)[None, None, :] + shifts[:, :, None]
    return jnp.clip(blocks, 0, U // BLOCK - 2).astype(jnp.int32)


def with_ends(entries, stream_key, smallest, largest):
    index_at = [jax.random.randint(jax.random.fold_in(stream_key, axis), (), 0, length) for axis, length in enumerate(entries.shape)]
    widest = entries.shape.index(max(entries.shape))
    next_to = index_at[:widest] + [(index_at[widest] + 1) % entries.shape[widest]] + index_at[widest + 1:]
    return entries.at[tuple(index_at)].set(smallest).at[tuple(next_to)].set(largest)


def block_levels(rng, shape, cuts, low, top_value):
    gain = 1.0
    for dim, shards_of in cuts:
        heights = jax.random.uniform(jax.random.fold_in(jax.random.fold_in(rng, 6), dim), (shards_of,), jnp.float32, low / len(cuts), top_value / len(cuts))
        gain = gain * jnp.repeat(jnp.exp(heights), shape[dim] // shards_of).reshape((-1,) + (1,) * (len(shape) - 1 - dim))
    return gain


def scatter_about(own_key, extent, scale, limit, cuts=(), held_as=jnp.bfloat16):
    level = block_levels(own_key, extent, cuts, -0.22, 0.18) if cuts else 1.0
    entries = jax.random.normal(own_key, extent, jnp.float32) * scale * level
    return jnp.minimum(jnp.maximum(entries, -limit), limit).astype(held_as)


def setup_inputs(seed: int = 0) -> dict:
    keys = jax.random.split(jax.random.key(seed), 6)
    return {
        "filtered": scatter_about(keys[0], (P_SIZE, V, U), 1.0, 6.0, ((1, 32), (2, 16))),
        "angle_index": with_ends(jax.random.randint(keys[1], (P_SIZE,), 0, NANG), jax.random.fold_in(keys[1], 1), 0, NANG - 1).astype(jnp.int32),
        "band_offset": draw_band_offset(jax.random.fold_in(keys[5], 71), 0),
        "band_length": draw_band_length(jax.random.fold_in(keys[5], 71), 0),
        "foot_block": draw_foot_block(jax.random.fold_in(keys[5], 71), 0),
    }


step_length = 0.25
smooth_weight = 0.3
gradient_floor = 0.01
shift_reach = 8.0

def geometry(angle_value):
    radians = 2.0 * math.pi * angle_value.astype(jnp.float32) / NANG
    stretch = 0.5 + 0.5 * jnp.abs(jnp.cos(radians))
    spread = 1.0 + jnp.abs(jnp.sin(radians))
    return (radians, stretch, spread)

def footprint(radians, stretch, spread, row_global, rows_total, block_size):
    shifted = shift_reach * jnp.sin(radians + 2.0 * math.pi * row_global / rows_total)
    inside = jnp.arange(block_size).astype(jnp.float32) - 0.5 * (block_size - 1)
    centre = block_size + inside[None, :] * stretch + shifted[:, None]
    places = jnp.arange(2 * block_size).astype(jnp.float32) + 0.5
    weights = jnp.maximum(0.0, 1.0 - jnp.abs(places[None, None, :] - centre[:, :, None]) / spread) / spread
    return weights.astype(jnp.bfloat16)

def axial_table(offsets, lengths, depth_count):
    offset_real = offsets.astype(jnp.float32)[..., None]
    length_real = lengths.astype(jnp.float32)[..., None]
    depth_place = jnp.arange(depth_count).astype(jnp.float32) + 0.5
    centre = offset_real + depth_place * length_real / depth_count
    row_number = jnp.arange(2 * depth_count).astype(jnp.int32)
    row_place = row_number.astype(jnp.float32) + 0.5
    triangle = jnp.maximum(0.0, 1.0 - jnp.abs(row_place - centre[..., None]))
    inside = (row_number >= offsets[..., None, None]) & (row_number < (offsets + lengths)[..., None, None])
    return jnp.where(inside, triangle, 0.0).astype(jnp.bfloat16)

def smooth_update(current, fidelity, row_first, depth_first, rows_total, depth_total):
    row_index = row_first + jnp.arange(current.shape[0])
    depth_index = depth_first + jnp.arange(current.shape[1])
    keep_rows = ((row_index >= 0) & (row_index < rows_total - 1)).astype(jnp.float32)[:, None, None]
    keep_depth = ((depth_index >= 0) & (depth_index < depth_total - 1)).astype(jnp.float32)[None, :, None]
    forward_rows = jnp.concatenate([current[1:] - current[:-1], jnp.zeros_like(current[:1])], 0) * keep_rows
    forward_depth = jnp.concatenate([current[:, 1:] - current[:, :-1], jnp.zeros_like(current[:, :1])], 1) * keep_depth
    forward_width = jnp.concatenate([current[:, :, 1:] - current[:, :, :-1], jnp.zeros_like(current[:, :, :1])], 2)
    magnitude = jnp.sqrt(forward_rows * forward_rows + forward_depth * forward_depth + forward_width * forward_width + gradient_floor)
    normal_rows = forward_rows / magnitude
    normal_depth = forward_depth / magnitude
    normal_width = forward_width / magnitude
    divergence = normal_rows - jnp.concatenate([jnp.zeros_like(normal_rows[:1]), normal_rows[:-1]], 0)
    divergence = divergence + normal_depth - jnp.concatenate([jnp.zeros_like(normal_depth[:, :1]), normal_depth[:, :-1]], 1)
    divergence = divergence + normal_width - jnp.concatenate([jnp.zeros_like(normal_width[:, :, :1]), normal_width[:, :, :-1]], 2)
    return current + step_length * (smooth_weight * divergence - (current - fidelity))

def reference(filtered, angle_index, band_offset, band_length, foot_block):
    half_band = Z_DEV // 2
    padded = jnp.pad(filtered, ((0, 0), (half_band, half_band), (0, 0)))
    row_pick = (jnp.arange(GROUPS) * Z_DEV)[:, None] + jnp.arange(2 * Z_DEV)[None, :]
    row_global = jnp.arange(YTOT).astype(jnp.float32)

    def one_projection(running, inputs):
        projection, angle_value, offsets, lengths, blocks = inputs
        radians, stretch, spread = geometry(angle_value)
        axial_weights = axial_table(offsets, lengths, Z_DEV)
        band_rows = projection[row_pick]
        columns = jnp.einsum('gzv,gvu->gzu', axial_weights.astype(jnp.float32), band_rows.astype(jnp.float32))
        columns = columns.astype(jnp.bfloat16).reshape(ZTOT, U)
        weights = footprint(radians, stretch, spread, row_global, YTOT, BLOCK)
        column_tiles = columns.reshape(ZTOT, U // BLOCK, BLOCK)

        def one_row(row_inputs):
            row_weights, row_blocks = row_inputs
            window = jnp.concatenate([column_tiles[:, row_blocks], column_tiles[:, row_blocks + 1]], axis=-1)
            product = jnp.einsum('iu,zbu->zbi', row_weights.astype(jnp.float32), window.astype(jnp.float32))
            return product.reshape(ZTOT, X)
        return (running + lax.map(one_row, (weights, blocks)), None)
    initial = jnp.zeros((YTOT, ZTOT, X), jnp.float32)
    summed, _unused = lax.scan(one_projection, initial, (padded, angle_index, band_offset, band_length, foot_block))
    backprojection = math.pi / P_SIZE * summed
    current = backprojection
    for turn_index in range(ITERS):
        current = smooth_update(current, backprojection, 0, 0, YTOT, ZTOT)
    return current
```

```python
import math

import jax
import jax.numpy as jnp
from jax import lax
from jax.sharding import PartitionSpec as P

X = 4096
P_SIZE = 16
NANG = 3600
BLOCK = 64
ITERS = 2


step_length = 0.25
smooth_weight = 0.3
gradient_floor = 0.01
shift_reach = 8.0


def with_halo(cells, sides, width):
    for axis, dim in sides:
        count = lax.axis_size(axis)
        ends = count - 1
        head = lax.slice_in_dim(cells, 0, width, axis=dim)
        tail = lax.slice_in_dim(cells, cells.shape[dim] - width, cells.shape[dim], axis=dim)
        cells = jnp.concatenate(
            [
                lax.ppermute(tail, axis, [(i, (i + 1) % count) for i in range(ends)]),
                cells,
                lax.ppermute(head, axis, [((i + 1) % count, i) for i in range(ends)]),
            ],
            axis=dim,
        )
    return cells


def geometry(angle_value):
    radians = 2.0 * math.pi * angle_value.astype(jnp.float32) / NANG
    stretch = 0.5 + 0.5 * jnp.abs(jnp.cos(radians))
    spread = 1.0 + jnp.abs(jnp.sin(radians))
    return (radians, stretch, spread)


def footprint(radians, stretch, spread, row_global, rows_total, block_size):
    shifted = shift_reach * jnp.sin(radians + 2.0 * math.pi * row_global / rows_total)
    inside = jnp.arange(block_size).astype(jnp.float32) - 0.5 * (block_size - 1)
    centre = block_size + inside[None, :] * stretch + shifted[:, None]
    places = jnp.arange(2 * block_size).astype(jnp.float32) + 0.5
    weights = (
        jnp.maximum(0.0, 1.0 - jnp.abs(places[None, None, :] - centre[:, :, None]) / spread)
        / spread
    )
    return weights.astype(jnp.bfloat16)


def axial_table(offsets, lengths, depth_count):
    offset_real = offsets.astype(jnp.float32)[..., None]
    length_real = lengths.astype(jnp.float32)[..., None]
    depth_place = jnp.arange(depth_count).astype(jnp.float32) + 0.5
    centre = offset_real + depth_place * length_real / depth_count
    row_number = jnp.arange(2 * depth_count)
    row_place = row_number.astype(jnp.float32) + 0.5
    triangle = jnp.maximum(0.0, 1.0 - jnp.abs(row_place - centre[..., None]))
    inside = (row_number >= offsets[..., None, None]) & (
        row_number < (offsets + lengths)[..., None, None]
    )
    return jnp.where(inside, triangle, 0.0).astype(jnp.bfloat16)


def smooth_update(current, fidelity, row_first, depth_first, rows_total, depth_total):
    row_index = row_first + jnp.arange(current.shape[0])
    depth_index = depth_first + jnp.arange(current.shape[1])
    keep_rows = ((row_index >= 0) & (row_index < rows_total - 1)).astype(jnp.float32)[:, None, None]
    keep_depth = ((depth_index >= 0) & (depth_index < depth_total - 1)).astype(jnp.float32)[
        None, :, None
    ]
    forward_rows = (
        jnp.concatenate([current[1:] - current[:-1], jnp.zeros_like(current[:1])], 0) * keep_rows
    )
    forward_depth = (
        jnp.concatenate([current[:, 1:] - current[:, :-1], jnp.zeros_like(current[:, :1])], 1)
        * keep_depth
    )
    forward_width = jnp.concatenate(
        [current[:, :, 1:] - current[:, :, :-1], jnp.zeros_like(current[:, :, :1])], 2
    )
    magnitude = jnp.sqrt(
        forward_rows * forward_rows
        + forward_depth * forward_depth
        + forward_width * forward_width
        + gradient_floor
    )
    normal_rows = forward_rows / magnitude
    normal_depth = forward_depth / magnitude
    normal_width = forward_width / magnitude
    divergence = normal_rows - jnp.concatenate(
        [jnp.zeros_like(normal_rows[:1]), normal_rows[:-1]], 0
    )
    divergence = (
        divergence
        + normal_depth
        - jnp.concatenate([jnp.zeros_like(normal_depth[:, :1]), normal_depth[:, :-1]], 1)
    )
    divergence = (
        divergence
        + normal_width
        - jnp.concatenate([jnp.zeros_like(normal_width[:, :, :1]), normal_width[:, :, :-1]], 2)
    )
    return current + step_length * (smooth_weight * divergence - (current - fidelity))


def per_device(filtered, angle_index, band_offset, band_length, foot_block):
    depth_count = filtered.shape[1]
    row_count = foot_block.shape[1]
    extended_band = with_halo(filtered, (("gz", 1),), depth_count // 2)
    axial_weights = axial_table(band_offset[:, 0], band_length[:, 0], depth_count)
    summed_rows = jnp.einsum(
        "pzv,pvu->pzu",
        axial_weights,
        extended_band,
        preferred_element_type=jnp.float32,
    )
    columns = lax.all_gather(summed_rows.astype(jnp.bfloat16), "gy", axis=2, tiled=True)
    column_count = columns.shape[2]
    row_base = lax.axis_index("gy") * row_count
    depth_base = lax.axis_index("gz") * depth_count
    rows_total = lax.axis_size("gy") * row_count
    depth_total = lax.axis_size("gz") * depth_count
    row_global = (row_base + jnp.arange(row_count)).astype(jnp.float32)

    def one_projection(running, inputs):
        projected, angle_value, blocks = inputs
        radians, stretch, spread = geometry(angle_value)
        weights = footprint(radians, stretch, spread, row_global, rows_total, BLOCK)
        column_tiles = projected.reshape(depth_count, column_count // BLOCK, BLOCK)
        window = jnp.concatenate([column_tiles[:, blocks], column_tiles[:, blocks + 1]], axis=-1)
        product = jnp.einsum("yiu,zybu->yzbi", weights, window, preferred_element_type=jnp.float32)
        return (running + product.reshape(running.shape), None)

    initial = jnp.zeros((row_count, depth_count, X), jnp.float32)
    summed, _unused = lax.scan(one_projection, initial, (columns, angle_index, foot_block))
    backprojection = math.pi / P_SIZE * summed
    current = backprojection
    padded_fidelity = jnp.pad(backprojection, ((1, 1), (1, 1), (0, 0)))
    for turn_index in range(ITERS):
        extended = with_halo(current, (("gz", 1), ("gy", 0)), 1)
        updated = smooth_update(
            extended, padded_fidelity, row_base - 1, depth_base - 1, rows_total, depth_total
        )
        current = updated[1:-1, 1:-1]
    return current


def solution(mesh):
    return jax.shard_map(
        per_device,
        mesh=mesh,
        in_specs=(P(None, "gz", "gy"), P(), P(None, "gz"), P(None, "gz"), P(None, "gy", None)),
        out_specs=P("gy", "gz", None),
        check_vma=False,
    )
```

```python
import functools
import math

import jax
import jax.numpy as jnp
from jax import lax
from jax.experimental import pallas as pl
from jax.experimental.pallas import tpu as pltpu
from jax.sharding import PartitionSpec as P

X = 4096
P_SIZE = 16
NANG = 3600
BLOCK = 64
ITERS = 2


step_length = 0.25
smooth_weight = 0.3
gradient_floor = 0.01
shift_reach = 8.0


def with_halo(cells, sides, width):
    for axis, dim in sides:
        count = lax.axis_size(axis)
        ends = count - 1
        head = lax.slice_in_dim(cells, 0, width, axis=dim)
        tail = lax.slice_in_dim(cells, cells.shape[dim] - width, cells.shape[dim], axis=dim)
        cells = jnp.concatenate(
            [
                lax.ppermute(tail, axis, [(i, (i + 1) % count) for i in range(ends)]),
                cells,
                lax.ppermute(head, axis, [((i + 1) % count, i) for i in range(ends)]),
            ],
            axis=dim,
        )
    return cells


def gather_kernel(count, local_ref, out_ref, send_sem, recv_sem, own_sem):
    me = lax.axis_index("gy")
    depth_index = lax.axis_index("gz")
    width = local_ref.shape[2]
    barrier = pltpu.get_barrier_semaphore()
    for step in range(1, count):
        peer = lax.rem(me + step, count)
        pl.semaphore_signal(
            barrier, inc=1, device_id=(depth_index, peer), device_id_type=pl.DeviceIdType.MESH
        )
    pl.semaphore_wait(barrier, count - 1)
    own_slot = pl.ds(pl.multiple_of(me * width, width), width)
    own = pltpu.make_async_copy(local_ref, out_ref.at[:, :, own_slot], own_sem)
    own.start()
    sends = []
    for step in range(1, count):
        peer = lax.rem(me + step, count)
        copy = pltpu.make_async_remote_copy(
            src_ref=local_ref,
            dst_ref=out_ref.at[:, :, own_slot],
            send_sem=send_sem.at[step],
            recv_sem=recv_sem.at[step],
            device_id=(depth_index, peer),
            device_id_type=pl.DeviceIdType.MESH,
        )
        copy.start()
        sends.append(copy)
    own.wait()
    for copy in sends:
        copy.wait_send()
    for step in range(1, count):
        sender = lax.rem(me + count - step, count)
        slot = pl.ds(pl.multiple_of(sender * width, width), width)
        arriving = pltpu.make_async_remote_copy(
            src_ref=local_ref,
            dst_ref=out_ref.at[:, :, slot],
            send_sem=send_sem.at[step],
            recv_sem=recv_sem.at[step],
            device_id=(depth_index, sender),
            device_id_type=pl.DeviceIdType.MESH,
        )
        arriving.wait_recv()


def gather_columns(local):
    count = lax.axis_size("gy")
    rows, depth, width = local.shape
    return pl.pallas_call(
        functools.partial(gather_kernel, count),
        out_shape=jax.ShapeDtypeStruct((rows, depth, width * count), local.dtype),
        in_specs=[pl.BlockSpec(memory_space=pl.ANY)],
        out_specs=pl.BlockSpec(memory_space=pl.ANY),
        scratch_shapes=[
            pltpu.SemaphoreType.DMA((count,)),
            pltpu.SemaphoreType.DMA((count,)),
            pltpu.SemaphoreType.DMA(()),
        ],
        compiler_params=pltpu.CompilerParams(collective_id=0, has_side_effects=True),
    )(local)


def geometry(angle_value):
    radians = 2.0 * math.pi * angle_value.astype(jnp.float32) / NANG
    stretch = 0.5 + 0.5 * jnp.abs(jnp.cos(radians))
    spread = 1.0 + jnp.abs(jnp.sin(radians))
    return (radians, stretch, spread)


def footprint(radians, stretch, spread, row_global, rows_total, block_size):
    shifted = shift_reach * jnp.sin(radians + 2.0 * math.pi * row_global / rows_total)
    inside = jnp.arange(block_size).astype(jnp.float32) - 0.5 * (block_size - 1)
    centre = block_size + inside[None, :] * stretch + shifted[:, None]
    places = jnp.arange(2 * block_size).astype(jnp.float32) + 0.5
    weights = (
        jnp.maximum(0.0, 1.0 - jnp.abs(places[None, None, :] - centre[:, :, None]) / spread)
        / spread
    )
    return weights.astype(jnp.bfloat16)


def axial_table(offsets, lengths, depth_count):
    offset_real = offsets.astype(jnp.float32)[..., None]
    length_real = lengths.astype(jnp.float32)[..., None]
    depth_place = jnp.arange(depth_count).astype(jnp.float32) + 0.5
    centre = offset_real + depth_place * length_real / depth_count
    row_number = jnp.arange(2 * depth_count)
    row_place = row_number.astype(jnp.float32) + 0.5
    triangle = jnp.maximum(0.0, 1.0 - jnp.abs(row_place - centre[..., None]))
    inside = (row_number >= offsets[..., None, None]) & (
        row_number < (offsets + lengths)[..., None, None]
    )
    return jnp.where(inside, triangle, 0.0).astype(jnp.bfloat16)


def smooth_update(current, fidelity, row_first, depth_first, rows_total, depth_total):
    row_index = row_first + jnp.arange(current.shape[0])
    depth_index = depth_first + jnp.arange(current.shape[1])
    keep_rows = ((row_index >= 0) & (row_index < rows_total - 1)).astype(jnp.float32)[:, None, None]
    keep_depth = ((depth_index >= 0) & (depth_index < depth_total - 1)).astype(jnp.float32)[
        None, :, None
    ]
    forward_rows = (
        jnp.concatenate([current[1:] - current[:-1], jnp.zeros_like(current[:1])], 0) * keep_rows
    )
    forward_depth = (
        jnp.concatenate([current[:, 1:] - current[:, :-1], jnp.zeros_like(current[:, :1])], 1)
        * keep_depth
    )
    forward_width = jnp.concatenate(
        [current[:, :, 1:] - current[:, :, :-1], jnp.zeros_like(current[:, :, :1])], 2
    )
    magnitude = jnp.sqrt(
        forward_rows * forward_rows
        + forward_depth * forward_depth
        + forward_width * forward_width
        + gradient_floor
    )
    normal_rows = forward_rows / magnitude
    normal_depth = forward_depth / magnitude
    normal_width = forward_width / magnitude
    divergence = normal_rows - jnp.concatenate(
        [jnp.zeros_like(normal_rows[:1]), normal_rows[:-1]], 0
    )
    divergence = (
        divergence
        + normal_depth
        - jnp.concatenate([jnp.zeros_like(normal_depth[:, :1]), normal_depth[:, :-1]], 1)
    )
    divergence = (
        divergence
        + normal_width
        - jnp.concatenate([jnp.zeros_like(normal_width[:, :, :1]), normal_width[:, :, :-1]], 2)
    )
    return current + step_length * (smooth_weight * divergence - (current - fidelity))


def per_device(filtered, angle_index, band_offset, band_length, foot_block):
    depth_count = filtered.shape[1]
    row_count = foot_block.shape[1]
    extended_band = with_halo(filtered, (("gz", 1),), depth_count // 2)
    axial_weights = axial_table(band_offset[:, 0], band_length[:, 0], depth_count)
    summed_rows = jnp.einsum(
        "pzv,pvu->pzu",
        axial_weights,
        extended_band,
        preferred_element_type=jnp.float32,
    )
    columns = gather_columns(summed_rows.astype(jnp.bfloat16))
    column_count = columns.shape[2]
    row_base = lax.axis_index("gy") * row_count
    depth_base = lax.axis_index("gz") * depth_count
    rows_total = lax.axis_size("gy") * row_count
    depth_total = lax.axis_size("gz") * depth_count
    row_global = (row_base + jnp.arange(row_count)).astype(jnp.float32)

    def one_projection(running, inputs):
        projected, angle_value, blocks = inputs
        radians, stretch, spread = geometry(angle_value)
        weights = footprint(radians, stretch, spread, row_global, rows_total, BLOCK)
        column_tiles = projected.reshape(depth_count, column_count // BLOCK, BLOCK)
        window = jnp.concatenate([column_tiles[:, blocks], column_tiles[:, blocks + 1]], axis=-1)
        product = jnp.einsum("yiu,zybu->yzbi", weights, window, preferred_element_type=jnp.float32)
        return (running + product.reshape(running.shape), None)

    initial = jnp.zeros((row_count, depth_count, X), jnp.float32)
    summed, _unused = lax.scan(one_projection, initial, (columns, angle_index, foot_block))
    backprojection = math.pi / P_SIZE * summed
    current = backprojection
    padded_fidelity = jnp.pad(backprojection, ((1, 1), (1, 1), (0, 0)))
    for turn_index in range(ITERS):
        extended = with_halo(current, (("gz", 1), ("gy", 0)), 1)
        updated = smooth_update(
            extended, padded_fidelity, row_base - 1, depth_base - 1, rows_total, depth_total
        )
        current = updated[1:-1, 1:-1]
    return current


def solution(mesh):
    return jax.shard_map(
        per_device,
        mesh=mesh,
        in_specs=(P(None, "gz", "gy"), P(), P(None, "gz"), P(None, "gz"), P(None, "gy", None)),
        out_specs=P("gy", "gz", None),
        check_vma=False,
    )
```

```python
import functools
import math

import jax
import jax.numpy as jnp
from jax import lax
from jax.experimental import pallas as pl
from jax.experimental.pallas import tpu as pltpu
from jax.sharding import PartitionSpec as P

X = 4096
P_SIZE = 16
NANG = 3600
BLOCK = 64
LANES = 128
ITERS = 2


step_length = 0.25
smooth_weight = 0.3
gradient_floor = 0.01
shift_reach = 8.0


def with_halo(cells, sides, width):
    for axis, dim in sides:
        count = lax.axis_size(axis)
        ends = count - 1
        head = lax.slice_in_dim(cells, 0, width, axis=dim)
        tail = lax.slice_in_dim(cells, cells.shape[dim] - width, cells.shape[dim], axis=dim)
        cells = jnp.concatenate(
            [
                lax.ppermute(tail, axis, [(i, (i + 1) % count) for i in range(ends)]),
                cells,
                lax.ppermute(head, axis, [((i + 1) % count, i) for i in range(ends)]),
            ],
            axis=dim,
        )
    return cells


def gather_kernel(count, local_ref, out_ref, send_sem, recv_sem, own_sem):
    me = lax.axis_index("gy")
    depth_index = lax.axis_index("gz")
    width = local_ref.shape[2]
    barrier = pltpu.get_barrier_semaphore()
    for step in range(1, count):
        peer = lax.rem(me + step, count)
        pl.semaphore_signal(
            barrier, inc=1, device_id=(depth_index, peer), device_id_type=pl.DeviceIdType.MESH
        )
    pl.semaphore_wait(barrier, count - 1)
    own_slot = pl.ds(pl.multiple_of(me * width, width), width)
    own = pltpu.make_async_copy(local_ref, out_ref.at[:, :, own_slot], own_sem)
    own.start()
    sends = []
    for step in range(1, count):
        peer = lax.rem(me + step, count)
        copy = pltpu.make_async_remote_copy(
            src_ref=local_ref,
            dst_ref=out_ref.at[:, :, own_slot],
            send_sem=send_sem.at[step],
            recv_sem=recv_sem.at[step],
            device_id=(depth_index, peer),
            device_id_type=pl.DeviceIdType.MESH,
        )
        copy.start()
        sends.append(copy)
    own.wait()
    for copy in sends:
        copy.wait_send()
    for step in range(1, count):
        sender = lax.rem(me + count - step, count)
        slot = pl.ds(pl.multiple_of(sender * width, width), width)
        arriving = pltpu.make_async_remote_copy(
            src_ref=local_ref,
            dst_ref=out_ref.at[:, :, slot],
            send_sem=send_sem.at[step],
            recv_sem=recv_sem.at[step],
            device_id=(depth_index, sender),
            device_id_type=pl.DeviceIdType.MESH,
        )
        arriving.wait_recv()


def gather_columns(local):
    count = lax.axis_size("gy")
    rows, depth, width = local.shape
    return pl.pallas_call(
        functools.partial(gather_kernel, count),
        out_shape=jax.ShapeDtypeStruct((rows, depth, width * count), local.dtype),
        in_specs=[pl.BlockSpec(memory_space=pl.ANY)],
        out_specs=pl.BlockSpec(memory_space=pl.ANY),
        scratch_shapes=[
            pltpu.SemaphoreType.DMA((count,)),
            pltpu.SemaphoreType.DMA((count,)),
            pltpu.SemaphoreType.DMA(()),
        ],
        compiler_params=pltpu.CompilerParams(collective_id=0, has_side_effects=True),
    )(local)


def geometry(angle_value):
    radians = 2.0 * math.pi * angle_value.astype(jnp.float32) / NANG
    stretch = 0.5 + 0.5 * jnp.abs(jnp.cos(radians))
    spread = 1.0 + jnp.abs(jnp.sin(radians))
    return (radians, stretch, spread)


def footprint(radians, stretch, spread, row_global, rows_total, block_size):
    shifted = shift_reach * jnp.sin(radians + 2.0 * math.pi * row_global / rows_total)
    inside = jnp.arange(block_size).astype(jnp.float32) - 0.5 * (block_size - 1)
    centre = block_size + inside[None, :] * stretch + shifted[:, None]
    places = jnp.arange(2 * block_size).astype(jnp.float32) + 0.5
    weights = (
        jnp.maximum(0.0, 1.0 - jnp.abs(places[None, None, :] - centre[:, :, None]) / spread)
        / spread
    )
    return weights.astype(jnp.bfloat16)


def axial_table(offsets, lengths, depth_count):
    offset_real = offsets.astype(jnp.float32)[..., None]
    length_real = lengths.astype(jnp.float32)[..., None]
    depth_place = jnp.arange(depth_count).astype(jnp.float32) + 0.5
    centre = offset_real + depth_place * length_real / depth_count
    row_number = jnp.arange(2 * depth_count)
    row_place = row_number.astype(jnp.float32) + 0.5
    triangle = jnp.maximum(0.0, 1.0 - jnp.abs(row_place - centre[..., None]))
    inside = (row_number >= offsets[..., None, None]) & (
        row_number < (offsets + lengths)[..., None, None]
    )
    return jnp.where(inside, triangle, 0.0).astype(jnp.bfloat16)


def smooth_update(current, fidelity, row_first, depth_first, rows_total, depth_total):
    row_index = row_first + jnp.arange(current.shape[0])
    depth_index = depth_first + jnp.arange(current.shape[1])
    keep_rows = ((row_index >= 0) & (row_index < rows_total - 1)).astype(jnp.float32)[:, None, None]
    keep_depth = ((depth_index >= 0) & (depth_index < depth_total - 1)).astype(jnp.float32)[
        None, :, None
    ]
    forward_rows = (
        jnp.concatenate([current[1:] - current[:-1], jnp.zeros_like(current[:1])], 0) * keep_rows
    )
    forward_depth = (
        jnp.concatenate([current[:, 1:] - current[:, :-1], jnp.zeros_like(current[:, :1])], 1)
        * keep_depth
    )
    forward_width = jnp.concatenate(
        [current[:, :, 1:] - current[:, :, :-1], jnp.zeros_like(current[:, :, :1])], 2
    )
    magnitude = jnp.sqrt(
        forward_rows * forward_rows
        + forward_depth * forward_depth
        + forward_width * forward_width
        + gradient_floor
    )
    normal_rows = forward_rows / magnitude
    normal_depth = forward_depth / magnitude
    normal_width = forward_width / magnitude
    divergence = normal_rows - jnp.concatenate(
        [jnp.zeros_like(normal_rows[:1]), normal_rows[:-1]], 0
    )
    divergence = (
        divergence
        + normal_depth
        - jnp.concatenate([jnp.zeros_like(normal_depth[:, :1]), normal_depth[:, :-1]], 1)
    )
    divergence = (
        divergence
        + normal_width
        - jnp.concatenate([jnp.zeros_like(normal_width[:, :, :1]), normal_width[:, :, :-1]], 2)
    )
    return current + step_length * (smooth_weight * divergence - (current - fidelity))


def footprint_mats(angle_value, shift, row_global, rows_total):
    radians, stretch, spread = geometry(angle_value)
    shifted = shift_reach * jnp.sin(radians + 2.0 * math.pi * row_global / rows_total)
    inside = jnp.arange(BLOCK).astype(jnp.float32) - 0.5 * (BLOCK - 1)
    centre = BLOCK + inside[None, :] * stretch + shifted[:, None]
    centre = jnp.concatenate([centre, centre], axis=1)
    parity = shift - 2 * ((shift + 2) // 2 - 1)
    half = (jnp.arange(LANES) >= BLOCK).astype(jnp.int32)
    place = jnp.arange(LANES)[:, None]
    taps = jnp.stack(
        [
            place - BLOCK * (half[None, None, :] + parity[:, None, None]),
            place + LANES - BLOCK * (half[None, None, :] + parity[:, None, None]),
            jnp.broadcast_to(place, (LANES, LANES))[None].repeat(shift.shape[0], 0),
        ],
        axis=1,
    )
    places = taps.astype(jnp.float32) + 0.5
    weights = (
        jnp.maximum(0.0, 1.0 - jnp.abs(places - centre[:, None, None, :]) / spread) / spread
    )
    valid = (taps >= 0) & (taps < 2 * BLOCK)
    return jnp.where(valid, weights, 0.0).astype(jnp.bfloat16)


def backproject_kernel(shift_ref, tiles_ref, mats_ref, out_ref):
    p = pl.program_id(0)
    tile_count = out_ref.shape[2] // LANES
    depth_count = out_ref.shape[1]

    @pl.when(p == 0)
    def _():
        out_ref[...] = jnp.zeros_like(out_ref)

    ends = jnp.concatenate([tiles_ref[0, 1], tiles_ref[0, tile_count]], axis=0).astype(jnp.bfloat16)
    for row in range(out_ref.shape[0]):
        shift = shift_ref[p, row]
        start = (shift + 2) // 2
        low = tiles_ref[0, pl.ds(start, tile_count)].reshape(tile_count * depth_count, LANES)
        high = tiles_ref[0, pl.ds(start + 1, tile_count)].reshape(tile_count * depth_count, LANES)
        result = jnp.dot(
            low.astype(jnp.bfloat16), mats_ref[0, row, 0], preferred_element_type=jnp.float32
        ) + jnp.dot(
            high.astype(jnp.bfloat16), mats_ref[0, row, 1], preferred_element_type=jnp.float32
        )
        edge = jnp.dot(ends, mats_ref[0, row, 2], preferred_element_type=jnp.float32)
        shift_vec = jnp.full((depth_count, LANES), shift, jnp.int32)
        for tile in range(tile_count):
            part = result[tile * depth_count:(tile + 1) * depth_count]
            if tile == 0:
                part = jnp.where(shift_vec < 0, edge[:depth_count], part)
            elif tile == tile_count - 2:
                part = jnp.where(shift_vec >= 2, edge[depth_count:], part)
            elif tile == tile_count - 1:
                part = jnp.where(shift_vec >= 0, edge[depth_count:], part)
            lanes = pl.ds(tile * LANES, LANES)
            out_ref[row, :, lanes] = out_ref[row, :, lanes] + part


def backproject(shifts, tiles, mats, column_count):
    count, rows = shifts.shape
    depth_count = tiles.shape[2]
    return pl.pallas_call(
        backproject_kernel,
        out_shape=jax.ShapeDtypeStruct((rows, depth_count, column_count), jnp.float32),
        grid_spec=pltpu.PrefetchScalarGridSpec(
            num_scalar_prefetch=1,
            grid=(count,),
            in_specs=[
                pl.BlockSpec((1,) + tiles.shape[1:], lambda p, s: (p, 0, 0, 0)),
                pl.BlockSpec((1,) + mats.shape[1:], lambda p, s: (p, 0, 0, 0, 0)),
            ],
            out_specs=pl.BlockSpec((rows, depth_count, column_count), lambda p, s: (0, 0, 0)),
        ),
        compiler_params=pltpu.CompilerParams(dimension_semantics=("arbitrary",)),
    )(shifts, tiles, mats)


def per_device(filtered, angle_index, band_offset, band_length, foot_block):
    depth_count = filtered.shape[1]
    row_count = foot_block.shape[1]
    extended_band = with_halo(filtered, (("gz", 1),), depth_count // 2)
    axial_weights = axial_table(band_offset[:, 0], band_length[:, 0], depth_count)
    summed_rows = jnp.einsum(
        "pzv,pvu->pzu",
        axial_weights,
        extended_band,
        preferred_element_type=jnp.float32,
    )
    columns = gather_columns(summed_rows.astype(jnp.bfloat16))
    column_count = columns.shape[2]
    row_base = lax.axis_index("gy") * row_count
    depth_base = lax.axis_index("gz") * depth_count
    rows_total = lax.axis_size("gy") * row_count
    depth_total = lax.axis_size("gz") * depth_count
    row_global = (row_base + jnp.arange(row_count)).astype(jnp.float32)
    shifts = foot_block[:, :, 2] - 2
    mats = jax.vmap(footprint_mats, in_axes=(0, 0, None, None))(
        angle_index, shifts, row_global, rows_total
    )
    tile_count = column_count // LANES
    tiles = columns.astype(jnp.float32).reshape(P_SIZE, depth_count, tile_count, LANES)
    tiles = jnp.pad(tiles.transpose(0, 2, 1, 3), ((0, 0), (1, 2), (0, 0), (0, 0)))
    summed = backproject(shifts, tiles, mats, column_count)
    backprojection = math.pi / P_SIZE * summed
    current = backprojection
    padded_fidelity = jnp.pad(backprojection, ((1, 1), (1, 1), (0, 0)))
    for turn_index in range(ITERS):
        extended = with_halo(current, (("gz", 1), ("gy", 0)), 1)
        updated = smooth_update(
            extended, padded_fidelity, row_base - 1, depth_base - 1, rows_total, depth_total
        )
        current = updated[1:-1, 1:-1]
    return current


def solution(mesh):
    return jax.shard_map(
        per_device,
        mesh=mesh,
        in_specs=(P(None, "gz", "gy"), P(), P(None, "gz"), P(None, "gz"), P(None, "gy", None)),
        out_specs=P("gy", "gz", None),
        check_vma=False,
    )
```

```python
import functools
import math

import jax
import jax.numpy as jnp
from jax import lax
from jax.experimental import pallas as pl
from jax.experimental.pallas import tpu as pltpu
from jax.sharding import PartitionSpec as P

X = 4096
P_SIZE = 16
NANG = 3600
BLOCK = 64
LANES = 128
ITERS = 2


step_length = 0.25
smooth_weight = 0.3
gradient_floor = 0.01
shift_reach = 8.0


def with_halo(cells, sides, width):
    for axis, dim in sides:
        count = lax.axis_size(axis)
        ends = count - 1
        head = lax.slice_in_dim(cells, 0, width, axis=dim)
        tail = lax.slice_in_dim(cells, cells.shape[dim] - width, cells.shape[dim], axis=dim)
        cells = jnp.concatenate(
            [
                lax.ppermute(tail, axis, [(i, (i + 1) % count) for i in range(ends)]),
                cells,
                lax.ppermute(head, axis, [((i + 1) % count, i) for i in range(ends)]),
            ],
            axis=dim,
        )
    return cells


def gather_kernel(count, local_ref, out_ref, send_sem, recv_sem, own_sem):
    me = lax.axis_index("gy")
    depth_index = lax.axis_index("gz")
    width = local_ref.shape[2]
    barrier = pltpu.get_barrier_semaphore()
    for step in range(1, count):
        peer = lax.rem(me + step, count)
        pl.semaphore_signal(
            barrier, inc=1, device_id=(depth_index, peer), device_id_type=pl.DeviceIdType.MESH
        )
    pl.semaphore_wait(barrier, count - 1)
    own_slot = pl.ds(pl.multiple_of(me * width, width), width)
    own = pltpu.make_async_copy(local_ref, out_ref.at[:, :, own_slot], own_sem)
    own.start()
    sends = []
    for step in range(1, count):
        peer = lax.rem(me + step, count)
        copy = pltpu.make_async_remote_copy(
            src_ref=local_ref,
            dst_ref=out_ref.at[:, :, own_slot],
            send_sem=send_sem.at[step],
            recv_sem=recv_sem.at[step],
            device_id=(depth_index, peer),
            device_id_type=pl.DeviceIdType.MESH,
        )
        copy.start()
        sends.append(copy)
    own.wait()
    for copy in sends:
        copy.wait_send()
    for step in range(1, count):
        sender = lax.rem(me + count - step, count)
        slot = pl.ds(pl.multiple_of(sender * width, width), width)
        arriving = pltpu.make_async_remote_copy(
            src_ref=local_ref,
            dst_ref=out_ref.at[:, :, slot],
            send_sem=send_sem.at[step],
            recv_sem=recv_sem.at[step],
            device_id=(depth_index, sender),
            device_id_type=pl.DeviceIdType.MESH,
        )
        arriving.wait_recv()


def gather_columns(local):
    count = lax.axis_size("gy")
    rows, depth, width = local.shape
    return pl.pallas_call(
        functools.partial(gather_kernel, count),
        out_shape=jax.ShapeDtypeStruct((rows, depth, width * count), local.dtype),
        in_specs=[pl.BlockSpec(memory_space=pl.ANY)],
        out_specs=pl.BlockSpec(memory_space=pl.ANY),
        scratch_shapes=[
            pltpu.SemaphoreType.DMA((count,)),
            pltpu.SemaphoreType.DMA((count,)),
            pltpu.SemaphoreType.DMA(()),
        ],
        compiler_params=pltpu.CompilerParams(collective_id=0, has_side_effects=True),
    )(local)


def with_wide_halo(cells, width):
    rows, depth = cells.shape[0], cells.shape[1]
    row_count = lax.axis_size("gy")
    depth_count = lax.axis_size("gz")

    def moved(piece, row_step, depth_step):
        pairs = []
        for a in range(depth_count):
            for b in range(row_count):
                ta, tb = a + depth_step, b + row_step
                if 0 <= ta < depth_count and 0 <= tb < row_count:
                    pairs.append((a * row_count + b, ta * row_count + tb))
        return lax.ppermute(piece, ("gz", "gy"), pairs)

    head_rows, tail_rows = slice(0, width), slice(rows - width, rows)
    head_depth, tail_depth = slice(0, width), slice(depth - width, depth)
    whole = slice(None)
    parts = {}
    for row_step, row_part in ((1, tail_rows), (0, whole), (-1, head_rows)):
        for depth_step, depth_part in ((1, tail_depth), (0, whole), (-1, head_depth)):
            if row_step == 0 and depth_step == 0:
                parts[(0, 0)] = cells
            else:
                parts[(row_step, depth_step)] = moved(
                    cells[row_part, depth_part], row_step, depth_step
                )
    bands = [
        jnp.concatenate([parts[(r, 1)], parts[(r, 0)], parts[(r, -1)]], axis=1) for r in (1, 0, -1)
    ]
    return jnp.concatenate(bands, axis=0)


def geometry(angle_value):
    radians = 2.0 * math.pi * angle_value.astype(jnp.float32) / NANG
    stretch = 0.5 + 0.5 * jnp.abs(jnp.cos(radians))
    spread = 1.0 + jnp.abs(jnp.sin(radians))
    return (radians, stretch, spread)


def footprint(radians, stretch, spread, row_global, rows_total, block_size):
    shifted = shift_reach * jnp.sin(radians + 2.0 * math.pi * row_global / rows_total)
    inside = jnp.arange(block_size).astype(jnp.float32) - 0.5 * (block_size - 1)
    centre = block_size + inside[None, :] * stretch + shifted[:, None]
    places = jnp.arange(2 * block_size).astype(jnp.float32) + 0.5
    weights = (
        jnp.maximum(0.0, 1.0 - jnp.abs(places[None, None, :] - centre[:, :, None]) / spread)
        / spread
    )
    return weights.astype(jnp.bfloat16)


def axial_table(offsets, lengths, depth_count):
    offset_real = offsets.astype(jnp.float32)[..., None]
    length_real = lengths.astype(jnp.float32)[..., None]
    depth_place = jnp.arange(depth_count).astype(jnp.float32) + 0.5
    centre = offset_real + depth_place * length_real / depth_count
    row_number = jnp.arange(2 * depth_count)
    row_place = row_number.astype(jnp.float32) + 0.5
    triangle = jnp.maximum(0.0, 1.0 - jnp.abs(row_place - centre[..., None]))
    inside = (row_number >= offsets[..., None, None]) & (
        row_number < (offsets + lengths)[..., None, None]
    )
    return jnp.where(inside, triangle, 0.0).astype(jnp.bfloat16)


def smooth_update(current, fidelity, row_first, depth_first, rows_total, depth_total):
    row_index = row_first + jnp.arange(current.shape[0])
    depth_index = depth_first + jnp.arange(current.shape[1])
    keep_rows = ((row_index >= 0) & (row_index < rows_total - 1)).astype(jnp.float32)[:, None, None]
    keep_depth = ((depth_index >= 0) & (depth_index < depth_total - 1)).astype(jnp.float32)[
        None, :, None
    ]
    forward_rows = (
        jnp.concatenate([current[1:] - current[:-1], jnp.zeros_like(current[:1])], 0) * keep_rows
    )
    forward_depth = (
        jnp.concatenate([current[:, 1:] - current[:, :-1], jnp.zeros_like(current[:, :1])], 1)
        * keep_depth
    )
    forward_width = jnp.concatenate(
        [current[:, :, 1:] - current[:, :, :-1], jnp.zeros_like(current[:, :, :1])], 2
    )
    magnitude = jnp.sqrt(
        forward_rows * forward_rows
        + forward_depth * forward_depth
        + forward_width * forward_width
        + gradient_floor
    )
    normal_rows = forward_rows / magnitude
    normal_depth = forward_depth / magnitude
    normal_width = forward_width / magnitude
    divergence = normal_rows - jnp.concatenate(
        [jnp.zeros_like(normal_rows[:1]), normal_rows[:-1]], 0
    )
    divergence = (
        divergence
        + normal_depth
        - jnp.concatenate([jnp.zeros_like(normal_depth[:, :1]), normal_depth[:, :-1]], 1)
    )
    divergence = (
        divergence
        + normal_width
        - jnp.concatenate([jnp.zeros_like(normal_width[:, :, :1]), normal_width[:, :, :-1]], 2)
    )
    return current + step_length * (smooth_weight * divergence - (current - fidelity))


def footprint_mats(angle_value, shift, row_global, rows_total):
    radians, stretch, spread = geometry(angle_value)
    shifted = shift_reach * jnp.sin(radians + 2.0 * math.pi * row_global / rows_total)
    inside = jnp.arange(BLOCK).astype(jnp.float32) - 0.5 * (BLOCK - 1)
    centre = BLOCK + inside[None, :] * stretch + shifted[:, None]
    centre = jnp.concatenate([centre, centre], axis=1)
    parity = shift - 2 * ((shift + 2) // 2 - 1)
    half = (jnp.arange(LANES) >= BLOCK).astype(jnp.int32)
    place = jnp.arange(LANES)[:, None]
    taps = jnp.stack(
        [
            place - BLOCK * (half[None, None, :] + parity[:, None, None]),
            place + LANES - BLOCK * (half[None, None, :] + parity[:, None, None]),
            jnp.broadcast_to(place, (LANES, LANES))[None].repeat(shift.shape[0], 0),
        ],
        axis=1,
    )
    places = taps.astype(jnp.float32) + 0.5
    weights = (
        jnp.maximum(0.0, 1.0 - jnp.abs(places - centre[:, None, None, :]) / spread) / spread
    )
    valid = (taps >= 0) & (taps < 2 * BLOCK)
    return jnp.where(valid, weights, 0.0).astype(jnp.bfloat16)


def backproject_kernel(shift_ref, tiles_ref, mats_ref, out_ref):
    p = pl.program_id(0)
    tile_count = out_ref.shape[2] // LANES
    depth_count = out_ref.shape[1]

    @pl.when(p == 0)
    def _():
        out_ref[...] = jnp.zeros_like(out_ref)

    ends = jnp.concatenate([tiles_ref[0, 1], tiles_ref[0, tile_count]], axis=0).astype(jnp.bfloat16)
    for row in range(out_ref.shape[0]):
        shift = shift_ref[p, row]
        start = (shift + 2) // 2
        low = tiles_ref[0, pl.ds(start, tile_count)].reshape(tile_count * depth_count, LANES)
        high = tiles_ref[0, pl.ds(start + 1, tile_count)].reshape(tile_count * depth_count, LANES)
        result = jnp.dot(
            low.astype(jnp.bfloat16), mats_ref[0, row, 0], preferred_element_type=jnp.float32
        ) + jnp.dot(
            high.astype(jnp.bfloat16), mats_ref[0, row, 1], preferred_element_type=jnp.float32
        )
        edge = jnp.dot(ends, mats_ref[0, row, 2], preferred_element_type=jnp.float32)
        shift_vec = jnp.full((depth_count, LANES), shift, jnp.int32)
        for tile in range(tile_count):
            part = result[tile * depth_count:(tile + 1) * depth_count]
            if tile == 0:
                part = jnp.where(shift_vec < 0, edge[:depth_count], part)
            elif tile == tile_count - 2:
                part = jnp.where(shift_vec >= 2, edge[depth_count:], part)
            elif tile == tile_count - 1:
                part = jnp.where(shift_vec >= 0, edge[depth_count:], part)
            lanes = pl.ds(tile * LANES, LANES)
            out_ref[row, :, lanes] = out_ref[row, :, lanes] + part


def backproject(shifts, tiles, mats, column_count):
    count, rows = shifts.shape
    depth_count = tiles.shape[2]
    return pl.pallas_call(
        backproject_kernel,
        out_shape=jax.ShapeDtypeStruct((rows, depth_count, column_count), jnp.float32),
        grid_spec=pltpu.PrefetchScalarGridSpec(
            num_scalar_prefetch=1,
            grid=(count,),
            in_specs=[
                pl.BlockSpec((1,) + tiles.shape[1:], lambda p, s: (p, 0, 0, 0)),
                pl.BlockSpec((1,) + mats.shape[1:], lambda p, s: (p, 0, 0, 0, 0)),
            ],
            out_specs=pl.BlockSpec((rows, depth_count, column_count), lambda p, s: (0, 0, 0)),
        ),
        compiler_params=pltpu.CompilerParams(dimension_semantics=("arbitrary",)),
    )(shifts, tiles, mats)


def per_device(filtered, angle_index, band_offset, band_length, foot_block):
    depth_count = filtered.shape[1]
    row_count = foot_block.shape[1]
    extended_band = with_halo(filtered, (("gz", 1),), depth_count // 2)
    axial_weights = axial_table(band_offset[:, 0], band_length[:, 0], depth_count)
    summed_rows = jnp.einsum(
        "pzv,pvu->pzu",
        axial_weights,
        extended_band,
        preferred_element_type=jnp.float32,
    )
    columns = gather_columns(summed_rows.astype(jnp.bfloat16))
    column_count = columns.shape[2]
    row_base = lax.axis_index("gy") * row_count
    depth_base = lax.axis_index("gz") * depth_count
    rows_total = lax.axis_size("gy") * row_count
    depth_total = lax.axis_size("gz") * depth_count
    row_global = (row_base + jnp.arange(row_count)).astype(jnp.float32)
    shifts = foot_block[:, :, 2] - 2
    mats = jax.vmap(footprint_mats, in_axes=(0, 0, None, None))(
        angle_index, shifts, row_global, rows_total
    )
    tile_count = column_count // LANES
    tiles = columns.astype(jnp.float32).reshape(P_SIZE, depth_count, tile_count, LANES)
    tiles = jnp.pad(tiles.transpose(0, 2, 1, 3), ((0, 0), (1, 2), (0, 0), (0, 0)))
    summed = backproject(shifts, tiles, mats, column_count)
    backprojection = math.pi / P_SIZE * summed
    current = backprojection
    extended = with_wide_halo(backprojection, ITERS)
    fidelity = extended
    current = extended
    for turn_index in range(ITERS):
        reach = ITERS - turn_index
        current = smooth_update(
            current, fidelity, row_base - reach, depth_base - reach, rows_total, depth_total
        )[1:-1, 1:-1]
        fidelity = fidelity[1:-1, 1:-1]
    return current


def solution(mesh):
    return jax.shard_map(
        per_device,
        mesh=mesh,
        in_specs=(P(None, "gz", "gy"), P(), P(None, "gz"), P(None, "gz"), P(None, "gy", None)),
        out_specs=P("gy", "gz", None),
        check_vma=False,
    )
```

```python
import functools
import math

import jax
import jax.numpy as jnp
from jax import lax
from jax.experimental import pallas as pl
from jax.experimental.pallas import tpu as pltpu
from jax.sharding import PartitionSpec as P

X = 4096
P_SIZE = 16
NANG = 3600
BLOCK = 64
LANES = 128
ITERS = 2


step_length = 0.25
smooth_weight = 0.3
gradient_floor = 0.01
shift_reach = 8.0


def with_halo(cells, sides, width):
    for axis, dim in sides:
        count = lax.axis_size(axis)
        ends = count - 1
        head = lax.slice_in_dim(cells, 0, width, axis=dim)
        tail = lax.slice_in_dim(cells, cells.shape[dim] - width, cells.shape[dim], axis=dim)
        cells = jnp.concatenate(
            [
                lax.ppermute(tail, axis, [(i, (i + 1) % count) for i in range(ends)]),
                cells,
                lax.ppermute(head, axis, [((i + 1) % count, i) for i in range(ends)]),
            ],
            axis=dim,
        )
    return cells


def gather_kernel(count, local_ref, out_ref, send_sem, recv_sem, own_sem):
    me = lax.axis_index("gy")
    depth_index = lax.axis_index("gz")
    width = local_ref.shape[2]
    barrier = pltpu.get_barrier_semaphore()
    for step in range(1, count):
        peer = lax.rem(me + step, count)
        pl.semaphore_signal(
            barrier, inc=1, device_id=(depth_index, peer), device_id_type=pl.DeviceIdType.MESH
        )
    pl.semaphore_wait(barrier, count - 1)
    own_slot = pl.ds(pl.multiple_of(me * width, width), width)
    own = pltpu.make_async_copy(local_ref, out_ref.at[:, :, own_slot], own_sem)
    own.start()
    sends = []
    for step in range(1, count):
        peer = lax.rem(me + step, count)
        copy = pltpu.make_async_remote_copy(
            src_ref=local_ref,
            dst_ref=out_ref.at[:, :, own_slot],
            send_sem=send_sem.at[step],
            recv_sem=recv_sem.at[step],
            device_id=(depth_index, peer),
            device_id_type=pl.DeviceIdType.MESH,
        )
        copy.start()
        sends.append(copy)
    own.wait()
    for copy in sends:
        copy.wait_send()
    for step in range(1, count):
        sender = lax.rem(me + count - step, count)
        slot = pl.ds(pl.multiple_of(sender * width, width), width)
        arriving = pltpu.make_async_remote_copy(
            src_ref=local_ref,
            dst_ref=out_ref.at[:, :, slot],
            send_sem=send_sem.at[step],
            recv_sem=recv_sem.at[step],
            device_id=(depth_index, sender),
            device_id_type=pl.DeviceIdType.MESH,
        )
        arriving.wait_recv()


def gather_columns(local):
    count = lax.axis_size("gy")
    rows, depth, width = local.shape
    return pl.pallas_call(
        functools.partial(gather_kernel, count),
        out_shape=jax.ShapeDtypeStruct((rows, depth, width * count), local.dtype),
        in_specs=[pl.BlockSpec(memory_space=pl.ANY)],
        out_specs=pl.BlockSpec(memory_space=pl.ANY),
        scratch_shapes=[
            pltpu.SemaphoreType.DMA((count,)),
            pltpu.SemaphoreType.DMA((count,)),
            pltpu.SemaphoreType.DMA(()),
        ],
        compiler_params=pltpu.CompilerParams(collective_id=0, has_side_effects=True),
    )(local)


STEPS = ((1, 1), (1, 0), (1, -1), (0, 1), (0, -1), (-1, 1), (-1, 0), (-1, -1))


def halo_kernel(count, *refs):
    pieces = len(STEPS)
    sources, targets = refs[:pieces], refs[pieces:2 * pieces]
    send_sem, recv_sem = refs[2 * pieces], refs[2 * pieces + 1]
    row_count, depth_count = count
    row_me = lax.axis_index("gy")
    depth_me = lax.axis_index("gz")
    peers = [
        (lax.rem(depth_me + depth_step + depth_count, depth_count),
         lax.rem(row_me + row_step + row_count, row_count))
        for row_step, depth_step in STEPS
    ]
    barrier = pltpu.get_barrier_semaphore()
    for peer in peers:
        pl.semaphore_signal(barrier, inc=1, device_id=peer, device_id_type=pl.DeviceIdType.MESH)
    pl.semaphore_wait(barrier, pieces)
    copies = []
    for k, peer in enumerate(peers):
        copy = pltpu.make_async_remote_copy(
            src_ref=sources[k],
            dst_ref=targets[k],
            send_sem=send_sem.at[k],
            recv_sem=recv_sem.at[k],
            device_id=peer,
            device_id_type=pl.DeviceIdType.MESH,
        )
        copy.start()
        copies.append(copy)
    for copy in copies:
        copy.wait()


def with_wide_halo(cells, width):
    rows, depth = cells.shape[0], cells.shape[1]
    count = (lax.axis_size("gy"), lax.axis_size("gz"))
    row_parts = {1: slice(rows - width, rows), 0: slice(None), -1: slice(0, width)}
    depth_parts = {1: slice(depth - width, depth), 0: slice(None), -1: slice(0, width)}
    sent = [cells[row_parts[r], depth_parts[d]] for r, d in STEPS]
    received = pl.pallas_call(
        functools.partial(halo_kernel, count),
        out_shape=[jax.ShapeDtypeStruct(piece.shape, piece.dtype) for piece in sent],
        in_specs=[pl.BlockSpec(memory_space=pl.ANY)] * len(STEPS),
        out_specs=[pl.BlockSpec(memory_space=pl.ANY)] * len(STEPS),
        scratch_shapes=[
            pltpu.SemaphoreType.DMA((len(STEPS),)),
            pltpu.SemaphoreType.DMA((len(STEPS),)),
        ],
        compiler_params=pltpu.CompilerParams(collective_id=1, has_side_effects=True),
    )(*sent)
    parts = dict(zip(STEPS, received))
    parts[(0, 0)] = cells
    bands = [
        jnp.concatenate([parts[(r, 1)], parts[(r, 0)], parts[(r, -1)]], axis=1) for r in (1, 0, -1)
    ]
    return jnp.concatenate(bands, axis=0)


def geometry(angle_value):
    radians = 2.0 * math.pi * angle_value.astype(jnp.float32) / NANG
    stretch = 0.5 + 0.5 * jnp.abs(jnp.cos(radians))
    spread = 1.0 + jnp.abs(jnp.sin(radians))
    return (radians, stretch, spread)


def footprint(radians, stretch, spread, row_global, rows_total, block_size):
    shifted = shift_reach * jnp.sin(radians + 2.0 * math.pi * row_global / rows_total)
    inside = jnp.arange(block_size).astype(jnp.float32) - 0.5 * (block_size - 1)
    centre = block_size + inside[None, :] * stretch + shifted[:, None]
    places = jnp.arange(2 * block_size).astype(jnp.float32) + 0.5
    weights = (
        jnp.maximum(0.0, 1.0 - jnp.abs(places[None, None, :] - centre[:, :, None]) / spread)
        / spread
    )
    return weights.astype(jnp.bfloat16)


def axial_table(offsets, lengths, depth_count):
    offset_real = offsets.astype(jnp.float32)[..., None]
    length_real = lengths.astype(jnp.float32)[..., None]
    depth_place = jnp.arange(depth_count).astype(jnp.float32) + 0.5
    centre = offset_real + depth_place * length_real / depth_count
    row_number = jnp.arange(2 * depth_count)
    row_place = row_number.astype(jnp.float32) + 0.5
    triangle = jnp.maximum(0.0, 1.0 - jnp.abs(row_place - centre[..., None]))
    inside = (row_number >= offsets[..., None, None]) & (
        row_number < (offsets + lengths)[..., None, None]
    )
    return jnp.where(inside, triangle, 0.0).astype(jnp.bfloat16)


def smooth_update(current, fidelity, row_first, depth_first, rows_total, depth_total):
    row_index = row_first + jnp.arange(current.shape[0])
    depth_index = depth_first + jnp.arange(current.shape[1])
    keep_rows = ((row_index >= 0) & (row_index < rows_total - 1)).astype(jnp.float32)[:, None, None]
    keep_depth = ((depth_index >= 0) & (depth_index < depth_total - 1)).astype(jnp.float32)[
        None, :, None
    ]
    forward_rows = (
        jnp.concatenate([current[1:] - current[:-1], jnp.zeros_like(current[:1])], 0) * keep_rows
    )
    forward_depth = (
        jnp.concatenate([current[:, 1:] - current[:, :-1], jnp.zeros_like(current[:, :1])], 1)
        * keep_depth
    )
    forward_width = jnp.concatenate(
        [current[:, :, 1:] - current[:, :, :-1], jnp.zeros_like(current[:, :, :1])], 2
    )
    magnitude = jnp.sqrt(
        forward_rows * forward_rows
        + forward_depth * forward_depth
        + forward_width * forward_width
        + gradient_floor
    )
    normal_rows = forward_rows / magnitude
    normal_depth = forward_depth / magnitude
    normal_width = forward_width / magnitude
    divergence = normal_rows - jnp.concatenate(
        [jnp.zeros_like(normal_rows[:1]), normal_rows[:-1]], 0
    )
    divergence = (
        divergence
        + normal_depth
        - jnp.concatenate([jnp.zeros_like(normal_depth[:, :1]), normal_depth[:, :-1]], 1)
    )
    divergence = (
        divergence
        + normal_width
        - jnp.concatenate([jnp.zeros_like(normal_width[:, :, :1]), normal_width[:, :, :-1]], 2)
    )
    return current + step_length * (smooth_weight * divergence - (current - fidelity))


def footprint_mats(angle_value, shift, row_global, rows_total):
    radians, stretch, spread = geometry(angle_value)
    shifted = shift_reach * jnp.sin(radians + 2.0 * math.pi * row_global / rows_total)
    inside = jnp.arange(BLOCK).astype(jnp.float32) - 0.5 * (BLOCK - 1)
    centre = BLOCK + inside[None, :] * stretch + shifted[:, None]
    centre = jnp.concatenate([centre, centre], axis=1)
    parity = shift - 2 * ((shift + 2) // 2 - 1)
    half = (jnp.arange(LANES) >= BLOCK).astype(jnp.int32)
    place = jnp.arange(LANES)[:, None]
    taps = jnp.stack(
        [
            place - BLOCK * (half[None, None, :] + parity[:, None, None]),
            place + LANES - BLOCK * (half[None, None, :] + parity[:, None, None]),
            jnp.broadcast_to(place, (LANES, LANES))[None].repeat(shift.shape[0], 0),
        ],
        axis=1,
    )
    places = taps.astype(jnp.float32) + 0.5
    weights = (
        jnp.maximum(0.0, 1.0 - jnp.abs(places - centre[:, None, None, :]) / spread) / spread
    )
    valid = (taps >= 0) & (taps < 2 * BLOCK)
    return jnp.where(valid, weights, 0.0).astype(jnp.bfloat16)


def backproject_kernel(shift_ref, tiles_ref, mats_ref, out_ref):
    p = pl.program_id(0)
    tile_count = out_ref.shape[2] // LANES
    depth_count = out_ref.shape[1]

    @pl.when(p == 0)
    def _():
        out_ref[...] = jnp.zeros_like(out_ref)

    ends = jnp.concatenate([tiles_ref[0, 1], tiles_ref[0, tile_count]], axis=0).astype(jnp.bfloat16)
    for row in range(out_ref.shape[0]):
        shift = shift_ref[p, row]
        start = (shift + 2) // 2
        low = tiles_ref[0, pl.ds(start, tile_count)].reshape(tile_count * depth_count, LANES)
        high = tiles_ref[0, pl.ds(start + 1, tile_count)].reshape(tile_count * depth_count, LANES)
        result = jnp.dot(
            low.astype(jnp.bfloat16), mats_ref[0, row, 0], preferred_element_type=jnp.float32
        ) + jnp.dot(
            high.astype(jnp.bfloat16), mats_ref[0, row, 1], preferred_element_type=jnp.float32
        )
        edge = jnp.dot(ends, mats_ref[0, row, 2], preferred_element_type=jnp.float32)
        shift_vec = jnp.full((depth_count, LANES), shift, jnp.int32)
        for tile in range(tile_count):
            part = result[tile * depth_count:(tile + 1) * depth_count]
            if tile == 0:
                part = jnp.where(shift_vec < 0, edge[:depth_count], part)
            elif tile == tile_count - 2:
                part = jnp.where(shift_vec >= 2, edge[depth_count:], part)
            elif tile == tile_count - 1:
                part = jnp.where(shift_vec >= 0, edge[depth_count:], part)
            lanes = pl.ds(tile * LANES, LANES)
            out_ref[row, :, lanes] = out_ref[row, :, lanes] + part


def backproject(shifts, tiles, mats, column_count):
    count, rows = shifts.shape
    depth_count = tiles.shape[2]
    return pl.pallas_call(
        backproject_kernel,
        out_shape=jax.ShapeDtypeStruct((rows, depth_count, column_count), jnp.float32),
        grid_spec=pltpu.PrefetchScalarGridSpec(
            num_scalar_prefetch=1,
            grid=(count,),
            in_specs=[
                pl.BlockSpec((1,) + tiles.shape[1:], lambda p, s: (p, 0, 0, 0)),
                pl.BlockSpec((1,) + mats.shape[1:], lambda p, s: (p, 0, 0, 0, 0)),
            ],
            out_specs=pl.BlockSpec((rows, depth_count, column_count), lambda p, s: (0, 0, 0)),
        ),
        compiler_params=pltpu.CompilerParams(dimension_semantics=("arbitrary",)),
    )(shifts, tiles, mats)


def per_device(filtered, angle_index, band_offset, band_length, foot_block):
    depth_count = filtered.shape[1]
    row_count = foot_block.shape[1]
    extended_band = with_halo(filtered, (("gz", 1),), depth_count // 2)
    axial_weights = axial_table(band_offset[:, 0], band_length[:, 0], depth_count)
    summed_rows = jnp.einsum(
        "pzv,pvu->pzu",
        axial_weights,
        extended_band,
        preferred_element_type=jnp.float32,
    )
    columns = gather_columns(summed_rows.astype(jnp.bfloat16))
    column_count = columns.shape[2]
    row_base = lax.axis_index("gy") * row_count
    depth_base = lax.axis_index("gz") * depth_count
    rows_total = lax.axis_size("gy") * row_count
    depth_total = lax.axis_size("gz") * depth_count
    row_global = (row_base + jnp.arange(row_count)).astype(jnp.float32)
    shifts = foot_block[:, :, 2] - 2
    mats = jax.vmap(footprint_mats, in_axes=(0, 0, None, None))(
        angle_index, shifts, row_global, rows_total
    )
    tile_count = column_count // LANES
    tiles = columns.astype(jnp.float32).reshape(P_SIZE, depth_count, tile_count, LANES)
    tiles = jnp.pad(tiles.transpose(0, 2, 1, 3), ((0, 0), (1, 2), (0, 0), (0, 0)))
    summed = backproject(shifts, tiles, mats, column_count)
    backprojection = math.pi / P_SIZE * summed
    current = backprojection
    extended = with_wide_halo(backprojection, ITERS)
    fidelity = extended
    current = extended
    for turn_index in range(ITERS):
        reach = ITERS - turn_index
        current = smooth_update(
            current, fidelity, row_base - reach, depth_base - reach, rows_total, depth_total
        )[1:-1, 1:-1]
        fidelity = fidelity[1:-1, 1:-1]
    return current


def solution(mesh):
    return jax.shard_map(
        per_device,
        mesh=mesh,
        in_specs=(P(None, "gz", "gy"), P(), P(None, "gz"), P(None, "gz"), P(None, "gy", None)),
        out_specs=P("gy", "gz", None),
        check_vma=False,
    )
```

```python
import functools
import math

import jax
import jax.numpy as jnp
from jax import lax
from jax.experimental import pallas as pl
from jax.experimental.pallas import tpu as pltpu
from jax.sharding import PartitionSpec as P

X = 4096
P_SIZE = 16
NANG = 3600
BLOCK = 64
LANES = 128
ITERS = 2


step_length = 0.25
smooth_weight = 0.3
gradient_floor = 0.01
shift_reach = 8.0


def with_halo(cells, sides, width):
    for axis, dim in sides:
        count = lax.axis_size(axis)
        ends = count - 1
        head = lax.slice_in_dim(cells, 0, width, axis=dim)
        tail = lax.slice_in_dim(cells, cells.shape[dim] - width, cells.shape[dim], axis=dim)
        cells = jnp.concatenate(
            [
                lax.ppermute(tail, axis, [(i, (i + 1) % count) for i in range(ends)]),
                cells,
                lax.ppermute(head, axis, [((i + 1) % count, i) for i in range(ends)]),
            ],
            axis=dim,
        )
    return cells


def gather_kernel(count, local_ref, out_ref, send_sem, recv_sem, own_sem):
    ring = count // 2
    forward_steps = ring // 2
    backward_steps = ring - 1 - forward_steps
    me = lax.axis_index("gy")
    depth_index = lax.axis_index("gz")
    half = me // ring
    place = me % ring
    width = local_ref.shape[2]
    mesh_kind = pl.DeviceIdType.MESH

    def device(half_of, place_of):
        return half_of * ring + lax.rem(place_of + 2 * ring, ring)

    partner = device(1 - half, place)
    right = device(half, place + 1)
    left = device(half, place - 1)

    def slot(index):
        return out_ref.at[:, :, pl.ds(pl.multiple_of(index * width, width), width)]

    barrier = pltpu.get_barrier_semaphore()
    for peer in (partner, right, left):
        pl.semaphore_signal(barrier, inc=1, device_id=(depth_index, peer), device_id_type=mesh_kind)
    pl.semaphore_wait(barrier, 3)

    own = pltpu.make_async_copy(local_ref, slot(me), own_sem)
    own.start()
    sends = []

    def send(source, index, peer):
        copy = pltpu.make_async_remote_copy(
            src_ref=source,
            dst_ref=slot(index),
            send_sem=send_sem.at[len(sends)],
            recv_sem=recv_sem.at[index],
            device_id=(depth_index, peer),
            device_id_type=mesh_kind,
        )
        copy.start()
        sends.append(copy)

    def arrived(index):
        pltpu.make_async_remote_copy(
            src_ref=local_ref,
            dst_ref=slot(index),
            send_sem=send_sem.at[0],
            recv_sem=recv_sem.at[index],
            device_id=(depth_index, partner),
            device_id_type=mesh_kind,
        ).wait_recv()

    send(local_ref, me, partner)
    arrived(partner)
    for step in range(1, forward_steps + 1):
        for direction, peer, limit in ((-1, right, forward_steps), (1, left, backward_steps)):
            if step > limit:
                continue
            if step == 1:
                send(local_ref, me, peer)
                send(slot(partner), partner, peer)
                continue
            for half_of in (0, 1):
                index = device(half_of, place + direction * (step - 1))
                arrived(index)
                send(slot(index), index, peer)
    for direction, steps in ((-1, forward_steps), (1, backward_steps)):
        for half_of in (0, 1):
            arrived(device(half_of, place + direction * steps))
    own.wait()
    for copy in sends:
        copy.wait_send()


def gather_columns(local):
    count = lax.axis_size("gy")
    rows, depth, width = local.shape
    return pl.pallas_call(
        functools.partial(gather_kernel, count),
        out_shape=jax.ShapeDtypeStruct((rows, depth, width * count), local.dtype),
        in_specs=[pl.BlockSpec(memory_space=pl.ANY)],
        out_specs=pl.BlockSpec(memory_space=pl.ANY),
        scratch_shapes=[
            pltpu.SemaphoreType.DMA((count,)),
            pltpu.SemaphoreType.DMA((count,)),
            pltpu.SemaphoreType.DMA(()),
        ],
        compiler_params=pltpu.CompilerParams(collective_id=0, has_side_effects=True),
    )(local)


STEPS = ((1, 1), (1, 0), (1, -1), (0, 1), (0, -1), (-1, 1), (-1, 0), (-1, -1))


def halo_kernel(count, *refs):
    pieces = len(STEPS)
    sources, targets = refs[:pieces], refs[pieces:2 * pieces]
    send_sem, recv_sem = refs[2 * pieces], refs[2 * pieces + 1]
    row_count, depth_count = count
    row_me = lax.axis_index("gy")
    depth_me = lax.axis_index("gz")
    peers = [
        (lax.rem(depth_me + depth_step + depth_count, depth_count),
         lax.rem(row_me + row_step + row_count, row_count))
        for row_step, depth_step in STEPS
    ]
    barrier = pltpu.get_barrier_semaphore()
    for peer in peers:
        pl.semaphore_signal(barrier, inc=1, device_id=peer, device_id_type=pl.DeviceIdType.MESH)
    pl.semaphore_wait(barrier, pieces)
    copies = []
    for k, peer in enumerate(peers):
        copy = pltpu.make_async_remote_copy(
            src_ref=sources[k],
            dst_ref=targets[k],
            send_sem=send_sem.at[k],
            recv_sem=recv_sem.at[k],
            device_id=peer,
            device_id_type=pl.DeviceIdType.MESH,
        )
        copy.start()
        copies.append(copy)
    for copy in copies:
        copy.wait()


def with_wide_halo(cells, width):
    rows, depth = cells.shape[0], cells.shape[1]
    count = (lax.axis_size("gy"), lax.axis_size("gz"))
    row_parts = {1: slice(rows - width, rows), 0: slice(None), -1: slice(0, width)}
    depth_parts = {1: slice(depth - width, depth), 0: slice(None), -1: slice(0, width)}
    sent = [cells[row_parts[r], depth_parts[d]] for r, d in STEPS]
    received = pl.pallas_call(
        functools.partial(halo_kernel, count),
        out_shape=[jax.ShapeDtypeStruct(piece.shape, piece.dtype) for piece in sent],
        in_specs=[pl.BlockSpec(memory_space=pl.ANY)] * len(STEPS),
        out_specs=[pl.BlockSpec(memory_space=pl.ANY)] * len(STEPS),
        scratch_shapes=[
            pltpu.SemaphoreType.DMA((len(STEPS),)),
            pltpu.SemaphoreType.DMA((len(STEPS),)),
        ],
        compiler_params=pltpu.CompilerParams(collective_id=1, has_side_effects=True),
    )(*sent)
    parts = dict(zip(STEPS, received))
    parts[(0, 0)] = cells
    bands = [
        jnp.concatenate([parts[(r, 1)], parts[(r, 0)], parts[(r, -1)]], axis=1) for r in (1, 0, -1)
    ]
    return jnp.concatenate(bands, axis=0)


def geometry(angle_value):
    radians = 2.0 * math.pi * angle_value.astype(jnp.float32) / NANG
    stretch = 0.5 + 0.5 * jnp.abs(jnp.cos(radians))
    spread = 1.0 + jnp.abs(jnp.sin(radians))
    return (radians, stretch, spread)


def footprint(radians, stretch, spread, row_global, rows_total, block_size):
    shifted = shift_reach * jnp.sin(radians + 2.0 * math.pi * row_global / rows_total)
    inside = jnp.arange(block_size).astype(jnp.float32) - 0.5 * (block_size - 1)
    centre = block_size + inside[None, :] * stretch + shifted[:, None]
    places = jnp.arange(2 * block_size).astype(jnp.float32) + 0.5
    weights = (
        jnp.maximum(0.0, 1.0 - jnp.abs(places[None, None, :] - centre[:, :, None]) / spread)
        / spread
    )
    return weights.astype(jnp.bfloat16)


def axial_table(offsets, lengths, depth_count):
    offset_real = offsets.astype(jnp.float32)[..., None]
    length_real = lengths.astype(jnp.float32)[..., None]
    depth_place = jnp.arange(depth_count).astype(jnp.float32) + 0.5
    centre = offset_real + depth_place * length_real / depth_count
    row_number = jnp.arange(2 * depth_count)
    row_place = row_number.astype(jnp.float32) + 0.5
    triangle = jnp.maximum(0.0, 1.0 - jnp.abs(row_place - centre[..., None]))
    inside = (row_number >= offsets[..., None, None]) & (
        row_number < (offsets + lengths)[..., None, None]
    )
    return jnp.where(inside, triangle, 0.0).astype(jnp.bfloat16)


def smooth_update(current, fidelity, row_first, depth_first, rows_total, depth_total):
    row_index = row_first + jnp.arange(current.shape[0])
    depth_index = depth_first + jnp.arange(current.shape[1])
    keep_rows = ((row_index >= 0) & (row_index < rows_total - 1)).astype(jnp.float32)[:, None, None]
    keep_depth = ((depth_index >= 0) & (depth_index < depth_total - 1)).astype(jnp.float32)[
        None, :, None
    ]
    forward_rows = (
        jnp.concatenate([current[1:] - current[:-1], jnp.zeros_like(current[:1])], 0) * keep_rows
    )
    forward_depth = (
        jnp.concatenate([current[:, 1:] - current[:, :-1], jnp.zeros_like(current[:, :1])], 1)
        * keep_depth
    )
    forward_width = jnp.concatenate(
        [current[:, :, 1:] - current[:, :, :-1], jnp.zeros_like(current[:, :, :1])], 2
    )
    magnitude = jnp.sqrt(
        forward_rows * forward_rows
        + forward_depth * forward_depth
        + forward_width * forward_width
        + gradient_floor
    )
    normal_rows = forward_rows / magnitude
    normal_depth = forward_depth / magnitude
    normal_width = forward_width / magnitude
    divergence = normal_rows - jnp.concatenate(
        [jnp.zeros_like(normal_rows[:1]), normal_rows[:-1]], 0
    )
    divergence = (
        divergence
        + normal_depth
        - jnp.concatenate([jnp.zeros_like(normal_depth[:, :1]), normal_depth[:, :-1]], 1)
    )
    divergence = (
        divergence
        + normal_width
        - jnp.concatenate([jnp.zeros_like(normal_width[:, :, :1]), normal_width[:, :, :-1]], 2)
    )
    return current + step_length * (smooth_weight * divergence - (current - fidelity))


def footprint_mats(angle_value, shift, row_global, rows_total):
    radians, stretch, spread = geometry(angle_value)
    shifted = shift_reach * jnp.sin(radians + 2.0 * math.pi * row_global / rows_total)
    inside = jnp.arange(BLOCK).astype(jnp.float32) - 0.5 * (BLOCK - 1)
    centre = BLOCK + inside[None, :] * stretch + shifted[:, None]
    centre = jnp.concatenate([centre, centre], axis=1)
    parity = shift - 2 * ((shift + 2) // 2 - 1)
    half = (jnp.arange(LANES) >= BLOCK).astype(jnp.int32)
    place = jnp.arange(LANES)[:, None]
    taps = jnp.stack(
        [
            place - BLOCK * (half[None, None, :] + parity[:, None, None]),
            place + LANES - BLOCK * (half[None, None, :] + parity[:, None, None]),
            jnp.broadcast_to(place, (LANES, LANES))[None].repeat(shift.shape[0], 0),
        ],
        axis=1,
    )
    places = taps.astype(jnp.float32) + 0.5
    weights = (
        jnp.maximum(0.0, 1.0 - jnp.abs(places - centre[:, None, None, :]) / spread) / spread
    )
    valid = (taps >= 0) & (taps < 2 * BLOCK)
    return jnp.where(valid, weights, 0.0).astype(jnp.bfloat16)


def backproject_kernel(shift_ref, tiles_ref, mats_ref, out_ref):
    p = pl.program_id(0)
    tile_count = out_ref.shape[2] // LANES
    depth_count = out_ref.shape[1]

    @pl.when(p == 0)
    def _():
        out_ref[...] = jnp.zeros_like(out_ref)

    ends = jnp.concatenate([tiles_ref[0, 1], tiles_ref[0, tile_count]], axis=0).astype(jnp.bfloat16)
    for row in range(out_ref.shape[0]):
        shift = shift_ref[p, row]
        start = (shift + 2) // 2
        low = tiles_ref[0, pl.ds(start, tile_count)].reshape(tile_count * depth_count, LANES)
        high = tiles_ref[0, pl.ds(start + 1, tile_count)].reshape(tile_count * depth_count, LANES)
        result = jnp.dot(
            low.astype(jnp.bfloat16), mats_ref[0, row, 0], preferred_element_type=jnp.float32
        ) + jnp.dot(
            high.astype(jnp.bfloat16), mats_ref[0, row, 1], preferred_element_type=jnp.float32
        )
        edge = jnp.dot(ends, mats_ref[0, row, 2], preferred_element_type=jnp.float32)
        shift_vec = jnp.full((depth_count, LANES), shift, jnp.int32)
        for tile in range(tile_count):
            part = result[tile * depth_count:(tile + 1) * depth_count]
            if tile == 0:
                part = jnp.where(shift_vec < 0, edge[:depth_count], part)
            elif tile == tile_count - 2:
                part = jnp.where(shift_vec >= 2, edge[depth_count:], part)
            elif tile == tile_count - 1:
                part = jnp.where(shift_vec >= 0, edge[depth_count:], part)
            lanes = pl.ds(tile * LANES, LANES)
            out_ref[row, :, lanes] = out_ref[row, :, lanes] + part


def backproject(shifts, tiles, mats, column_count):
    count, rows = shifts.shape
    depth_count = tiles.shape[2]
    return pl.pallas_call(
        backproject_kernel,
        out_shape=jax.ShapeDtypeStruct((rows, depth_count, column_count), jnp.float32),
        grid_spec=pltpu.PrefetchScalarGridSpec(
            num_scalar_prefetch=1,
            grid=(count,),
            in_specs=[
                pl.BlockSpec((1,) + tiles.shape[1:], lambda p, s: (p, 0, 0, 0)),
                pl.BlockSpec((1,) + mats.shape[1:], lambda p, s: (p, 0, 0, 0, 0)),
            ],
            out_specs=pl.BlockSpec((rows, depth_count, column_count), lambda p, s: (0, 0, 0)),
        ),
        compiler_params=pltpu.CompilerParams(dimension_semantics=("arbitrary",)),
    )(shifts, tiles, mats)


def per_device(filtered, angle_index, band_offset, band_length, foot_block):
    depth_count = filtered.shape[1]
    row_count = foot_block.shape[1]
    extended_band = with_halo(filtered, (("gz", 1),), depth_count // 2)
    axial_weights = axial_table(band_offset[:, 0], band_length[:, 0], depth_count)
    summed_rows = jnp.einsum(
        "pzv,pvu->pzu",
        axial_weights,
        extended_band,
        preferred_element_type=jnp.float32,
    )
    columns = gather_columns(summed_rows.astype(jnp.bfloat16))
    column_count = columns.shape[2]
    row_base = lax.axis_index("gy") * row_count
    depth_base = lax.axis_index("gz") * depth_count
    rows_total = lax.axis_size("gy") * row_count
    depth_total = lax.axis_size("gz") * depth_count
    row_global = (row_base + jnp.arange(row_count)).astype(jnp.float32)
    shifts = foot_block[:, :, 2] - 2
    mats = jax.vmap(footprint_mats, in_axes=(0, 0, None, None))(
        angle_index, shifts, row_global, rows_total
    )
    tile_count = column_count // LANES
    tiles = columns.astype(jnp.float32).reshape(P_SIZE, depth_count, tile_count, LANES)
    tiles = jnp.pad(tiles.transpose(0, 2, 1, 3), ((0, 0), (1, 2), (0, 0), (0, 0)))
    summed = backproject(shifts, tiles, mats, column_count)
    backprojection = math.pi / P_SIZE * summed
    current = backprojection
    extended = with_wide_halo(backprojection, ITERS)
    fidelity = extended
    current = extended
    for turn_index in range(ITERS):
        reach = ITERS - turn_index
        current = smooth_update(
            current, fidelity, row_base - reach, depth_base - reach, rows_total, depth_total
        )[1:-1, 1:-1]
        fidelity = fidelity[1:-1, 1:-1]
    return current


def solution(mesh):
    return jax.shard_map(
        per_device,
        mesh=mesh,
        in_specs=(P(None, "gz", "gy"), P(), P(None, "gz"), P(None, "gz"), P(None, "gy", None)),
        out_specs=P("gy", "gz", None),
        check_vma=False,
    )
```

```python
import functools
import math

import jax
import jax.numpy as jnp
from jax import lax
from jax.experimental import pallas as pl
from jax.experimental.pallas import tpu as pltpu
from jax.sharding import PartitionSpec as P

X = 4096
P_SIZE = 16
NANG = 3600
BLOCK = 64
LANES = 128
ITERS = 2


step_length = 0.25
smooth_weight = 0.3
gradient_floor = 0.01
shift_reach = 8.0


def with_halo(cells, sides, width):
    for axis, dim in sides:
        count = lax.axis_size(axis)
        ends = count - 1
        head = lax.slice_in_dim(cells, 0, width, axis=dim)
        tail = lax.slice_in_dim(cells, cells.shape[dim] - width, cells.shape[dim], axis=dim)
        cells = jnp.concatenate(
            [
                lax.ppermute(tail, axis, [(i, (i + 1) % count) for i in range(ends)]),
                cells,
                lax.ppermute(head, axis, [((i + 1) % count, i) for i in range(ends)]),
            ],
            axis=dim,
        )
    return cells


def gather_kernel(count, local_ref, out_ref, send_sem, recv_sem, own_sem):
    ring = count // 2
    forward_steps = ring // 2
    backward_steps = ring - 1 - forward_steps
    me = lax.axis_index("gy")
    depth_index = lax.axis_index("gz")
    half = me // ring
    place = me % ring
    width = local_ref.shape[2]
    mesh_kind = pl.DeviceIdType.MESH

    def device(half_of, place_of):
        return half_of * ring + lax.rem(place_of + 2 * ring, ring)

    partner = device(1 - half, place)
    right = device(half, place + 1)
    left = device(half, place - 1)

    def slot(index):
        return out_ref.at[:, :, pl.ds(pl.multiple_of(index * width, width), width)]

    barrier = pltpu.get_barrier_semaphore()
    for peer in (partner, right, left):
        pl.semaphore_signal(barrier, inc=1, device_id=(depth_index, peer), device_id_type=mesh_kind)
    pl.semaphore_wait(barrier, 3)

    own = pltpu.make_async_copy(local_ref, slot(me), own_sem)
    own.start()
    sends = []

    def send(source, index, peer):
        copy = pltpu.make_async_remote_copy(
            src_ref=source,
            dst_ref=slot(index),
            send_sem=send_sem.at[len(sends)],
            recv_sem=recv_sem.at[index],
            device_id=(depth_index, peer),
            device_id_type=mesh_kind,
        )
        copy.start()
        sends.append(copy)

    def arrived(index):
        pltpu.make_async_remote_copy(
            src_ref=local_ref,
            dst_ref=slot(index),
            send_sem=send_sem.at[0],
            recv_sem=recv_sem.at[index],
            device_id=(depth_index, partner),
            device_id_type=mesh_kind,
        ).wait_recv()

    send(local_ref, me, partner)
    arrived(partner)
    for step in range(1, forward_steps + 1):
        for direction, peer, limit in ((-1, right, forward_steps), (1, left, backward_steps)):
            if step > limit:
                continue
            if step == 1:
                send(local_ref, me, peer)
                send(slot(partner), partner, peer)
                continue
            for half_of in (0, 1):
                index = device(half_of, place + direction * (step - 1))
                arrived(index)
                send(slot(index), index, peer)
    for direction, steps in ((-1, forward_steps), (1, backward_steps)):
        for half_of in (0, 1):
            arrived(device(half_of, place + direction * steps))
    own.wait()
    for copy in sends:
        copy.wait_send()


def gather_columns(local):
    count = lax.axis_size("gy")
    rows, depth, width = local.shape
    return pl.pallas_call(
        functools.partial(gather_kernel, count),
        out_shape=jax.ShapeDtypeStruct((rows, depth, width * count), local.dtype),
        in_specs=[pl.BlockSpec(memory_space=pl.ANY)],
        out_specs=pl.BlockSpec(memory_space=pl.ANY),
        scratch_shapes=[
            pltpu.SemaphoreType.DMA((count,)),
            pltpu.SemaphoreType.DMA((count,)),
            pltpu.SemaphoreType.DMA(()),
        ],
        compiler_params=pltpu.CompilerParams(collective_id=0, has_side_effects=True),
    )(local)


STEPS = ((1, 1), (1, 0), (1, -1), (0, 1), (0, -1), (-1, 1), (-1, 0), (-1, -1))


def halo_kernel(count, *refs):
    pieces = len(STEPS)
    sources, targets = refs[:pieces], refs[pieces:2 * pieces]
    send_sem, recv_sem = refs[2 * pieces], refs[2 * pieces + 1]
    row_count, depth_count = count
    row_me = lax.axis_index("gy")
    depth_me = lax.axis_index("gz")
    peers = [
        (lax.rem(depth_me + depth_step + depth_count, depth_count),
         lax.rem(row_me + row_step + row_count, row_count))
        for row_step, depth_step in STEPS
    ]
    barrier = pltpu.get_barrier_semaphore()
    for peer in peers:
        pl.semaphore_signal(barrier, inc=1, device_id=peer, device_id_type=pl.DeviceIdType.MESH)
    pl.semaphore_wait(barrier, pieces)
    copies = []
    for k, peer in enumerate(peers):
        copy = pltpu.make_async_remote_copy(
            src_ref=sources[k],
            dst_ref=targets[k],
            send_sem=send_sem.at[k],
            recv_sem=recv_sem.at[k],
            device_id=peer,
            device_id_type=pl.DeviceIdType.MESH,
        )
        copy.start()
        copies.append(copy)
    for copy in copies:
        copy.wait()


def with_wide_halo(cells, width):
    rows, depth = cells.shape[0], cells.shape[1]
    count = (lax.axis_size("gy"), lax.axis_size("gz"))
    row_parts = {1: slice(rows - width, rows), 0: slice(None), -1: slice(0, width)}
    depth_parts = {1: slice(depth - width, depth), 0: slice(None), -1: slice(0, width)}
    sent = [cells[row_parts[r], depth_parts[d]] for r, d in STEPS]
    received = pl.pallas_call(
        functools.partial(halo_kernel, count),
        out_shape=[jax.ShapeDtypeStruct(piece.shape, piece.dtype) for piece in sent],
        in_specs=[pl.BlockSpec(memory_space=pl.ANY)] * len(STEPS),
        out_specs=[pl.BlockSpec(memory_space=pl.ANY)] * len(STEPS),
        scratch_shapes=[
            pltpu.SemaphoreType.DMA((len(STEPS),)),
            pltpu.SemaphoreType.DMA((len(STEPS),)),
        ],
        compiler_params=pltpu.CompilerParams(collective_id=1, has_side_effects=True),
    )(*sent)
    parts = dict(zip(STEPS, received))
    parts[(0, 0)] = cells
    bands = [
        jnp.concatenate([parts[(r, 1)], parts[(r, 0)], parts[(r, -1)]], axis=1) for r in (1, 0, -1)
    ]
    return jnp.concatenate(bands, axis=0)


def geometry(angle_value):
    radians = 2.0 * math.pi * angle_value.astype(jnp.float32) / NANG
    stretch = 0.5 + 0.5 * jnp.abs(jnp.cos(radians))
    spread = 1.0 + jnp.abs(jnp.sin(radians))
    return (radians, stretch, spread)


def footprint(radians, stretch, spread, row_global, rows_total, block_size):
    shifted = shift_reach * jnp.sin(radians + 2.0 * math.pi * row_global / rows_total)
    inside = jnp.arange(block_size).astype(jnp.float32) - 0.5 * (block_size - 1)
    centre = block_size + inside[None, :] * stretch + shifted[:, None]
    places = jnp.arange(2 * block_size).astype(jnp.float32) + 0.5
    weights = (
        jnp.maximum(0.0, 1.0 - jnp.abs(places[None, None, :] - centre[:, :, None]) / spread)
        / spread
    )
    return weights.astype(jnp.bfloat16)


def axial_table(offsets, lengths, depth_count):
    offset_real = offsets.astype(jnp.float32)[..., None]
    length_real = lengths.astype(jnp.float32)[..., None]
    depth_place = jnp.arange(depth_count).astype(jnp.float32) + 0.5
    centre = offset_real + depth_place * length_real / depth_count
    row_number = jnp.arange(2 * depth_count)
    row_place = row_number.astype(jnp.float32) + 0.5
    triangle = jnp.maximum(0.0, 1.0 - jnp.abs(row_place - centre[..., None]))
    inside = (row_number >= offsets[..., None, None]) & (
        row_number < (offsets + lengths)[..., None, None]
    )
    return jnp.where(inside, triangle, 0.0).astype(jnp.bfloat16)


def smooth_update(current, fidelity, row_first, depth_first, rows_total, depth_total):
    row_index = row_first + jnp.arange(current.shape[0])
    depth_index = depth_first + jnp.arange(current.shape[1])
    keep_rows = ((row_index >= 0) & (row_index < rows_total - 1)).astype(jnp.float32)[:, None, None]
    keep_depth = ((depth_index >= 0) & (depth_index < depth_total - 1)).astype(jnp.float32)[
        None, :, None
    ]
    forward_rows = (
        jnp.concatenate([current[1:] - current[:-1], jnp.zeros_like(current[:1])], 0) * keep_rows
    )
    forward_depth = (
        jnp.concatenate([current[:, 1:] - current[:, :-1], jnp.zeros_like(current[:, :1])], 1)
        * keep_depth
    )
    forward_width = jnp.concatenate(
        [current[:, :, 1:] - current[:, :, :-1], jnp.zeros_like(current[:, :, :1])], 2
    )
    magnitude = jnp.sqrt(
        forward_rows * forward_rows
        + forward_depth * forward_depth
        + forward_width * forward_width
        + gradient_floor
    )
    normal_rows = forward_rows / magnitude
    normal_depth = forward_depth / magnitude
    normal_width = forward_width / magnitude
    divergence = normal_rows - jnp.concatenate(
        [jnp.zeros_like(normal_rows[:1]), normal_rows[:-1]], 0
    )
    divergence = (
        divergence
        + normal_depth
        - jnp.concatenate([jnp.zeros_like(normal_depth[:, :1]), normal_depth[:, :-1]], 1)
    )
    divergence = (
        divergence
        + normal_width
        - jnp.concatenate([jnp.zeros_like(normal_width[:, :, :1]), normal_width[:, :, :-1]], 2)
    )
    return current + step_length * (smooth_weight * divergence - (current - fidelity))


def footprint_mats(angle_value, row_global, rows_total):
    radians, stretch, spread = geometry(angle_value)
    shifted = shift_reach * jnp.sin(radians + 2.0 * math.pi * row_global / rows_total)
    inside = jnp.arange(BLOCK).astype(jnp.float32) - 0.5 * (BLOCK - 1)
    centre = BLOCK + inside[None, :] * stretch + shifted[:, None]
    centre = jnp.concatenate([centre, centre], axis=1)
    places = jnp.arange(LANES).astype(jnp.float32)[:, None] + 0.5
    weights = (
        jnp.maximum(0.0, 1.0 - jnp.abs(places[None] - centre[:, None, :]) / spread) / spread
    )
    return weights.astype(jnp.bfloat16)


def backproject_kernel(shift_ref, tiles_ref, mats_ref, out_ref):
    p = pl.program_id(0)
    tile_count = out_ref.shape[2] // LANES
    depth_count = out_ref.shape[1]

    @pl.when(p == 0)
    def _():
        out_ref[...] = jnp.zeros_like(out_ref)

    ends = jnp.concatenate([tiles_ref[0, 1], tiles_ref[0, tile_count]], axis=0).astype(jnp.bfloat16)
    second_half = lax.broadcasted_iota(jnp.int32, (LANES, LANES), 1) >= BLOCK
    empty = jnp.zeros((BLOCK, LANES), jnp.bfloat16)
    for row in range(out_ref.shape[0]):
        shift = shift_ref[p, row]
        start = (shift + 2) // 2
        odd = jnp.full((LANES, LANES), shift - 2 * (start - 1), jnp.int32) == 1
        whole = mats_ref[0, row]
        down = jnp.concatenate([empty, whole[:BLOCK]], axis=0)
        up = jnp.concatenate([whole[BLOCK:], empty], axis=0)
        nothing = jnp.zeros_like(whole)
        first = jnp.where(
            second_half, jnp.where(odd, nothing, down), jnp.where(odd, down, whole)
        )
        second = jnp.where(
            second_half, jnp.where(odd, whole, up), jnp.where(odd, up, nothing)
        )
        low = tiles_ref[0, pl.ds(start, tile_count)].reshape(tile_count * depth_count, LANES)
        high = tiles_ref[0, pl.ds(start + 1, tile_count)].reshape(tile_count * depth_count, LANES)
        taps = jnp.concatenate([low, high], axis=1).astype(jnp.bfloat16)
        result = jnp.dot(
            taps, jnp.concatenate([first, second], axis=0), preferred_element_type=jnp.float32
        )
        edge = jnp.dot(ends, whole, preferred_element_type=jnp.float32)
        shift_vec = jnp.full((depth_count, LANES), shift, jnp.int32)
        for tile in range(tile_count):
            part = result[tile * depth_count:(tile + 1) * depth_count]
            if tile == 0:
                part = jnp.where(shift_vec < 0, edge[:depth_count], part)
            elif tile == tile_count - 2:
                part = jnp.where(shift_vec >= 2, edge[depth_count:], part)
            elif tile == tile_count - 1:
                part = jnp.where(shift_vec >= 0, edge[depth_count:], part)
            lanes = pl.ds(tile * LANES, LANES)
            out_ref[row, :, lanes] = out_ref[row, :, lanes] + part


def backproject(shifts, tiles, mats, column_count):
    count, rows = shifts.shape
    depth_count = tiles.shape[2]
    return pl.pallas_call(
        backproject_kernel,
        out_shape=jax.ShapeDtypeStruct((rows, depth_count, column_count), jnp.float32),
        grid_spec=pltpu.PrefetchScalarGridSpec(
            num_scalar_prefetch=1,
            grid=(count,),
            in_specs=[
                pl.BlockSpec((1,) + tiles.shape[1:], lambda p, s: (p, 0, 0, 0)),
                pl.BlockSpec((1,) + mats.shape[1:], lambda p, s: (p, 0, 0, 0)),
            ],
            out_specs=pl.BlockSpec((rows, depth_count, column_count), lambda p, s: (0, 0, 0)),
        ),
        compiler_params=pltpu.CompilerParams(dimension_semantics=("arbitrary",)),
    )(shifts, tiles, mats)


def per_device(filtered, angle_index, band_offset, band_length, foot_block):
    depth_count = filtered.shape[1]
    row_count = foot_block.shape[1]
    extended_band = with_halo(filtered, (("gz", 1),), depth_count // 2)
    axial_weights = axial_table(band_offset[:, 0], band_length[:, 0], depth_count)
    summed_rows = jnp.einsum(
        "pzv,pvu->pzu",
        axial_weights,
        extended_band,
        preferred_element_type=jnp.float32,
    )
    columns = gather_columns(summed_rows.astype(jnp.bfloat16))
    column_count = columns.shape[2]
    row_base = lax.axis_index("gy") * row_count
    depth_base = lax.axis_index("gz") * depth_count
    rows_total = lax.axis_size("gy") * row_count
    depth_total = lax.axis_size("gz") * depth_count
    row_global = (row_base + jnp.arange(row_count)).astype(jnp.float32)
    shifts = foot_block[:, :, 2] - 2
    mats = jax.vmap(footprint_mats, in_axes=(0, None, None))(angle_index, row_global, rows_total)
    tile_count = column_count // LANES
    tiles = columns.astype(jnp.float32).reshape(P_SIZE, depth_count, tile_count, LANES)
    tiles = jnp.pad(tiles.transpose(0, 2, 1, 3), ((0, 0), (1, 2), (0, 0), (0, 0)))
    summed = backproject(shifts, tiles, mats, column_count)
    backprojection = math.pi / P_SIZE * summed
    current = backprojection
    extended = with_wide_halo(backprojection, ITERS)
    fidelity = extended
    current = extended
    for turn_index in range(ITERS):
        reach = ITERS - turn_index
        current = smooth_update(
            current, fidelity, row_base - reach, depth_base - reach, rows_total, depth_total
        )[1:-1, 1:-1]
        fidelity = fidelity[1:-1, 1:-1]
    return current


def solution(mesh):
    return jax.shard_map(
        per_device,
        mesh=mesh,
        in_specs=(P(None, "gz", "gy"), P(), P(None, "gz"), P(None, "gz"), P(None, "gy", None)),
        out_specs=P("gy", "gz", None),
        check_vma=False,
    )
```

```python
import functools
import math

import jax
import jax.numpy as jnp
from jax import lax
from jax.experimental import pallas as pl
from jax.experimental.pallas import tpu as pltpu
from jax.sharding import PartitionSpec as P

X = 4096
P_SIZE = 16
NANG = 3600
BLOCK = 64
LANES = 128
ITERS = 2


step_length = 0.25
smooth_weight = 0.3
gradient_floor = 0.01
shift_reach = 8.0


def with_halo(cells, sides, width):
    for axis, dim in sides:
        count = lax.axis_size(axis)
        ends = count - 1
        head = lax.slice_in_dim(cells, 0, width, axis=dim)
        tail = lax.slice_in_dim(cells, cells.shape[dim] - width, cells.shape[dim], axis=dim)
        cells = jnp.concatenate(
            [
                lax.ppermute(tail, axis, [(i, (i + 1) % count) for i in range(ends)]),
                cells,
                lax.ppermute(head, axis, [((i + 1) % count, i) for i in range(ends)]),
            ],
            axis=dim,
        )
    return cells


def gather_kernel(count, local_ref, out_ref, send_sem, recv_sem, own_sem):
    ring = count // 2
    forward_steps = ring // 2
    backward_steps = ring - 1 - forward_steps
    me = lax.axis_index("gy")
    depth_index = lax.axis_index("gz")
    half = me // ring
    place = me % ring
    width = local_ref.shape[2]
    mesh_kind = pl.DeviceIdType.MESH

    def device(half_of, place_of):
        return half_of * ring + lax.rem(place_of + 2 * ring, ring)

    partner = device(1 - half, place)
    right = device(half, place + 1)
    left = device(half, place - 1)

    def slot(index):
        return out_ref.at[:, :, pl.ds(pl.multiple_of(index * width, width), width)]

    barrier = pltpu.get_barrier_semaphore()
    for peer in (partner, right, left):
        pl.semaphore_signal(barrier, inc=1, device_id=(depth_index, peer), device_id_type=mesh_kind)
    pl.semaphore_wait(barrier, 3)

    own = pltpu.make_async_copy(local_ref, slot(me), own_sem)
    own.start()
    sends = []

    def send(source, index, peer):
        copy = pltpu.make_async_remote_copy(
            src_ref=source,
            dst_ref=slot(index),
            send_sem=send_sem.at[len(sends)],
            recv_sem=recv_sem.at[index],
            device_id=(depth_index, peer),
            device_id_type=mesh_kind,
        )
        copy.start()
        sends.append(copy)

    def arrived(index):
        pltpu.make_async_remote_copy(
            src_ref=local_ref,
            dst_ref=slot(index),
            send_sem=send_sem.at[0],
            recv_sem=recv_sem.at[index],
            device_id=(depth_index, partner),
            device_id_type=mesh_kind,
        ).wait_recv()

    send(local_ref, me, partner)
    arrived(partner)
    for step in range(1, forward_steps + 1):
        for direction, peer, limit in ((-1, right, forward_steps), (1, left, backward_steps)):
            if step > limit:
                continue
            if step == 1:
                send(local_ref, me, peer)
                send(slot(partner), partner, peer)
                continue
            for half_of in (0, 1):
                index = device(half_of, place + direction * (step - 1))
                arrived(index)
                send(slot(index), index, peer)
    for direction, steps in ((-1, forward_steps), (1, backward_steps)):
        for half_of in (0, 1):
            arrived(device(half_of, place + direction * steps))
    own.wait()
    for copy in sends:
        copy.wait_send()


def gather_columns(local):
    count = lax.axis_size("gy")
    rows, depth, width = local.shape
    return pl.pallas_call(
        functools.partial(gather_kernel, count),
        out_shape=jax.ShapeDtypeStruct((rows, depth, width * count), local.dtype),
        in_specs=[pl.BlockSpec(memory_space=pl.ANY)],
        out_specs=pl.BlockSpec(memory_space=pl.ANY),
        scratch_shapes=[
            pltpu.SemaphoreType.DMA((count,)),
            pltpu.SemaphoreType.DMA((count,)),
            pltpu.SemaphoreType.DMA(()),
        ],
        compiler_params=pltpu.CompilerParams(collective_id=0, has_side_effects=True),
    )(local)


STEPS = ((1, 1), (1, 0), (1, -1), (0, 1), (0, -1), (-1, 1), (-1, 0), (-1, -1))


def halo_kernel(count, *refs):
    pieces = len(STEPS)
    sources, targets = refs[:pieces], refs[pieces:2 * pieces]
    send_sem, recv_sem = refs[2 * pieces], refs[2 * pieces + 1]
    row_count, depth_count = count
    row_me = lax.axis_index("gy")
    depth_me = lax.axis_index("gz")
    peers = [
        (lax.rem(depth_me + depth_step + depth_count, depth_count),
         lax.rem(row_me + row_step + row_count, row_count))
        for row_step, depth_step in STEPS
    ]
    barrier = pltpu.get_barrier_semaphore()
    for peer in peers:
        pl.semaphore_signal(barrier, inc=1, device_id=peer, device_id_type=pl.DeviceIdType.MESH)
    pl.semaphore_wait(barrier, pieces)
    copies = []
    for k, peer in enumerate(peers):
        copy = pltpu.make_async_remote_copy(
            src_ref=sources[k],
            dst_ref=targets[k],
            send_sem=send_sem.at[k],
            recv_sem=recv_sem.at[k],
            device_id=peer,
            device_id_type=pl.DeviceIdType.MESH,
        )
        copy.start()
        copies.append(copy)
    for copy in copies:
        copy.wait()


def with_wide_halo(cells, width):
    rows, depth = cells.shape[0], cells.shape[1]
    count = (lax.axis_size("gy"), lax.axis_size("gz"))
    row_parts = {1: slice(rows - width, rows), 0: slice(None), -1: slice(0, width)}
    depth_parts = {1: slice(depth - width, depth), 0: slice(None), -1: slice(0, width)}
    sent = [cells[row_parts[r], depth_parts[d]] for r, d in STEPS]
    received = pl.pallas_call(
        functools.partial(halo_kernel, count),
        out_shape=[jax.ShapeDtypeStruct(piece.shape, piece.dtype) for piece in sent],
        in_specs=[pl.BlockSpec(memory_space=pl.ANY)] * len(STEPS),
        out_specs=[pl.BlockSpec(memory_space=pl.ANY)] * len(STEPS),
        scratch_shapes=[
            pltpu.SemaphoreType.DMA((len(STEPS),)),
            pltpu.SemaphoreType.DMA((len(STEPS),)),
        ],
        compiler_params=pltpu.CompilerParams(collective_id=1, has_side_effects=True),
    )(*sent)
    parts = dict(zip(STEPS, received))
    parts[(0, 0)] = cells
    bands = [
        jnp.concatenate([parts[(r, 1)], parts[(r, 0)], parts[(r, -1)]], axis=1) for r in (1, 0, -1)
    ]
    return jnp.concatenate(bands, axis=0)


def geometry(angle_value):
    radians = 2.0 * math.pi * angle_value.astype(jnp.float32) / NANG
    stretch = 0.5 + 0.5 * jnp.abs(jnp.cos(radians))
    spread = 1.0 + jnp.abs(jnp.sin(radians))
    return (radians, stretch, spread)


def footprint(radians, stretch, spread, row_global, rows_total, block_size):
    shifted = shift_reach * jnp.sin(radians + 2.0 * math.pi * row_global / rows_total)
    inside = jnp.arange(block_size).astype(jnp.float32) - 0.5 * (block_size - 1)
    centre = block_size + inside[None, :] * stretch + shifted[:, None]
    places = jnp.arange(2 * block_size).astype(jnp.float32) + 0.5
    weights = (
        jnp.maximum(0.0, 1.0 - jnp.abs(places[None, None, :] - centre[:, :, None]) / spread)
        / spread
    )
    return weights.astype(jnp.bfloat16)


def axial_table(offsets, lengths, depth_count):
    offset_real = offsets.astype(jnp.float32)[..., None]
    length_real = lengths.astype(jnp.float32)[..., None]
    depth_place = jnp.arange(depth_count).astype(jnp.float32) + 0.5
    centre = offset_real + depth_place * length_real / depth_count
    row_number = jnp.arange(2 * depth_count)
    row_place = row_number.astype(jnp.float32) + 0.5
    triangle = jnp.maximum(0.0, 1.0 - jnp.abs(row_place - centre[..., None]))
    inside = (row_number >= offsets[..., None, None]) & (
        row_number < (offsets + lengths)[..., None, None]
    )
    return jnp.where(inside, triangle, 0.0).astype(jnp.bfloat16)


def smooth_update(current, fidelity, row_first, depth_first, rows_total, depth_total):
    row_index = row_first + jnp.arange(current.shape[0])
    depth_index = depth_first + jnp.arange(current.shape[1])
    keep_rows = ((row_index >= 0) & (row_index < rows_total - 1)).astype(jnp.float32)[:, None, None]
    keep_depth = ((depth_index >= 0) & (depth_index < depth_total - 1)).astype(jnp.float32)[
        None, :, None
    ]
    forward_rows = (
        jnp.concatenate([current[1:] - current[:-1], jnp.zeros_like(current[:1])], 0) * keep_rows
    )
    forward_depth = (
        jnp.concatenate([current[:, 1:] - current[:, :-1], jnp.zeros_like(current[:, :1])], 1)
        * keep_depth
    )
    forward_width = jnp.concatenate(
        [current[:, :, 1:] - current[:, :, :-1], jnp.zeros_like(current[:, :, :1])], 2
    )
    inverse = lax.rsqrt(
        forward_rows * forward_rows
        + forward_depth * forward_depth
        + forward_width * forward_width
        + gradient_floor
    )
    normal_rows = forward_rows * inverse
    normal_depth = forward_depth * inverse
    normal_width = forward_width * inverse
    divergence = normal_rows - jnp.concatenate(
        [jnp.zeros_like(normal_rows[:1]), normal_rows[:-1]], 0
    )
    divergence = (
        divergence
        + normal_depth
        - jnp.concatenate([jnp.zeros_like(normal_depth[:, :1]), normal_depth[:, :-1]], 1)
    )
    divergence = (
        divergence
        + normal_width
        - jnp.concatenate([jnp.zeros_like(normal_width[:, :, :1]), normal_width[:, :, :-1]], 2)
    )
    return current + step_length * (smooth_weight * divergence - (current - fidelity))


def footprint_mats(angle_value, row_global, rows_total):
    radians, stretch, spread = geometry(angle_value)
    shifted = shift_reach * jnp.sin(radians + 2.0 * math.pi * row_global / rows_total)
    inside = jnp.arange(BLOCK).astype(jnp.float32) - 0.5 * (BLOCK - 1)
    centre = BLOCK + inside[None, :] * stretch + shifted[:, None]
    centre = jnp.concatenate([centre, centre], axis=1)
    places = jnp.arange(LANES).astype(jnp.float32)[:, None] + 0.5
    weights = (
        jnp.maximum(0.0, 1.0 - jnp.abs(places[None] - centre[:, None, :]) / spread) / spread
    )
    return weights.astype(jnp.bfloat16)


def backproject_kernel(shift_ref, tiles_ref, mats_ref, out_ref):
    p = pl.program_id(0)
    tile_count = out_ref.shape[2] // LANES
    depth_count = out_ref.shape[1]

    @pl.when(p == 0)
    def _():
        out_ref[...] = jnp.zeros_like(out_ref)

    ends = jnp.concatenate([tiles_ref[0, 1], tiles_ref[0, tile_count]], axis=0).astype(jnp.bfloat16)
    second_half = lax.broadcasted_iota(jnp.int32, (LANES, LANES), 1) >= BLOCK
    empty = jnp.zeros((BLOCK, LANES), jnp.bfloat16)
    for row in range(out_ref.shape[0]):
        shift = shift_ref[p, row]
        start = (shift + 2) // 2
        odd = jnp.full((LANES, LANES), shift - 2 * (start - 1), jnp.int32) == 1
        whole = mats_ref[0, row]
        down = jnp.concatenate([empty, whole[:BLOCK]], axis=0)
        up = jnp.concatenate([whole[BLOCK:], empty], axis=0)
        nothing = jnp.zeros_like(whole)
        first = jnp.where(
            second_half, jnp.where(odd, nothing, down), jnp.where(odd, down, whole)
        )
        second = jnp.where(
            second_half, jnp.where(odd, whole, up), jnp.where(odd, up, nothing)
        )
        low = tiles_ref[0, pl.ds(start, tile_count)].reshape(tile_count * depth_count, LANES)
        high = tiles_ref[0, pl.ds(start + 1, tile_count)].reshape(tile_count * depth_count, LANES)
        taps = jnp.concatenate([low, high], axis=1).astype(jnp.bfloat16)
        result = jnp.dot(
            taps, jnp.concatenate([first, second], axis=0), preferred_element_type=jnp.float32
        )
        edge = jnp.dot(ends, whole, preferred_element_type=jnp.float32)
        shift_vec = jnp.full((depth_count, LANES), shift, jnp.int32)
        for tile in range(tile_count):
            part = result[tile * depth_count:(tile + 1) * depth_count]
            if tile == 0:
                part = jnp.where(shift_vec < 0, edge[:depth_count], part)
            elif tile == tile_count - 2:
                part = jnp.where(shift_vec >= 2, edge[depth_count:], part)
            elif tile == tile_count - 1:
                part = jnp.where(shift_vec >= 0, edge[depth_count:], part)
            lanes = pl.ds(tile * LANES, LANES)
            out_ref[row, :, lanes] = out_ref[row, :, lanes] + part


def backproject(shifts, tiles, mats, column_count):
    count, rows = shifts.shape
    depth_count = tiles.shape[2]
    return pl.pallas_call(
        backproject_kernel,
        out_shape=jax.ShapeDtypeStruct((rows, depth_count, column_count), jnp.float32),
        grid_spec=pltpu.PrefetchScalarGridSpec(
            num_scalar_prefetch=1,
            grid=(count,),
            in_specs=[
                pl.BlockSpec((1,) + tiles.shape[1:], lambda p, s: (p, 0, 0, 0)),
                pl.BlockSpec((1,) + mats.shape[1:], lambda p, s: (p, 0, 0, 0)),
            ],
            out_specs=pl.BlockSpec((rows, depth_count, column_count), lambda p, s: (0, 0, 0)),
        ),
        compiler_params=pltpu.CompilerParams(dimension_semantics=("arbitrary",)),
    )(shifts, tiles, mats)


def per_device(filtered, angle_index, band_offset, band_length, foot_block):
    depth_count = filtered.shape[1]
    row_count = foot_block.shape[1]
    extended_band = with_halo(filtered, (("gz", 1),), depth_count // 2)
    axial_weights = axial_table(band_offset[:, 0], band_length[:, 0], depth_count)
    summed_rows = jnp.einsum(
        "pzv,pvu->pzu",
        axial_weights,
        extended_band,
        preferred_element_type=jnp.float32,
    )
    columns = gather_columns(summed_rows.astype(jnp.bfloat16))
    column_count = columns.shape[2]
    row_base = lax.axis_index("gy") * row_count
    depth_base = lax.axis_index("gz") * depth_count
    rows_total = lax.axis_size("gy") * row_count
    depth_total = lax.axis_size("gz") * depth_count
    row_global = (row_base + jnp.arange(row_count)).astype(jnp.float32)
    shifts = foot_block[:, :, 2] - 2
    mats = jax.vmap(footprint_mats, in_axes=(0, None, None))(angle_index, row_global, rows_total)
    tile_count = column_count // LANES
    tiles = columns.astype(jnp.float32).reshape(P_SIZE, depth_count, tile_count, LANES)
    tiles = jnp.pad(tiles.transpose(0, 2, 1, 3), ((0, 0), (1, 2), (0, 0), (0, 0)))
    summed = backproject(shifts, tiles, mats, column_count)
    backprojection = math.pi / P_SIZE * summed
    current = backprojection
    extended = with_wide_halo(backprojection, ITERS)
    fidelity = extended
    current = extended
    for turn_index in range(ITERS):
        reach = ITERS - turn_index
        current = smooth_update(
            current, fidelity, row_base - reach, depth_base - reach, rows_total, depth_total
        )[1:-1, 1:-1]
        fidelity = fidelity[1:-1, 1:-1]
    return current


def solution(mesh):
    return jax.shard_map(
        per_device,
        mesh=mesh,
        in_specs=(P(None, "gz", "gy"), P(), P(None, "gz"), P(None, "gz"), P(None, "gy", None)),
        out_specs=P("gy", "gz", None),
        check_vma=False,
    )
```

```python
import functools
import math

import jax
import jax.numpy as jnp
from jax import lax
from jax.experimental import pallas as pl
from jax.experimental.pallas import tpu as pltpu
from jax.sharding import PartitionSpec as P

X = 4096
P_SIZE = 16
NANG = 3600
BLOCK = 64
LANES = 128
ITERS = 2


step_length = 0.25
smooth_weight = 0.3
gradient_floor = 0.01
shift_reach = 8.0


def with_halo(cells, sides, width):
    for axis, dim in sides:
        count = lax.axis_size(axis)
        ends = count - 1
        head = lax.slice_in_dim(cells, 0, width, axis=dim)
        tail = lax.slice_in_dim(cells, cells.shape[dim] - width, cells.shape[dim], axis=dim)
        cells = jnp.concatenate(
            [
                lax.ppermute(tail, axis, [(i, (i + 1) % count) for i in range(ends)]),
                cells,
                lax.ppermute(head, axis, [((i + 1) % count, i) for i in range(ends)]),
            ],
            axis=dim,
        )
    return cells


def gather_kernel(count, local_ref, out_ref, send_sem, recv_sem, own_sem):
    ring = count // 2
    forward_steps = ring // 2
    backward_steps = ring - 1 - forward_steps
    me = lax.axis_index("gy")
    depth_index = lax.axis_index("gz")
    half = me // ring
    place = me % ring
    width = local_ref.shape[2]
    mesh_kind = pl.DeviceIdType.MESH

    def device(half_of, place_of):
        return half_of * ring + lax.rem(place_of + 2 * ring, ring)

    partner = device(1 - half, place)
    right = device(half, place + 1)
    left = device(half, place - 1)

    def slot(index):
        return out_ref.at[:, :, pl.ds(pl.multiple_of(index * width, width), width)]

    barrier = pltpu.get_barrier_semaphore()
    for peer in (partner, right, left):
        pl.semaphore_signal(barrier, inc=1, device_id=(depth_index, peer), device_id_type=mesh_kind)
    pl.semaphore_wait(barrier, 3)

    own = pltpu.make_async_copy(local_ref, slot(me), own_sem)
    own.start()
    sends = []

    def send(source, index, peer):
        copy = pltpu.make_async_remote_copy(
            src_ref=source,
            dst_ref=slot(index),
            send_sem=send_sem.at[len(sends)],
            recv_sem=recv_sem.at[index],
            device_id=(depth_index, peer),
            device_id_type=mesh_kind,
        )
        copy.start()
        sends.append(copy)

    def arrived(index):
        pltpu.make_async_remote_copy(
            src_ref=local_ref,
            dst_ref=slot(index),
            send_sem=send_sem.at[0],
            recv_sem=recv_sem.at[index],
            device_id=(depth_index, partner),
            device_id_type=mesh_kind,
        ).wait_recv()

    send(local_ref, me, partner)
    arrived(partner)
    for step in range(1, forward_steps + 1):
        for direction, peer, limit in ((-1, right, forward_steps), (1, left, backward_steps)):
            if step > limit:
                continue
            if step == 1:
                send(local_ref, me, peer)
                send(slot(partner), partner, peer)
                continue
            for half_of in (0, 1):
                index = device(half_of, place + direction * (step - 1))
                arrived(index)
                send(slot(index), index, peer)
    for direction, steps in ((-1, forward_steps), (1, backward_steps)):
        for half_of in (0, 1):
            arrived(device(half_of, place + direction * steps))
    own.wait()
    for copy in sends:
        copy.wait_send()


def gather_columns(local):
    count = lax.axis_size("gy")
    rows, depth, width = local.shape
    return pl.pallas_call(
        functools.partial(gather_kernel, count),
        out_shape=jax.ShapeDtypeStruct((rows, depth, width * count), local.dtype),
        in_specs=[pl.BlockSpec(memory_space=pl.ANY)],
        out_specs=pl.BlockSpec(memory_space=pl.ANY),
        scratch_shapes=[
            pltpu.SemaphoreType.DMA((count,)),
            pltpu.SemaphoreType.DMA((count,)),
            pltpu.SemaphoreType.DMA(()),
        ],
        compiler_params=pltpu.CompilerParams(collective_id=0, has_side_effects=True),
    )(local)


STEPS = ((1, 1), (1, 0), (1, -1), (0, 1), (0, -1), (-1, 1), (-1, 0), (-1, -1))


def halo_kernel(count, *refs):
    pieces = len(STEPS)
    sources, targets = refs[:pieces], refs[pieces:2 * pieces]
    send_sem, recv_sem = refs[2 * pieces], refs[2 * pieces + 1]
    row_count, depth_count = count
    row_me = lax.axis_index("gy")
    depth_me = lax.axis_index("gz")
    peers = [
        (lax.rem(depth_me + depth_step + depth_count, depth_count),
         lax.rem(row_me + row_step + row_count, row_count))
        for row_step, depth_step in STEPS
    ]
    barrier = pltpu.get_barrier_semaphore()
    for peer in peers:
        pl.semaphore_signal(barrier, inc=1, device_id=peer, device_id_type=pl.DeviceIdType.MESH)
    pl.semaphore_wait(barrier, pieces)
    copies = []
    for k, peer in enumerate(peers):
        copy = pltpu.make_async_remote_copy(
            src_ref=sources[k],
            dst_ref=targets[k],
            send_sem=send_sem.at[k],
            recv_sem=recv_sem.at[k],
            device_id=peer,
            device_id_type=pl.DeviceIdType.MESH,
        )
        copy.start()
        copies.append(copy)
    for copy in copies:
        copy.wait()


def with_wide_halo(cells, width):
    rows, depth = cells.shape[0], cells.shape[1]
    count = (lax.axis_size("gy"), lax.axis_size("gz"))
    row_parts = {1: slice(rows - width, rows), 0: slice(None), -1: slice(0, width)}
    depth_parts = {1: slice(depth - width, depth), 0: slice(None), -1: slice(0, width)}
    sent = [cells[row_parts[r], depth_parts[d]] for r, d in STEPS]
    received = pl.pallas_call(
        functools.partial(halo_kernel, count),
        out_shape=[jax.ShapeDtypeStruct(piece.shape, piece.dtype) for piece in sent],
        in_specs=[pl.BlockSpec(memory_space=pl.ANY)] * len(STEPS),
        out_specs=[pl.BlockSpec(memory_space=pl.ANY)] * len(STEPS),
        scratch_shapes=[
            pltpu.SemaphoreType.DMA((len(STEPS),)),
            pltpu.SemaphoreType.DMA((len(STEPS),)),
        ],
        compiler_params=pltpu.CompilerParams(collective_id=1, has_side_effects=True),
    )(*sent)
    parts = dict(zip(STEPS, received))
    parts[(0, 0)] = cells
    bands = [
        jnp.concatenate([parts[(r, 1)], parts[(r, 0)], parts[(r, -1)]], axis=1) for r in (1, 0, -1)
    ]
    return jnp.concatenate(bands, axis=0)


def geometry(angle_value):
    radians = 2.0 * math.pi * angle_value.astype(jnp.float32) / NANG
    stretch = 0.5 + 0.5 * jnp.abs(jnp.cos(radians))
    spread = 1.0 + jnp.abs(jnp.sin(radians))
    return (radians, stretch, spread)


def footprint(radians, stretch, spread, row_global, rows_total, block_size):
    shifted = shift_reach * jnp.sin(radians + 2.0 * math.pi * row_global / rows_total)
    inside = jnp.arange(block_size).astype(jnp.float32) - 0.5 * (block_size - 1)
    centre = block_size + inside[None, :] * stretch + shifted[:, None]
    places = jnp.arange(2 * block_size).astype(jnp.float32) + 0.5
    weights = (
        jnp.maximum(0.0, 1.0 - jnp.abs(places[None, None, :] - centre[:, :, None]) / spread)
        / spread
    )
    return weights.astype(jnp.bfloat16)


def axial_table(offsets, lengths, depth_count):
    offset_real = offsets.astype(jnp.float32)[..., None]
    length_real = lengths.astype(jnp.float32)[..., None]
    depth_place = jnp.arange(depth_count).astype(jnp.float32) + 0.5
    centre = offset_real + depth_place * length_real / depth_count
    row_number = jnp.arange(2 * depth_count)
    row_place = row_number.astype(jnp.float32) + 0.5
    triangle = jnp.maximum(0.0, 1.0 - jnp.abs(row_place - centre[..., None]))
    inside = (row_number >= offsets[..., None, None]) & (
        row_number < (offsets + lengths)[..., None, None]
    )
    return jnp.where(inside, triangle, 0.0).astype(jnp.bfloat16)


def smooth_update(current, fidelity, row_first, depth_first, rows_total, depth_total):
    row_index = row_first + jnp.arange(current.shape[0])
    depth_index = depth_first + jnp.arange(current.shape[1])
    keep_rows = ((row_index >= 0) & (row_index < rows_total - 1)).astype(jnp.float32)[:, None, None]
    keep_depth = ((depth_index >= 0) & (depth_index < depth_total - 1)).astype(jnp.float32)[
        None, :, None
    ]
    forward_rows = (
        jnp.concatenate([current[1:] - current[:-1], jnp.zeros_like(current[:1])], 0) * keep_rows
    )
    forward_depth = (
        jnp.concatenate([current[:, 1:] - current[:, :-1], jnp.zeros_like(current[:, :1])], 1)
        * keep_depth
    )
    forward_width = jnp.concatenate(
        [current[:, :, 1:] - current[:, :, :-1], jnp.zeros_like(current[:, :, :1])], 2
    )
    inverse = lax.rsqrt(
        forward_rows * forward_rows
        + forward_depth * forward_depth
        + forward_width * forward_width
        + gradient_floor
    )
    normal_rows = forward_rows * inverse
    normal_depth = forward_depth * inverse
    normal_width = forward_width * inverse
    divergence = normal_rows - jnp.concatenate(
        [jnp.zeros_like(normal_rows[:1]), normal_rows[:-1]], 0
    )
    divergence = (
        divergence
        + normal_depth
        - jnp.concatenate([jnp.zeros_like(normal_depth[:, :1]), normal_depth[:, :-1]], 1)
    )
    divergence = (
        divergence
        + normal_width
        - jnp.concatenate([jnp.zeros_like(normal_width[:, :, :1]), normal_width[:, :, :-1]], 2)
    )
    return current + step_length * (smooth_weight * divergence - (current - fidelity))


def footprint_mats(angle_value, row_global, rows_total):
    radians, stretch, spread = geometry(angle_value)
    shifted = shift_reach * jnp.sin(radians + 2.0 * math.pi * row_global / rows_total)
    inside = jnp.arange(BLOCK).astype(jnp.float32) - 0.5 * (BLOCK - 1)
    centre = BLOCK + inside[None, :] * stretch + shifted[:, None]
    centre = jnp.concatenate([centre, centre], axis=1)
    places = jnp.arange(LANES).astype(jnp.float32)[:, None] + 0.5
    weights = (
        jnp.maximum(0.0, 1.0 - jnp.abs(places[None] - centre[:, None, :]) / spread) / spread
    )
    return weights.astype(jnp.bfloat16)


def backproject_kernel(shift_ref, columns_ref, mats_ref, out_ref, tiles_ref):
    p = pl.program_id(0)
    tile_count = out_ref.shape[2] // LANES
    depth_count = out_ref.shape[1]

    @pl.when(p == 0)
    def _():
        out_ref[...] = jnp.zeros_like(out_ref)
        tiles_ref[...] = jnp.zeros_like(tiles_ref)

    for tile in range(tile_count):
        tiles_ref[0, tile + 1] = columns_ref[0, :, tile * LANES:(tile + 1) * LANES].astype(
            jnp.float32
        )

    ends = jnp.concatenate([tiles_ref[0, 1], tiles_ref[0, tile_count]], axis=0).astype(jnp.bfloat16)
    second_half = lax.broadcasted_iota(jnp.int32, (LANES, LANES), 1) >= BLOCK
    empty = jnp.zeros((BLOCK, LANES), jnp.bfloat16)
    for row in range(out_ref.shape[0]):
        shift = shift_ref[p, row]
        start = (shift + 2) // 2
        odd = jnp.full((LANES, LANES), shift - 2 * (start - 1), jnp.int32) == 1
        whole = mats_ref[0, row]
        down = jnp.concatenate([empty, whole[:BLOCK]], axis=0)
        up = jnp.concatenate([whole[BLOCK:], empty], axis=0)
        nothing = jnp.zeros_like(whole)
        first = jnp.where(
            second_half, jnp.where(odd, nothing, down), jnp.where(odd, down, whole)
        )
        second = jnp.where(
            second_half, jnp.where(odd, whole, up), jnp.where(odd, up, nothing)
        )
        low = tiles_ref[0, pl.ds(start, tile_count)].reshape(tile_count * depth_count, LANES)
        high = tiles_ref[0, pl.ds(start + 1, tile_count)].reshape(tile_count * depth_count, LANES)
        taps = jnp.concatenate([low, high], axis=1).astype(jnp.bfloat16)
        result = jnp.dot(
            taps, jnp.concatenate([first, second], axis=0), preferred_element_type=jnp.float32
        )
        edge = jnp.dot(ends, whole, preferred_element_type=jnp.float32)
        shift_vec = jnp.full((depth_count, LANES), shift, jnp.int32)
        for tile in range(tile_count):
            part = result[tile * depth_count:(tile + 1) * depth_count]
            if tile == 0:
                part = jnp.where(shift_vec < 0, edge[:depth_count], part)
            elif tile == tile_count - 2:
                part = jnp.where(shift_vec >= 2, edge[depth_count:], part)
            elif tile == tile_count - 1:
                part = jnp.where(shift_vec >= 0, edge[depth_count:], part)
            lanes = pl.ds(tile * LANES, LANES)
            out_ref[row, :, lanes] = out_ref[row, :, lanes] + part

    @pl.when(p == pl.num_programs(0) - 1)
    def _():
        out_ref[...] = math.pi / P_SIZE * out_ref[...]


def backproject(shifts, columns, mats):
    count, rows = shifts.shape
    depth_count, column_count = columns.shape[1], columns.shape[2]
    tile_count = column_count // LANES
    return pl.pallas_call(
        backproject_kernel,
        out_shape=jax.ShapeDtypeStruct((rows, depth_count, column_count), jnp.float32),
        grid_spec=pltpu.PrefetchScalarGridSpec(
            num_scalar_prefetch=1,
            grid=(count,),
            in_specs=[
                pl.BlockSpec((1,) + columns.shape[1:], lambda p, s: (p, 0, 0)),
                pl.BlockSpec((1,) + mats.shape[1:], lambda p, s: (p, 0, 0, 0)),
            ],
            out_specs=pl.BlockSpec((rows, depth_count, column_count), lambda p, s: (0, 0, 0)),
            scratch_shapes=[pltpu.VMEM((1, tile_count + 3, depth_count, LANES), jnp.float32)],
        ),
        compiler_params=pltpu.CompilerParams(dimension_semantics=("arbitrary",)),
    )(shifts, columns, mats)


def per_device(filtered, angle_index, band_offset, band_length, foot_block):
    depth_count = filtered.shape[1]
    row_count = foot_block.shape[1]
    extended_band = with_halo(filtered, (("gz", 1),), depth_count // 2)
    axial_weights = axial_table(band_offset[:, 0], band_length[:, 0], depth_count)
    summed_rows = jnp.einsum(
        "pzv,pvu->pzu",
        axial_weights,
        extended_band,
        preferred_element_type=jnp.float32,
    )
    columns = gather_columns(summed_rows.astype(jnp.bfloat16))
    column_count = columns.shape[2]
    row_base = lax.axis_index("gy") * row_count
    depth_base = lax.axis_index("gz") * depth_count
    rows_total = lax.axis_size("gy") * row_count
    depth_total = lax.axis_size("gz") * depth_count
    row_global = (row_base + jnp.arange(row_count)).astype(jnp.float32)
    shifts = foot_block[:, :, 2] - 2
    mats = jax.vmap(footprint_mats, in_axes=(0, None, None))(angle_index, row_global, rows_total)
    backprojection = backproject(shifts, columns, mats)
    current = backprojection
    extended = with_wide_halo(backprojection, ITERS)
    fidelity = extended
    current = extended
    for turn_index in range(ITERS):
        reach = ITERS - turn_index
        current = smooth_update(
            current, fidelity, row_base - reach, depth_base - reach, rows_total, depth_total
        )[1:-1, 1:-1]
        fidelity = fidelity[1:-1, 1:-1]
    return current


def solution(mesh):
    return jax.shard_map(
        per_device,
        mesh=mesh,
        in_specs=(P(None, "gz", "gy"), P(), P(None, "gz"), P(None, "gz"), P(None, "gy", None)),
        out_specs=P("gy", "gz", None),
        check_vma=False,
    )
```

```python
import functools
import math

import jax
import jax.numpy as jnp
from jax import lax
from jax.experimental import pallas as pl
from jax.experimental.pallas import tpu as pltpu
from jax.sharding import PartitionSpec as P

X = 4096
P_SIZE = 16
NANG = 3600
BLOCK = 64
LANES = 128
ITERS = 2


step_length = 0.25
smooth_weight = 0.3
gradient_floor = 0.01
shift_reach = 8.0


def with_halo(cells, sides, width):
    for axis, dim in sides:
        count = lax.axis_size(axis)
        ends = count - 1
        head = lax.slice_in_dim(cells, 0, width, axis=dim)
        tail = lax.slice_in_dim(cells, cells.shape[dim] - width, cells.shape[dim], axis=dim)
        cells = jnp.concatenate(
            [
                lax.ppermute(tail, axis, [(i, (i + 1) % count) for i in range(ends)]),
                cells,
                lax.ppermute(head, axis, [((i + 1) % count, i) for i in range(ends)]),
            ],
            axis=dim,
        )
    return cells


def gather_kernel(count, local_ref, out_ref, send_sem, recv_sem, own_sem):
    ring = count // 2
    forward_steps = ring // 2
    backward_steps = ring - 1 - forward_steps
    me = lax.axis_index("gy")
    depth_index = lax.axis_index("gz")
    half = me // ring
    place = me % ring
    width = local_ref.shape[2]
    mesh_kind = pl.DeviceIdType.MESH

    def device(half_of, place_of):
        return half_of * ring + lax.rem(place_of + 2 * ring, ring)

    partner = device(1 - half, place)
    right = device(half, place + 1)
    left = device(half, place - 1)

    def slot(index):
        return out_ref.at[:, :, pl.ds(pl.multiple_of(index * width, width), width)]

    barrier = pltpu.get_barrier_semaphore()
    for peer in (partner, right, left):
        pl.semaphore_signal(barrier, inc=1, device_id=(depth_index, peer), device_id_type=mesh_kind)
    pl.semaphore_wait(barrier, 3)

    own = pltpu.make_async_copy(local_ref, slot(me), own_sem)
    own.start()
    sends = []

    def send(source, index, peer):
        copy = pltpu.make_async_remote_copy(
            src_ref=source,
            dst_ref=slot(index),
            send_sem=send_sem.at[len(sends)],
            recv_sem=recv_sem.at[index],
            device_id=(depth_index, peer),
            device_id_type=mesh_kind,
        )
        copy.start()
        sends.append(copy)

    def arrived(index):
        pltpu.make_async_remote_copy(
            src_ref=local_ref,
            dst_ref=slot(index),
            send_sem=send_sem.at[0],
            recv_sem=recv_sem.at[index],
            device_id=(depth_index, partner),
            device_id_type=mesh_kind,
        ).wait_recv()

    send(local_ref, me, partner)
    arrived(partner)
    for step in range(1, forward_steps + 1):
        for direction, peer, limit in ((-1, right, forward_steps), (1, left, backward_steps)):
            if step > limit:
                continue
            if step == 1:
                send(local_ref, me, peer)
                send(slot(partner), partner, peer)
                continue
            for half_of in (0, 1):
                index = device(half_of, place + direction * (step - 1))
                arrived(index)
                send(slot(index), index, peer)
    for direction, steps in ((-1, forward_steps), (1, backward_steps)):
        for half_of in (0, 1):
            arrived(device(half_of, place + direction * steps))
    own.wait()
    for copy in sends:
        copy.wait_send()


def gather_columns(local):
    count = lax.axis_size("gy")
    rows, depth, width = local.shape
    return pl.pallas_call(
        functools.partial(gather_kernel, count),
        out_shape=jax.ShapeDtypeStruct((rows, depth, width * count), local.dtype),
        in_specs=[pl.BlockSpec(memory_space=pl.ANY)],
        out_specs=pl.BlockSpec(memory_space=pl.ANY),
        scratch_shapes=[
            pltpu.SemaphoreType.DMA((count,)),
            pltpu.SemaphoreType.DMA((count,)),
            pltpu.SemaphoreType.DMA(()),
        ],
        compiler_params=pltpu.CompilerParams(collective_id=0, has_side_effects=True),
    )(local)


STEPS = ((1, 1), (1, 0), (1, -1), (0, 1), (0, -1), (-1, 1), (-1, 0), (-1, -1))


def halo_kernel(count, width, cells_ref, *refs):
    pieces = len(STEPS)
    targets = refs[:pieces]
    send_sem, recv_sem = refs[pieces], refs[pieces + 1]
    row_count, depth_count = count
    rows, depth = cells_ref.shape[0], cells_ref.shape[1]
    row_parts = {1: pl.ds(rows - width, width), 0: pl.ds(0, rows), -1: pl.ds(0, width)}
    depth_parts = {1: pl.ds(depth - width, width), 0: pl.ds(0, depth), -1: pl.ds(0, width)}
    row_me = lax.axis_index("gy")
    depth_me = lax.axis_index("gz")
    peers = [
        (lax.rem(depth_me + depth_step + depth_count, depth_count),
         lax.rem(row_me + row_step + row_count, row_count))
        for row_step, depth_step in STEPS
    ]
    barrier = pltpu.get_barrier_semaphore()
    for peer in peers:
        pl.semaphore_signal(barrier, inc=1, device_id=peer, device_id_type=pl.DeviceIdType.MESH)
    pl.semaphore_wait(barrier, pieces)
    copies = []
    for k, peer in enumerate(peers):
        row_step, depth_step = STEPS[k]
        copy = pltpu.make_async_remote_copy(
            src_ref=cells_ref.at[row_parts[row_step], depth_parts[depth_step]],
            dst_ref=targets[k],
            send_sem=send_sem.at[k],
            recv_sem=recv_sem.at[k],
            device_id=peer,
            device_id_type=pl.DeviceIdType.MESH,
        )
        copy.start()
        copies.append(copy)
    for copy in copies:
        copy.wait()


def with_wide_halo(cells, width):
    rows, depth = cells.shape[0], cells.shape[1]
    count = (lax.axis_size("gy"), lax.axis_size("gz"))
    row_parts = {1: slice(rows - width, rows), 0: slice(None), -1: slice(0, width)}
    depth_parts = {1: slice(depth - width, depth), 0: slice(None), -1: slice(0, width)}
    sent = [cells[row_parts[r], depth_parts[d]] for r, d in STEPS]
    received = pl.pallas_call(
        functools.partial(halo_kernel, count, width),
        out_shape=[jax.ShapeDtypeStruct(piece.shape, piece.dtype) for piece in sent],
        in_specs=[pl.BlockSpec(memory_space=pl.ANY)],
        out_specs=[pl.BlockSpec(memory_space=pl.ANY)] * len(STEPS),
        scratch_shapes=[
            pltpu.SemaphoreType.DMA((len(STEPS),)),
            pltpu.SemaphoreType.DMA((len(STEPS),)),
        ],
        compiler_params=pltpu.CompilerParams(collective_id=1, has_side_effects=True),
    )(cells)
    parts = dict(zip(STEPS, received))
    parts[(0, 0)] = cells
    bands = [
        jnp.concatenate([parts[(r, 1)], parts[(r, 0)], parts[(r, -1)]], axis=1) for r in (1, 0, -1)
    ]
    return jnp.concatenate(bands, axis=0)


def geometry(angle_value):
    radians = 2.0 * math.pi * angle_value.astype(jnp.float32) / NANG
    stretch = 0.5 + 0.5 * jnp.abs(jnp.cos(radians))
    spread = 1.0 + jnp.abs(jnp.sin(radians))
    return (radians, stretch, spread)


def footprint(radians, stretch, spread, row_global, rows_total, block_size):
    shifted = shift_reach * jnp.sin(radians + 2.0 * math.pi * row_global / rows_total)
    inside = jnp.arange(block_size).astype(jnp.float32) - 0.5 * (block_size - 1)
    centre = block_size + inside[None, :] * stretch + shifted[:, None]
    places = jnp.arange(2 * block_size).astype(jnp.float32) + 0.5
    weights = (
        jnp.maximum(0.0, 1.0 - jnp.abs(places[None, None, :] - centre[:, :, None]) / spread)
        / spread
    )
    return weights.astype(jnp.bfloat16)


def axial_table(offsets, lengths, depth_count):
    offset_real = offsets.astype(jnp.float32)[..., None]
    length_real = lengths.astype(jnp.float32)[..., None]
    depth_place = jnp.arange(depth_count).astype(jnp.float32) + 0.5
    centre = offset_real + depth_place * length_real / depth_count
    row_number = jnp.arange(2 * depth_count)
    row_place = row_number.astype(jnp.float32) + 0.5
    triangle = jnp.maximum(0.0, 1.0 - jnp.abs(row_place - centre[..., None]))
    inside = (row_number >= offsets[..., None, None]) & (
        row_number < (offsets + lengths)[..., None, None]
    )
    return jnp.where(inside, triangle, 0.0).astype(jnp.bfloat16)


def smooth_update(current, fidelity, row_first, depth_first, rows_total, depth_total):
    row_index = row_first + jnp.arange(current.shape[0])
    depth_index = depth_first + jnp.arange(current.shape[1])
    keep_rows = ((row_index >= 0) & (row_index < rows_total - 1)).astype(jnp.float32)[:, None, None]
    keep_depth = ((depth_index >= 0) & (depth_index < depth_total - 1)).astype(jnp.float32)[
        None, :, None
    ]
    forward_rows = (
        jnp.concatenate([current[1:] - current[:-1], jnp.zeros_like(current[:1])], 0) * keep_rows
    )
    forward_depth = (
        jnp.concatenate([current[:, 1:] - current[:, :-1], jnp.zeros_like(current[:, :1])], 1)
        * keep_depth
    )
    forward_width = jnp.concatenate(
        [current[:, :, 1:] - current[:, :, :-1], jnp.zeros_like(current[:, :, :1])], 2
    )
    inverse = lax.rsqrt(
        forward_rows * forward_rows
        + forward_depth * forward_depth
        + forward_width * forward_width
        + gradient_floor
    )
    normal_rows = forward_rows * inverse
    normal_depth = forward_depth * inverse
    normal_width = forward_width * inverse
    divergence = normal_rows - jnp.concatenate(
        [jnp.zeros_like(normal_rows[:1]), normal_rows[:-1]], 0
    )
    divergence = (
        divergence
        + normal_depth
        - jnp.concatenate([jnp.zeros_like(normal_depth[:, :1]), normal_depth[:, :-1]], 1)
    )
    divergence = (
        divergence
        + normal_width
        - jnp.concatenate([jnp.zeros_like(normal_width[:, :, :1]), normal_width[:, :, :-1]], 2)
    )
    return current + step_length * (smooth_weight * divergence - (current - fidelity))


def footprint_mats(angle_value, row_global, rows_total):
    radians, stretch, spread = geometry(angle_value)
    shifted = shift_reach * jnp.sin(radians + 2.0 * math.pi * row_global / rows_total)
    inside = jnp.arange(BLOCK).astype(jnp.float32) - 0.5 * (BLOCK - 1)
    centre = BLOCK + inside[None, :] * stretch + shifted[:, None]
    centre = jnp.concatenate([centre, centre], axis=1)
    places = jnp.arange(LANES).astype(jnp.float32)[:, None] + 0.5
    weights = (
        jnp.maximum(0.0, 1.0 - jnp.abs(places[None] - centre[:, None, :]) / spread) / spread
    )
    return weights.astype(jnp.bfloat16)


def backproject_kernel(shift_ref, columns_ref, mats_ref, out_ref, tiles_ref):
    p = pl.program_id(0)
    tile_count = out_ref.shape[2] // LANES
    depth_count = out_ref.shape[1]

    @pl.when(p == 0)
    def _():
        out_ref[...] = jnp.zeros_like(out_ref)
        tiles_ref[...] = jnp.zeros_like(tiles_ref)

    for tile in range(tile_count):
        tiles_ref[0, tile + 1] = columns_ref[0, :, tile * LANES:(tile + 1) * LANES].astype(
            jnp.float32
        )

    ends = jnp.concatenate([tiles_ref[0, 1], tiles_ref[0, tile_count]], axis=0).astype(jnp.bfloat16)
    second_half = lax.broadcasted_iota(jnp.int32, (LANES, LANES), 1) >= BLOCK
    empty = jnp.zeros((BLOCK, LANES), jnp.bfloat16)
    for row in range(out_ref.shape[0]):
        shift = shift_ref[p, row]
        start = (shift + 2) // 2
        odd = jnp.full((LANES, LANES), shift - 2 * (start - 1), jnp.int32) == 1
        whole = mats_ref[0, row]
        down = jnp.concatenate([empty, whole[:BLOCK]], axis=0)
        up = jnp.concatenate([whole[BLOCK:], empty], axis=0)
        nothing = jnp.zeros_like(whole)
        first = jnp.where(
            second_half, jnp.where(odd, nothing, down), jnp.where(odd, down, whole)
        )
        second = jnp.where(
            second_half, jnp.where(odd, whole, up), jnp.where(odd, up, nothing)
        )
        low = tiles_ref[0, pl.ds(start, tile_count)].reshape(tile_count * depth_count, LANES)
        high = tiles_ref[0, pl.ds(start + 1, tile_count)].reshape(tile_count * depth_count, LANES)
        taps = jnp.concatenate([low, high], axis=1).astype(jnp.bfloat16)
        result = jnp.dot(
            taps, jnp.concatenate([first, second], axis=0), preferred_element_type=jnp.float32
        )
        edge = jnp.dot(ends, whole, preferred_element_type=jnp.float32)
        shift_vec = jnp.full((depth_count, LANES), shift, jnp.int32)
        for tile in range(tile_count):
            part = result[tile * depth_count:(tile + 1) * depth_count]
            if tile == 0:
                part = jnp.where(shift_vec < 0, edge[:depth_count], part)
            elif tile == tile_count - 2:
                part = jnp.where(shift_vec >= 2, edge[depth_count:], part)
            elif tile == tile_count - 1:
                part = jnp.where(shift_vec >= 0, edge[depth_count:], part)
            lanes = pl.ds(tile * LANES, LANES)
            out_ref[row, :, lanes] = out_ref[row, :, lanes] + part

    @pl.when(p == pl.num_programs(0) - 1)
    def _():
        out_ref[...] = math.pi / P_SIZE * out_ref[...]


def backproject(shifts, columns, mats):
    count, rows = shifts.shape
    depth_count, column_count = columns.shape[1], columns.shape[2]
    tile_count = column_count // LANES
    return pl.pallas_call(
        backproject_kernel,
        out_shape=jax.ShapeDtypeStruct((rows, depth_count, column_count), jnp.float32),
        grid_spec=pltpu.PrefetchScalarGridSpec(
            num_scalar_prefetch=1,
            grid=(count,),
            in_specs=[
                pl.BlockSpec((1,) + columns.shape[1:], lambda p, s: (p, 0, 0)),
                pl.BlockSpec((1,) + mats.shape[1:], lambda p, s: (p, 0, 0, 0)),
            ],
            out_specs=pl.BlockSpec((rows, depth_count, column_count), lambda p, s: (0, 0, 0)),
            scratch_shapes=[pltpu.VMEM((1, tile_count + 3, depth_count, LANES), jnp.float32)],
        ),
        compiler_params=pltpu.CompilerParams(dimension_semantics=("arbitrary",)),
    )(shifts, columns, mats)


def per_device(filtered, angle_index, band_offset, band_length, foot_block):
    depth_count = filtered.shape[1]
    row_count = foot_block.shape[1]
    extended_band = with_halo(filtered, (("gz", 1),), depth_count // 2)
    axial_weights = axial_table(band_offset[:, 0], band_length[:, 0], depth_count)
    summed_rows = jnp.einsum(
        "pzv,pvu->pzu",
        axial_weights,
        extended_band,
        preferred_element_type=jnp.float32,
    )
    columns = gather_columns(summed_rows.astype(jnp.bfloat16))
    column_count = columns.shape[2]
    row_base = lax.axis_index("gy") * row_count
    depth_base = lax.axis_index("gz") * depth_count
    rows_total = lax.axis_size("gy") * row_count
    depth_total = lax.axis_size("gz") * depth_count
    row_global = (row_base + jnp.arange(row_count)).astype(jnp.float32)
    shifts = foot_block[:, :, 2] - 2
    mats = jax.vmap(footprint_mats, in_axes=(0, None, None))(angle_index, row_global, rows_total)
    backprojection = backproject(shifts, columns, mats)
    current = backprojection
    extended = with_wide_halo(backprojection, ITERS)
    fidelity = extended
    current = extended
    for turn_index in range(ITERS):
        reach = ITERS - turn_index
        current = smooth_update(
            current, fidelity, row_base - reach, depth_base - reach, rows_total, depth_total
        )[1:-1, 1:-1]
        fidelity = fidelity[1:-1, 1:-1]
    return current


def solution(mesh):
    return jax.shard_map(
        per_device,
        mesh=mesh,
        in_specs=(P(None, "gz", "gy"), P(), P(None, "gz"), P(None, "gz"), P(None, "gy", None)),
        out_specs=P("gy", "gz", None),
        check_vma=False,
    )
```

```python
import functools
import math

import jax
import jax.numpy as jnp
from jax import lax
from jax.experimental import pallas as pl
from jax.experimental.pallas import tpu as pltpu
from jax.sharding import PartitionSpec as P

X = 4096
P_SIZE = 16
NANG = 3600
BLOCK = 64
LANES = 128
ITERS = 2


step_length = 0.25
smooth_weight = 0.3
gradient_floor = 0.01
shift_reach = 8.0


def with_halo(cells, sides, width):
    for axis, dim in sides:
        count = lax.axis_size(axis)
        ends = count - 1
        head = lax.slice_in_dim(cells, 0, width, axis=dim)
        tail = lax.slice_in_dim(cells, cells.shape[dim] - width, cells.shape[dim], axis=dim)
        cells = jnp.concatenate(
            [
                lax.ppermute(tail, axis, [(i, (i + 1) % count) for i in range(ends)]),
                cells,
                lax.ppermute(head, axis, [((i + 1) % count, i) for i in range(ends)]),
            ],
            axis=dim,
        )
    return cells


def gather_kernel(count, local_ref, out_ref, send_sem, recv_sem, own_sem):
    ring = count // 2
    forward_steps = ring // 2
    backward_steps = ring - 1 - forward_steps
    me = lax.axis_index("gy")
    depth_index = lax.axis_index("gz")
    half = me // ring
    place = me % ring
    width = local_ref.shape[2]
    mesh_kind = pl.DeviceIdType.MESH

    def device(half_of, place_of):
        return half_of * ring + lax.rem(place_of + 2 * ring, ring)

    partner = device(1 - half, place)
    right = device(half, place + 1)
    left = device(half, place - 1)

    def slot(index):
        return out_ref.at[:, :, pl.ds(pl.multiple_of(index * width, width), width)]

    barrier = pltpu.get_barrier_semaphore()
    for peer in (partner, right, left):
        pl.semaphore_signal(barrier, inc=1, device_id=(depth_index, peer), device_id_type=mesh_kind)
    pl.semaphore_wait(barrier, 3)

    own = pltpu.make_async_copy(local_ref, slot(me), own_sem)
    own.start()
    sends = []

    def send(source, index, peer):
        copy = pltpu.make_async_remote_copy(
            src_ref=source,
            dst_ref=slot(index),
            send_sem=send_sem.at[len(sends)],
            recv_sem=recv_sem.at[index],
            device_id=(depth_index, peer),
            device_id_type=mesh_kind,
        )
        copy.start()
        sends.append(copy)

    def arrived(index):
        pltpu.make_async_remote_copy(
            src_ref=local_ref,
            dst_ref=slot(index),
            send_sem=send_sem.at[0],
            recv_sem=recv_sem.at[index],
            device_id=(depth_index, partner),
            device_id_type=mesh_kind,
        ).wait_recv()

    send(local_ref, me, partner)
    arrived(partner)
    for step in range(1, forward_steps + 1):
        for direction, peer, limit in ((-1, right, forward_steps), (1, left, backward_steps)):
            if step > limit:
                continue
            if step == 1:
                send(local_ref, me, peer)
                send(slot(partner), partner, peer)
                continue
            for half_of in (0, 1):
                index = device(half_of, place + direction * (step - 1))
                arrived(index)
                send(slot(index), index, peer)
    for direction, steps in ((-1, forward_steps), (1, backward_steps)):
        for half_of in (0, 1):
            arrived(device(half_of, place + direction * steps))
    own.wait()
    for copy in sends:
        copy.wait_send()


def gather_columns(local):
    count = lax.axis_size("gy")
    rows, depth, width = local.shape
    return pl.pallas_call(
        functools.partial(gather_kernel, count),
        out_shape=jax.ShapeDtypeStruct((rows, depth, width * count), local.dtype),
        in_specs=[pl.BlockSpec(memory_space=pl.ANY)],
        out_specs=pl.BlockSpec(memory_space=pl.ANY),
        scratch_shapes=[
            pltpu.SemaphoreType.DMA((count,)),
            pltpu.SemaphoreType.DMA((count,)),
            pltpu.SemaphoreType.DMA(()),
        ],
        compiler_params=pltpu.CompilerParams(collective_id=0, has_side_effects=True),
    )(local)


STEPS = ((1, 1), (1, 0), (1, -1), (0, 1), (0, -1), (-1, 1), (-1, 0), (-1, -1))


def halo_kernel(count, width, cells_ref, extended_ref, send_sem, recv_sem, own_sem):
    pieces = len(STEPS)
    row_count, depth_count = count
    rows, depth = cells_ref.shape[0], cells_ref.shape[1]
    row_parts = {1: pl.ds(rows - width, width), 0: pl.ds(0, rows), -1: pl.ds(0, width)}
    depth_parts = {1: pl.ds(depth - width, width), 0: pl.ds(0, depth), -1: pl.ds(0, width)}
    row_places = {1: pl.ds(0, width), 0: pl.ds(width, rows), -1: pl.ds(width + rows, width)}
    depth_places = {
        1: pl.ds(depth - width, width), 0: pl.ds(depth, depth), -1: pl.ds(2 * depth, width)
    }
    row_me = lax.axis_index("gy")
    depth_me = lax.axis_index("gz")
    peers = [
        (lax.rem(depth_me + depth_step + depth_count, depth_count),
         lax.rem(row_me + row_step + row_count, row_count))
        for row_step, depth_step in STEPS
    ]
    barrier = pltpu.get_barrier_semaphore()
    for peer in peers:
        pl.semaphore_signal(barrier, inc=1, device_id=peer, device_id_type=pl.DeviceIdType.MESH)
    own = pltpu.make_async_copy(
        cells_ref, extended_ref.at[row_places[0], depth_places[0]], own_sem
    )
    own.start()
    pl.semaphore_wait(barrier, pieces)
    copies = []
    for k, peer in enumerate(peers):
        row_step, depth_step = STEPS[k]
        copy = pltpu.make_async_remote_copy(
            src_ref=cells_ref.at[row_parts[row_step], depth_parts[depth_step]],
            dst_ref=extended_ref.at[row_places[row_step], depth_places[depth_step]],
            send_sem=send_sem.at[k],
            recv_sem=recv_sem.at[k],
            device_id=peer,
            device_id_type=pl.DeviceIdType.MESH,
        )
        copy.start()
        copies.append(copy)
    own.wait()
    for copy in copies:
        copy.wait()


def with_wide_halo(cells, width):
    rows, depth, cols = cells.shape
    count = (lax.axis_size("gy"), lax.axis_size("gz"))
    return pl.pallas_call(
        functools.partial(halo_kernel, count, width),
        out_shape=jax.ShapeDtypeStruct((rows + 2 * width, 3 * depth, cols), cells.dtype),
        in_specs=[pl.BlockSpec(memory_space=pl.ANY)],
        out_specs=pl.BlockSpec(memory_space=pl.ANY),
        scratch_shapes=[
            pltpu.SemaphoreType.DMA((len(STEPS),)),
            pltpu.SemaphoreType.DMA((len(STEPS),)),
            pltpu.SemaphoreType.DMA(()),
        ],
        compiler_params=pltpu.CompilerParams(collective_id=1, has_side_effects=True),
    )(cells)[:, depth - width:2 * depth + width]


def geometry(angle_value):
    radians = 2.0 * math.pi * angle_value.astype(jnp.float32) / NANG
    stretch = 0.5 + 0.5 * jnp.abs(jnp.cos(radians))
    spread = 1.0 + jnp.abs(jnp.sin(radians))
    return (radians, stretch, spread)


def footprint(radians, stretch, spread, row_global, rows_total, block_size):
    shifted = shift_reach * jnp.sin(radians + 2.0 * math.pi * row_global / rows_total)
    inside = jnp.arange(block_size).astype(jnp.float32) - 0.5 * (block_size - 1)
    centre = block_size + inside[None, :] * stretch + shifted[:, None]
    places = jnp.arange(2 * block_size).astype(jnp.float32) + 0.5
    weights = (
        jnp.maximum(0.0, 1.0 - jnp.abs(places[None, None, :] - centre[:, :, None]) / spread)
        / spread
    )
    return weights.astype(jnp.bfloat16)


def axial_table(offsets, lengths, depth_count):
    offset_real = offsets.astype(jnp.float32)[..., None]
    length_real = lengths.astype(jnp.float32)[..., None]
    depth_place = jnp.arange(depth_count).astype(jnp.float32) + 0.5
    centre = offset_real + depth_place * length_real / depth_count
    row_number = jnp.arange(2 * depth_count)
    row_place = row_number.astype(jnp.float32) + 0.5
    triangle = jnp.maximum(0.0, 1.0 - jnp.abs(row_place - centre[..., None]))
    inside = (row_number >= offsets[..., None, None]) & (
        row_number < (offsets + lengths)[..., None, None]
    )
    return jnp.where(inside, triangle, 0.0).astype(jnp.bfloat16)


def smooth_update(current, fidelity, row_first, depth_first, rows_total, depth_total):
    row_index = row_first + jnp.arange(current.shape[0])
    depth_index = depth_first + jnp.arange(current.shape[1])
    keep_rows = ((row_index >= 0) & (row_index < rows_total - 1)).astype(jnp.float32)[:, None, None]
    keep_depth = ((depth_index >= 0) & (depth_index < depth_total - 1)).astype(jnp.float32)[
        None, :, None
    ]
    forward_rows = (
        jnp.concatenate([current[1:] - current[:-1], jnp.zeros_like(current[:1])], 0) * keep_rows
    )
    forward_depth = (
        jnp.concatenate([current[:, 1:] - current[:, :-1], jnp.zeros_like(current[:, :1])], 1)
        * keep_depth
    )
    forward_width = jnp.concatenate(
        [current[:, :, 1:] - current[:, :, :-1], jnp.zeros_like(current[:, :, :1])], 2
    )
    inverse = lax.rsqrt(
        forward_rows * forward_rows
        + forward_depth * forward_depth
        + forward_width * forward_width
        + gradient_floor
    )
    normal_rows = forward_rows * inverse
    normal_depth = forward_depth * inverse
    normal_width = forward_width * inverse
    divergence = normal_rows - jnp.concatenate(
        [jnp.zeros_like(normal_rows[:1]), normal_rows[:-1]], 0
    )
    divergence = (
        divergence
        + normal_depth
        - jnp.concatenate([jnp.zeros_like(normal_depth[:, :1]), normal_depth[:, :-1]], 1)
    )
    divergence = (
        divergence
        + normal_width
        - jnp.concatenate([jnp.zeros_like(normal_width[:, :, :1]), normal_width[:, :, :-1]], 2)
    )
    return current + step_length * (smooth_weight * divergence - (current - fidelity))


def footprint_mats(angle_value, row_global, rows_total):
    radians, stretch, spread = geometry(angle_value)
    shifted = shift_reach * jnp.sin(radians + 2.0 * math.pi * row_global / rows_total)
    inside = jnp.arange(BLOCK).astype(jnp.float32) - 0.5 * (BLOCK - 1)
    centre = BLOCK + inside[None, :] * stretch + shifted[:, None]
    centre = jnp.concatenate([centre, centre], axis=1)
    places = jnp.arange(LANES).astype(jnp.float32)[:, None] + 0.5
    weights = (
        jnp.maximum(0.0, 1.0 - jnp.abs(places[None] - centre[:, None, :]) / spread) / spread
    )
    return weights.astype(jnp.bfloat16)


def backproject_kernel(shift_ref, columns_ref, mats_ref, out_ref, tiles_ref):
    p = pl.program_id(0)
    tile_count = out_ref.shape[2] // LANES
    depth_count = out_ref.shape[1]

    @pl.when(p == 0)
    def _():
        out_ref[...] = jnp.zeros_like(out_ref)
        tiles_ref[...] = jnp.zeros_like(tiles_ref)

    for tile in range(tile_count):
        tiles_ref[0, tile + 1] = columns_ref[0, :, tile * LANES:(tile + 1) * LANES].astype(
            jnp.float32
        )

    ends = jnp.concatenate([tiles_ref[0, 1], tiles_ref[0, tile_count]], axis=0).astype(jnp.bfloat16)
    second_half = lax.broadcasted_iota(jnp.int32, (LANES, LANES), 1) >= BLOCK
    empty = jnp.zeros((BLOCK, LANES), jnp.bfloat16)
    for row in range(out_ref.shape[0]):
        shift = shift_ref[p, row]
        start = (shift + 2) // 2
        odd = jnp.full((LANES, LANES), shift - 2 * (start - 1), jnp.int32) == 1
        whole = mats_ref[0, row]
        down = jnp.concatenate([empty, whole[:BLOCK]], axis=0)
        up = jnp.concatenate([whole[BLOCK:], empty], axis=0)
        nothing = jnp.zeros_like(whole)
        first = jnp.where(
            second_half, jnp.where(odd, nothing, down), jnp.where(odd, down, whole)
        )
        second = jnp.where(
            second_half, jnp.where(odd, whole, up), jnp.where(odd, up, nothing)
        )
        low = tiles_ref[0, pl.ds(start, tile_count)].reshape(tile_count * depth_count, LANES)
        high = tiles_ref[0, pl.ds(start + 1, tile_count)].reshape(tile_count * depth_count, LANES)
        taps = jnp.concatenate([low, high], axis=1).astype(jnp.bfloat16)
        result = jnp.dot(
            taps, jnp.concatenate([first, second], axis=0), preferred_element_type=jnp.float32
        )
        edge = jnp.dot(ends, whole, preferred_element_type=jnp.float32)
        shift_vec = jnp.full((depth_count, LANES), shift, jnp.int32)
        for tile in range(tile_count):
            part = result[tile * depth_count:(tile + 1) * depth_count]
            if tile == 0:
                part = jnp.where(shift_vec < 0, edge[:depth_count], part)
            elif tile == tile_count - 2:
                part = jnp.where(shift_vec >= 2, edge[depth_count:], part)
            elif tile == tile_count - 1:
                part = jnp.where(shift_vec >= 0, edge[depth_count:], part)
            lanes = pl.ds(tile * LANES, LANES)
            out_ref[row, :, lanes] = out_ref[row, :, lanes] + part

    @pl.when(p == pl.num_programs(0) - 1)
    def _():
        out_ref[...] = math.pi / P_SIZE * out_ref[...]


def backproject(shifts, columns, mats):
    count, rows = shifts.shape
    depth_count, column_count = columns.shape[1], columns.shape[2]
    tile_count = column_count // LANES
    return pl.pallas_call(
        backproject_kernel,
        out_shape=jax.ShapeDtypeStruct((rows, depth_count, column_count), jnp.float32),
        grid_spec=pltpu.PrefetchScalarGridSpec(
            num_scalar_prefetch=1,
            grid=(count,),
            in_specs=[
                pl.BlockSpec((1,) + columns.shape[1:], lambda p, s: (p, 0, 0)),
                pl.BlockSpec((1,) + mats.shape[1:], lambda p, s: (p, 0, 0, 0)),
            ],
            out_specs=pl.BlockSpec((rows, depth_count, column_count), lambda p, s: (0, 0, 0)),
            scratch_shapes=[pltpu.VMEM((1, tile_count + 3, depth_count, LANES), jnp.float32)],
        ),
        compiler_params=pltpu.CompilerParams(dimension_semantics=("arbitrary",)),
    )(shifts, columns, mats)


def per_device(filtered, angle_index, band_offset, band_length, foot_block):
    depth_count = filtered.shape[1]
    row_count = foot_block.shape[1]
    extended_band = with_halo(filtered, (("gz", 1),), depth_count // 2)
    axial_weights = axial_table(band_offset[:, 0], band_length[:, 0], depth_count)
    summed_rows = jnp.einsum(
        "pzv,pvu->pzu",
        axial_weights,
        extended_band,
        preferred_element_type=jnp.float32,
    )
    columns = gather_columns(summed_rows.astype(jnp.bfloat16))
    column_count = columns.shape[2]
    row_base = lax.axis_index("gy") * row_count
    depth_base = lax.axis_index("gz") * depth_count
    rows_total = lax.axis_size("gy") * row_count
    depth_total = lax.axis_size("gz") * depth_count
    row_global = (row_base + jnp.arange(row_count)).astype(jnp.float32)
    shifts = foot_block[:, :, 2] - 2
    mats = jax.vmap(footprint_mats, in_axes=(0, None, None))(angle_index, row_global, rows_total)
    backprojection = backproject(shifts, columns, mats)
    current = backprojection
    extended = with_wide_halo(backprojection, ITERS)
    fidelity = extended
    current = extended
    for turn_index in range(ITERS):
        reach = ITERS - turn_index
        current = smooth_update(
            current, fidelity, row_base - reach, depth_base - reach, rows_total, depth_total
        )[1:-1, 1:-1]
        fidelity = fidelity[1:-1, 1:-1]
    return current


def solution(mesh):
    return jax.shard_map(
        per_device,
        mesh=mesh,
        in_specs=(P(None, "gz", "gy"), P(), P(None, "gz"), P(None, "gz"), P(None, "gy", None)),
        out_specs=P("gy", "gz", None),
        check_vma=False,
    )
```

```python
import functools
import math

import jax
import jax.numpy as jnp
from jax import lax
from jax.experimental import pallas as pl
from jax.experimental.pallas import tpu as pltpu
from jax.sharding import PartitionSpec as P

X = 4096
P_SIZE = 16
NANG = 3600
BLOCK = 64
LANES = 128
GATHER_CHUNKS = 2
ITERS = 2


step_length = 0.25
smooth_weight = 0.3
gradient_floor = 0.01
shift_reach = 8.0


def with_halo(cells, sides, width):
    for axis, dim in sides:
        count = lax.axis_size(axis)
        ends = count - 1
        head = lax.slice_in_dim(cells, 0, width, axis=dim)
        tail = lax.slice_in_dim(cells, cells.shape[dim] - width, cells.shape[dim], axis=dim)
        cells = jnp.concatenate(
            [
                lax.ppermute(tail, axis, [(i, (i + 1) % count) for i in range(ends)]),
                cells,
                lax.ppermute(head, axis, [((i + 1) % count, i) for i in range(ends)]),
            ],
            axis=dim,
        )
    return cells


def gather_kernel(count, local_ref, out_ref, send_sem, recv_sem, own_sem):
    ring = count // 2
    forward_steps = ring // 2
    backward_steps = ring - 1 - forward_steps
    me = lax.axis_index("gy")
    depth_index = lax.axis_index("gz")
    half = me // ring
    place = me % ring
    width = local_ref.shape[2]
    mesh_kind = pl.DeviceIdType.MESH

    def device(half_of, place_of):
        return half_of * ring + lax.rem(place_of + 2 * ring, ring)

    partner = device(1 - half, place)
    right = device(half, place + 1)
    left = device(half, place - 1)

    chunks = GATHER_CHUNKS
    chunk_rows = local_ref.shape[0] // chunks

    def rows_of(chunk):
        return pl.ds(chunk * chunk_rows, chunk_rows)

    def slot(index, chunk):
        columns = pl.ds(pl.multiple_of(index * width, width), width)
        return out_ref.at[rows_of(chunk), :, columns]

    barrier = pltpu.get_barrier_semaphore()
    for peer in (partner, right, left):
        pl.semaphore_signal(barrier, inc=1, device_id=(depth_index, peer), device_id_type=mesh_kind)
    pl.semaphore_wait(barrier, 3)

    own = pltpu.make_async_copy(local_ref, out_ref.at[:, :, pl.ds(pl.multiple_of(me * width, width), width)], own_sem)
    own.start()
    sends = []

    def send(source, index, chunk, peer):
        copy = pltpu.make_async_remote_copy(
            src_ref=source,
            dst_ref=slot(index, chunk),
            send_sem=send_sem.at[len(sends)],
            recv_sem=recv_sem.at[index, chunk],
            device_id=(depth_index, peer),
            device_id_type=mesh_kind,
        )
        copy.start()
        sends.append(copy)

    def arrived(index, chunk):
        pltpu.make_async_remote_copy(
            src_ref=local_ref.at[rows_of(chunk)],
            dst_ref=slot(index, chunk),
            send_sem=send_sem.at[0],
            recv_sem=recv_sem.at[index, chunk],
            device_id=(depth_index, partner),
            device_id_type=mesh_kind,
        ).wait_recv()

    for chunk in range(chunks):
        send(local_ref.at[rows_of(chunk)], me, chunk, partner)
    for step in range(1, forward_steps + 1):
        for chunk in range(chunks):
            for direction, peer, limit in ((-1, right, forward_steps), (1, left, backward_steps)):
                if step > limit:
                    continue
                if step == 1:
                    send(local_ref.at[rows_of(chunk)], me, chunk, peer)
                    if direction == -1:
                        arrived(partner, chunk)
                    send(slot(partner, chunk), partner, chunk, peer)
                    continue
                for half_of in (0, 1):
                    index = device(half_of, place + direction * (step - 1))
                    arrived(index, chunk)
                    send(slot(index, chunk), index, chunk, peer)
    for direction, steps in ((-1, forward_steps), (1, backward_steps)):
        for half_of in (0, 1):
            for chunk in range(chunks):
                arrived(device(half_of, place + direction * steps), chunk)
    own.wait()
    for copy in sends:
        copy.wait_send()


def gather_columns(local):
    count = lax.axis_size("gy")
    rows, depth, width = local.shape
    return pl.pallas_call(
        functools.partial(gather_kernel, count),
        out_shape=jax.ShapeDtypeStruct((rows, depth, width * count), local.dtype),
        in_specs=[pl.BlockSpec(memory_space=pl.ANY)],
        out_specs=pl.BlockSpec(memory_space=pl.ANY),
        scratch_shapes=[
            pltpu.SemaphoreType.DMA((count * GATHER_CHUNKS,)),
            pltpu.SemaphoreType.DMA((count, GATHER_CHUNKS)),
            pltpu.SemaphoreType.DMA(()),
        ],
        compiler_params=pltpu.CompilerParams(collective_id=0, has_side_effects=True),
    )(local)


STEPS = ((1, 1), (1, 0), (1, -1), (0, 1), (0, -1), (-1, 1), (-1, 0), (-1, -1))


def halo_kernel(count, width, cells_ref, *refs):
    pieces = len(STEPS)
    targets = refs[:pieces]
    send_sem, recv_sem = refs[pieces], refs[pieces + 1]
    row_count, depth_count = count
    rows, depth = cells_ref.shape[0], cells_ref.shape[1]
    row_parts = {1: pl.ds(rows - width, width), 0: pl.ds(0, rows), -1: pl.ds(0, width)}
    depth_parts = {1: pl.ds(depth - width, width), 0: pl.ds(0, depth), -1: pl.ds(0, width)}
    row_me = lax.axis_index("gy")
    depth_me = lax.axis_index("gz")
    peers = [
        (lax.rem(depth_me + depth_step + depth_count, depth_count),
         lax.rem(row_me + row_step + row_count, row_count))
        for row_step, depth_step in STEPS
    ]
    barrier = pltpu.get_barrier_semaphore()
    for peer in peers:
        pl.semaphore_signal(barrier, inc=1, device_id=peer, device_id_type=pl.DeviceIdType.MESH)
    pl.semaphore_wait(barrier, pieces)
    copies = []
    for k, peer in enumerate(peers):
        row_step, depth_step = STEPS[k]
        copy = pltpu.make_async_remote_copy(
            src_ref=cells_ref.at[row_parts[row_step], depth_parts[depth_step]],
            dst_ref=targets[k],
            send_sem=send_sem.at[k],
            recv_sem=recv_sem.at[k],
            device_id=peer,
            device_id_type=pl.DeviceIdType.MESH,
        )
        copy.start()
        copies.append(copy)
    for copy in copies:
        copy.wait()


def with_wide_halo(cells, width):
    rows, depth = cells.shape[0], cells.shape[1]
    count = (lax.axis_size("gy"), lax.axis_size("gz"))
    row_parts = {1: slice(rows - width, rows), 0: slice(None), -1: slice(0, width)}
    depth_parts = {1: slice(depth - width, depth), 0: slice(None), -1: slice(0, width)}
    sent = [cells[row_parts[r], depth_parts[d]] for r, d in STEPS]
    received = pl.pallas_call(
        functools.partial(halo_kernel, count, width),
        out_shape=[jax.ShapeDtypeStruct(piece.shape, piece.dtype) for piece in sent],
        in_specs=[pl.BlockSpec(memory_space=pl.ANY)],
        out_specs=[pl.BlockSpec(memory_space=pl.ANY)] * len(STEPS),
        scratch_shapes=[
            pltpu.SemaphoreType.DMA((len(STEPS),)),
            pltpu.SemaphoreType.DMA((len(STEPS),)),
        ],
        compiler_params=pltpu.CompilerParams(collective_id=1, has_side_effects=True),
    )(cells)
    parts = dict(zip(STEPS, received))
    parts[(0, 0)] = cells
    bands = [
        jnp.concatenate([parts[(r, 1)], parts[(r, 0)], parts[(r, -1)]], axis=1) for r in (1, 0, -1)
    ]
    return jnp.concatenate(bands, axis=0)


def geometry(angle_value):
    radians = 2.0 * math.pi * angle_value.astype(jnp.float32) / NANG
    stretch = 0.5 + 0.5 * jnp.abs(jnp.cos(radians))
    spread = 1.0 + jnp.abs(jnp.sin(radians))
    return (radians, stretch, spread)


def footprint(radians, stretch, spread, row_global, rows_total, block_size):
    shifted = shift_reach * jnp.sin(radians + 2.0 * math.pi * row_global / rows_total)
    inside = jnp.arange(block_size).astype(jnp.float32) - 0.5 * (block_size - 1)
    centre = block_size + inside[None, :] * stretch + shifted[:, None]
    places = jnp.arange(2 * block_size).astype(jnp.float32) + 0.5
    weights = (
        jnp.maximum(0.0, 1.0 - jnp.abs(places[None, None, :] - centre[:, :, None]) / spread)
        / spread
    )
    return weights.astype(jnp.bfloat16)


def axial_table(offsets, lengths, depth_count):
    offset_real = offsets.astype(jnp.float32)[..., None]
    length_real = lengths.astype(jnp.float32)[..., None]
    depth_place = jnp.arange(depth_count).astype(jnp.float32) + 0.5
    centre = offset_real + depth_place * length_real / depth_count
    row_number = jnp.arange(2 * depth_count)
    row_place = row_number.astype(jnp.float32) + 0.5
    triangle = jnp.maximum(0.0, 1.0 - jnp.abs(row_place - centre[..., None]))
    inside = (row_number >= offsets[..., None, None]) & (
        row_number < (offsets + lengths)[..., None, None]
    )
    return jnp.where(inside, triangle, 0.0).astype(jnp.bfloat16)


def smooth_update(current, fidelity, row_first, depth_first, rows_total, depth_total):
    row_index = row_first + jnp.arange(current.shape[0])
    depth_index = depth_first + jnp.arange(current.shape[1])
    keep_rows = ((row_index >= 0) & (row_index < rows_total - 1)).astype(jnp.float32)[:, None, None]
    keep_depth = ((depth_index >= 0) & (depth_index < depth_total - 1)).astype(jnp.float32)[
        None, :, None
    ]
    forward_rows = (
        jnp.concatenate([current[1:] - current[:-1], jnp.zeros_like(current[:1])], 0) * keep_rows
    )
    forward_depth = (
        jnp.concatenate([current[:, 1:] - current[:, :-1], jnp.zeros_like(current[:, :1])], 1)
        * keep_depth
    )
    forward_width = jnp.concatenate(
        [current[:, :, 1:] - current[:, :, :-1], jnp.zeros_like(current[:, :, :1])], 2
    )
    inverse = lax.rsqrt(
        forward_rows * forward_rows
        + forward_depth * forward_depth
        + forward_width * forward_width
        + gradient_floor
    )
    normal_rows = forward_rows * inverse
    normal_depth = forward_depth * inverse
    normal_width = forward_width * inverse
    divergence = normal_rows - jnp.concatenate(
        [jnp.zeros_like(normal_rows[:1]), normal_rows[:-1]], 0
    )
    divergence = (
        divergence
        + normal_depth
        - jnp.concatenate([jnp.zeros_like(normal_depth[:, :1]), normal_depth[:, :-1]], 1)
    )
    divergence = (
        divergence
        + normal_width
        - jnp.concatenate([jnp.zeros_like(normal_width[:, :, :1]), normal_width[:, :, :-1]], 2)
    )
    return current + step_length * (smooth_weight * divergence - (current - fidelity))


def footprint_mats(angle_value, row_global, rows_total):
    radians, stretch, spread = geometry(angle_value)
    shifted = shift_reach * jnp.sin(radians + 2.0 * math.pi * row_global / rows_total)
    inside = jnp.arange(BLOCK).astype(jnp.float32) - 0.5 * (BLOCK - 1)
    centre = BLOCK + inside[None, :] * stretch + shifted[:, None]
    centre = jnp.concatenate([centre, centre], axis=1)
    places = jnp.arange(LANES).astype(jnp.float32)[:, None] + 0.5
    weights = (
        jnp.maximum(0.0, 1.0 - jnp.abs(places[None] - centre[:, None, :]) / spread) / spread
    )
    return weights.astype(jnp.bfloat16)


def backproject_kernel(shift_ref, columns_ref, mats_ref, out_ref, tiles_ref):
    p = pl.program_id(0)
    tile_count = out_ref.shape[2] // LANES
    depth_count = out_ref.shape[1]

    @pl.when(p == 0)
    def _():
        out_ref[...] = jnp.zeros_like(out_ref)
        tiles_ref[...] = jnp.zeros_like(tiles_ref)

    for tile in range(tile_count):
        tiles_ref[0, tile + 1] = columns_ref[0, :, tile * LANES:(tile + 1) * LANES].astype(
            jnp.float32
        )

    ends = jnp.concatenate([tiles_ref[0, 1], tiles_ref[0, tile_count]], axis=0).astype(jnp.bfloat16)
    second_half = lax.broadcasted_iota(jnp.int32, (LANES, LANES), 1) >= BLOCK
    empty = jnp.zeros((BLOCK, LANES), jnp.bfloat16)
    for row in range(out_ref.shape[0]):
        shift = shift_ref[p, row]
        start = (shift + 2) // 2
        odd = jnp.full((LANES, LANES), shift - 2 * (start - 1), jnp.int32) == 1
        whole = mats_ref[0, row]
        down = jnp.concatenate([empty, whole[:BLOCK]], axis=0)
        up = jnp.concatenate([whole[BLOCK:], empty], axis=0)
        nothing = jnp.zeros_like(whole)
        first = jnp.where(
            second_half, jnp.where(odd, nothing, down), jnp.where(odd, down, whole)
        )
        second = jnp.where(
            second_half, jnp.where(odd, whole, up), jnp.where(odd, up, nothing)
        )
        low = tiles_ref[0, pl.ds(start, tile_count)].reshape(tile_count * depth_count, LANES)
        high = tiles_ref[0, pl.ds(start + 1, tile_count)].reshape(tile_count * depth_count, LANES)
        taps = jnp.concatenate([low, high], axis=1).astype(jnp.bfloat16)
        result = jnp.dot(
            taps, jnp.concatenate([first, second], axis=0), preferred_element_type=jnp.float32
        )
        edge = jnp.dot(ends, whole, preferred_element_type=jnp.float32)
        shift_vec = jnp.full((depth_count, LANES), shift, jnp.int32)
        for tile in range(tile_count):
            part = result[tile * depth_count:(tile + 1) * depth_count]
            if tile == 0:
                part = jnp.where(shift_vec < 0, edge[:depth_count], part)
            elif tile == tile_count - 2:
                part = jnp.where(shift_vec >= 2, edge[depth_count:], part)
            elif tile == tile_count - 1:
                part = jnp.where(shift_vec >= 0, edge[depth_count:], part)
            lanes = pl.ds(tile * LANES, LANES)
            out_ref[row, :, lanes] = out_ref[row, :, lanes] + part

    @pl.when(p == pl.num_programs(0) - 1)
    def _():
        out_ref[...] = math.pi / P_SIZE * out_ref[...]


def backproject(shifts, columns, mats):
    count, rows = shifts.shape
    depth_count, column_count = columns.shape[1], columns.shape[2]
    tile_count = column_count // LANES
    return pl.pallas_call(
        backproject_kernel,
        out_shape=jax.ShapeDtypeStruct((rows, depth_count, column_count), jnp.float32),
        grid_spec=pltpu.PrefetchScalarGridSpec(
            num_scalar_prefetch=1,
            grid=(count,),
            in_specs=[
                pl.BlockSpec((1,) + columns.shape[1:], lambda p, s: (p, 0, 0)),
                pl.BlockSpec((1,) + mats.shape[1:], lambda p, s: (p, 0, 0, 0)),
            ],
            out_specs=pl.BlockSpec((rows, depth_count, column_count), lambda p, s: (0, 0, 0)),
            scratch_shapes=[pltpu.VMEM((1, tile_count + 3, depth_count, LANES), jnp.float32)],
        ),
        compiler_params=pltpu.CompilerParams(dimension_semantics=("arbitrary",)),
    )(shifts, columns, mats)


def per_device(filtered, angle_index, band_offset, band_length, foot_block):
    depth_count = filtered.shape[1]
    row_count = foot_block.shape[1]
    extended_band = with_halo(filtered, (("gz", 1),), depth_count // 2)
    axial_weights = axial_table(band_offset[:, 0], band_length[:, 0], depth_count)
    summed_rows = jnp.einsum(
        "pzv,pvu->pzu",
        axial_weights,
        extended_band,
        preferred_element_type=jnp.float32,
    )
    columns = gather_columns(summed_rows.astype(jnp.bfloat16))
    column_count = columns.shape[2]
    row_base = lax.axis_index("gy") * row_count
    depth_base = lax.axis_index("gz") * depth_count
    rows_total = lax.axis_size("gy") * row_count
    depth_total = lax.axis_size("gz") * depth_count
    row_global = (row_base + jnp.arange(row_count)).astype(jnp.float32)
    shifts = foot_block[:, :, 2] - 2
    mats = jax.vmap(footprint_mats, in_axes=(0, None, None))(angle_index, row_global, rows_total)
    backprojection = backproject(shifts, columns, mats)
    current = backprojection
    extended = with_wide_halo(backprojection, ITERS)
    fidelity = extended
    current = extended
    for turn_index in range(ITERS):
        reach = ITERS - turn_index
        current = smooth_update(
            current, fidelity, row_base - reach, depth_base - reach, rows_total, depth_total
        )[1:-1, 1:-1]
        fidelity = fidelity[1:-1, 1:-1]
    return current


def solution(mesh):
    return jax.shard_map(
        per_device,
        mesh=mesh,
        in_specs=(P(None, "gz", "gy"), P(), P(None, "gz"), P(None, "gz"), P(None, "gy", None)),
        out_specs=P("gy", "gz", None),
        check_vma=False,
    )
```

```python
import functools
import math

import jax
import jax.numpy as jnp
from jax import lax
from jax.experimental import pallas as pl
from jax.experimental.pallas import tpu as pltpu
from jax.sharding import PartitionSpec as P

X = 4096
P_SIZE = 16
NANG = 3600
BLOCK = 64
LANES = 128
GATHER_CHUNKS = 4
ITERS = 2


step_length = 0.25
smooth_weight = 0.3
gradient_floor = 0.01
shift_reach = 8.0


def with_halo(cells, sides, width):
    for axis, dim in sides:
        count = lax.axis_size(axis)
        ends = count - 1
        head = lax.slice_in_dim(cells, 0, width, axis=dim)
        tail = lax.slice_in_dim(cells, cells.shape[dim] - width, cells.shape[dim], axis=dim)
        cells = jnp.concatenate(
            [
                lax.ppermute(tail, axis, [(i, (i + 1) % count) for i in range(ends)]),
                cells,
                lax.ppermute(head, axis, [((i + 1) % count, i) for i in range(ends)]),
            ],
            axis=dim,
        )
    return cells


def gather_kernel(count, local_ref, out_ref, send_sem, recv_sem, own_sem):
    ring = count // 2
    forward_steps = ring // 2
    backward_steps = ring - 1 - forward_steps
    me = lax.axis_index("gy")
    depth_index = lax.axis_index("gz")
    half = me // ring
    place = me % ring
    width = local_ref.shape[2]
    mesh_kind = pl.DeviceIdType.MESH

    def device(half_of, place_of):
        return half_of * ring + lax.rem(place_of + 2 * ring, ring)

    partner = device(1 - half, place)
    right = device(half, place + 1)
    left = device(half, place - 1)

    chunks = GATHER_CHUNKS
    chunk_rows = local_ref.shape[0] // chunks

    def rows_of(chunk):
        return pl.ds(chunk * chunk_rows, chunk_rows)

    def slot(index, chunk):
        columns = pl.ds(pl.multiple_of(index * width, width), width)
        return out_ref.at[rows_of(chunk), :, columns]

    barrier = pltpu.get_barrier_semaphore()
    for peer in (partner, right, left):
        pl.semaphore_signal(barrier, inc=1, device_id=(depth_index, peer), device_id_type=mesh_kind)
    pl.semaphore_wait(barrier, 3)

    own = pltpu.make_async_copy(local_ref, out_ref.at[:, :, pl.ds(pl.multiple_of(me * width, width), width)], own_sem)
    own.start()
    sends = []

    def send(source, index, chunk, peer):
        copy = pltpu.make_async_remote_copy(
            src_ref=source,
            dst_ref=slot(index, chunk),
            send_sem=send_sem.at[len(sends)],
            recv_sem=recv_sem.at[index, chunk],
            device_id=(depth_index, peer),
            device_id_type=mesh_kind,
        )
        copy.start()
        sends.append(copy)

    def arrived(index, chunk):
        pltpu.make_async_remote_copy(
            src_ref=local_ref.at[rows_of(chunk)],
            dst_ref=slot(index, chunk),
            send_sem=send_sem.at[0],
            recv_sem=recv_sem.at[index, chunk],
            device_id=(depth_index, partner),
            device_id_type=mesh_kind,
        ).wait_recv()

    for chunk in range(chunks):
        send(local_ref.at[rows_of(chunk)], me, chunk, partner)
    for step in range(1, forward_steps + 1):
        for chunk in range(chunks):
            for direction, peer, limit in ((-1, right, forward_steps), (1, left, backward_steps)):
                if step > limit:
                    continue
                if step == 1:
                    send(local_ref.at[rows_of(chunk)], me, chunk, peer)
                    if direction == -1:
                        arrived(partner, chunk)
                    send(slot(partner, chunk), partner, chunk, peer)
                    continue
                for half_of in (0, 1):
                    index = device(half_of, place + direction * (step - 1))
                    arrived(index, chunk)
                    send(slot(index, chunk), index, chunk, peer)
    for direction, steps in ((-1, forward_steps), (1, backward_steps)):
        for half_of in (0, 1):
            for chunk in range(chunks):
                arrived(device(half_of, place + direction * steps), chunk)
    own.wait()
    for copy in sends:
        copy.wait_send()


def gather_columns(local):
    count = lax.axis_size("gy")
    rows, depth, width = local.shape
    return pl.pallas_call(
        functools.partial(gather_kernel, count),
        out_shape=jax.ShapeDtypeStruct((rows, depth, width * count), local.dtype),
        in_specs=[pl.BlockSpec(memory_space=pl.ANY)],
        out_specs=pl.BlockSpec(memory_space=pl.ANY),
        scratch_shapes=[
            pltpu.SemaphoreType.DMA((count * GATHER_CHUNKS,)),
            pltpu.SemaphoreType.DMA((count, GATHER_CHUNKS)),
            pltpu.SemaphoreType.DMA(()),
        ],
        compiler_params=pltpu.CompilerParams(collective_id=0, has_side_effects=True),
    )(local)


STEPS = ((1, 1), (1, 0), (1, -1), (0, 1), (0, -1), (-1, 1), (-1, 0), (-1, -1))


def halo_kernel(count, width, cells_ref, *refs):
    pieces = len(STEPS)
    targets = refs[:pieces]
    send_sem, recv_sem = refs[pieces], refs[pieces + 1]
    row_count, depth_count = count
    rows, depth = cells_ref.shape[0], cells_ref.shape[1]
    row_parts = {1: pl.ds(rows - width, width), 0: pl.ds(0, rows), -1: pl.ds(0, width)}
    depth_parts = {1: pl.ds(depth - width, width), 0: pl.ds(0, depth), -1: pl.ds(0, width)}
    row_me = lax.axis_index("gy")
    depth_me = lax.axis_index("gz")
    peers = [
        (lax.rem(depth_me + depth_step + depth_count, depth_count),
         lax.rem(row_me + row_step + row_count, row_count))
        for row_step, depth_step in STEPS
    ]
    barrier = pltpu.get_barrier_semaphore()
    for peer in peers:
        pl.semaphore_signal(barrier, inc=1, device_id=peer, device_id_type=pl.DeviceIdType.MESH)
    pl.semaphore_wait(barrier, pieces)
    copies = []
    for k, peer in enumerate(peers):
        row_step, depth_step = STEPS[k]
        copy = pltpu.make_async_remote_copy(
            src_ref=cells_ref.at[row_parts[row_step], depth_parts[depth_step]],
            dst_ref=targets[k],
            send_sem=send_sem.at[k],
            recv_sem=recv_sem.at[k],
            device_id=peer,
            device_id_type=pl.DeviceIdType.MESH,
        )
        copy.start()
        copies.append(copy)
    for copy in copies:
        copy.wait()


def with_wide_halo(cells, width):
    rows, depth = cells.shape[0], cells.shape[1]
    count = (lax.axis_size("gy"), lax.axis_size("gz"))
    row_parts = {1: slice(rows - width, rows), 0: slice(None), -1: slice(0, width)}
    depth_parts = {1: slice(depth - width, depth), 0: slice(None), -1: slice(0, width)}
    sent = [cells[row_parts[r], depth_parts[d]] for r, d in STEPS]
    received = pl.pallas_call(
        functools.partial(halo_kernel, count, width),
        out_shape=[jax.ShapeDtypeStruct(piece.shape, piece.dtype) for piece in sent],
        in_specs=[pl.BlockSpec(memory_space=pl.ANY)],
        out_specs=[pl.BlockSpec(memory_space=pl.ANY)] * len(STEPS),
        scratch_shapes=[
            pltpu.SemaphoreType.DMA((len(STEPS),)),
            pltpu.SemaphoreType.DMA((len(STEPS),)),
        ],
        compiler_params=pltpu.CompilerParams(collective_id=1, has_side_effects=True),
    )(cells)
    parts = dict(zip(STEPS, received))
    parts[(0, 0)] = cells
    bands = [
        jnp.concatenate([parts[(r, 1)], parts[(r, 0)], parts[(r, -1)]], axis=1) for r in (1, 0, -1)
    ]
    return jnp.concatenate(bands, axis=0)


def geometry(angle_value):
    radians = 2.0 * math.pi * angle_value.astype(jnp.float32) / NANG
    stretch = 0.5 + 0.5 * jnp.abs(jnp.cos(radians))
    spread = 1.0 + jnp.abs(jnp.sin(radians))
    return (radians, stretch, spread)


def footprint(radians, stretch, spread, row_global, rows_total, block_size):
    shifted = shift_reach * jnp.sin(radians + 2.0 * math.pi * row_global / rows_total)
    inside = jnp.arange(block_size).astype(jnp.float32) - 0.5 * (block_size - 1)
    centre = block_size + inside[None, :] * stretch + shifted[:, None]
    places = jnp.arange(2 * block_size).astype(jnp.float32) + 0.5
    weights = (
        jnp.maximum(0.0, 1.0 - jnp.abs(places[None, None, :] - centre[:, :, None]) / spread)
        / spread
    )
    return weights.astype(jnp.bfloat16)


def axial_table(offsets, lengths, depth_count):
    offset_real = offsets.astype(jnp.float32)[..., None]
    length_real = lengths.astype(jnp.float32)[..., None]
    depth_place = jnp.arange(depth_count).astype(jnp.float32) + 0.5
    centre = offset_real + depth_place * length_real / depth_count
    row_number = jnp.arange(2 * depth_count)
    row_place = row_number.astype(jnp.float32) + 0.5
    triangle = jnp.maximum(0.0, 1.0 - jnp.abs(row_place - centre[..., None]))
    inside = (row_number >= offsets[..., None, None]) & (
        row_number < (offsets + lengths)[..., None, None]
    )
    return jnp.where(inside, triangle, 0.0).astype(jnp.bfloat16)


def smooth_update(current, fidelity, row_first, depth_first, rows_total, depth_total):
    row_index = row_first + jnp.arange(current.shape[0])
    depth_index = depth_first + jnp.arange(current.shape[1])
    keep_rows = ((row_index >= 0) & (row_index < rows_total - 1)).astype(jnp.float32)[:, None, None]
    keep_depth = ((depth_index >= 0) & (depth_index < depth_total - 1)).astype(jnp.float32)[
        None, :, None
    ]
    forward_rows = (
        jnp.concatenate([current[1:] - current[:-1], jnp.zeros_like(current[:1])], 0) * keep_rows
    )
    forward_depth = (
        jnp.concatenate([current[:, 1:] - current[:, :-1], jnp.zeros_like(current[:, :1])], 1)
        * keep_depth
    )
    forward_width = jnp.concatenate(
        [current[:, :, 1:] - current[:, :, :-1], jnp.zeros_like(current[:, :, :1])], 2
    )
    inverse = lax.rsqrt(
        forward_rows * forward_rows
        + forward_depth * forward_depth
        + forward_width * forward_width
        + gradient_floor
    )
    normal_rows = forward_rows * inverse
    normal_depth = forward_depth * inverse
    normal_width = forward_width * inverse
    divergence = normal_rows - jnp.concatenate(
        [jnp.zeros_like(normal_rows[:1]), normal_rows[:-1]], 0
    )
    divergence = (
        divergence
        + normal_depth
        - jnp.concatenate([jnp.zeros_like(normal_depth[:, :1]), normal_depth[:, :-1]], 1)
    )
    divergence = (
        divergence
        + normal_width
        - jnp.concatenate([jnp.zeros_like(normal_width[:, :, :1]), normal_width[:, :, :-1]], 2)
    )
    return current + step_length * (smooth_weight * divergence - (current - fidelity))


def footprint_mats(angle_value, row_global, rows_total):
    radians, stretch, spread = geometry(angle_value)
    shifted = shift_reach * jnp.sin(radians + 2.0 * math.pi * row_global / rows_total)
    inside = jnp.arange(BLOCK).astype(jnp.float32) - 0.5 * (BLOCK - 1)
    centre = BLOCK + inside[None, :] * stretch + shifted[:, None]
    centre = jnp.concatenate([centre, centre], axis=1)
    places = jnp.arange(LANES).astype(jnp.float32)[:, None] + 0.5
    weights = (
        jnp.maximum(0.0, 1.0 - jnp.abs(places[None] - centre[:, None, :]) / spread) / spread
    )
    return weights.astype(jnp.bfloat16)


def backproject_kernel(shift_ref, columns_ref, mats_ref, out_ref, tiles_ref):
    p = pl.program_id(0)
    tile_count = out_ref.shape[2] // LANES
    depth_count = out_ref.shape[1]

    @pl.when(p == 0)
    def _():
        out_ref[...] = jnp.zeros_like(out_ref)
        tiles_ref[...] = jnp.zeros_like(tiles_ref)

    for tile in range(tile_count):
        tiles_ref[0, tile + 1] = columns_ref[0, :, tile * LANES:(tile + 1) * LANES].astype(
            jnp.float32
        )

    ends = jnp.concatenate([tiles_ref[0, 1], tiles_ref[0, tile_count]], axis=0).astype(jnp.bfloat16)
    second_half = lax.broadcasted_iota(jnp.int32, (LANES, LANES), 1) >= BLOCK
    empty = jnp.zeros((BLOCK, LANES), jnp.bfloat16)
    for row in range(out_ref.shape[0]):
        shift = shift_ref[p, row]
        start = (shift + 2) // 2
        odd = jnp.full((LANES, LANES), shift - 2 * (start - 1), jnp.int32) == 1
        whole = mats_ref[0, row]
        down = jnp.concatenate([empty, whole[:BLOCK]], axis=0)
        up = jnp.concatenate([whole[BLOCK:], empty], axis=0)
        nothing = jnp.zeros_like(whole)
        first = jnp.where(
            second_half, jnp.where(odd, nothing, down), jnp.where(odd, down, whole)
        )
        second = jnp.where(
            second_half, jnp.where(odd, whole, up), jnp.where(odd, up, nothing)
        )
        low = tiles_ref[0, pl.ds(start, tile_count)].reshape(tile_count * depth_count, LANES)
        high = tiles_ref[0, pl.ds(start + 1, tile_count)].reshape(tile_count * depth_count, LANES)
        taps = jnp.concatenate([low, high], axis=1).astype(jnp.bfloat16)
        result = jnp.dot(
            taps, jnp.concatenate([first, second], axis=0), preferred_element_type=jnp.float32
        )
        edge = jnp.dot(ends, whole, preferred_element_type=jnp.float32)
        shift_vec = jnp.full((depth_count, LANES), shift, jnp.int32)
        for tile in range(tile_count):
            part = result[tile * depth_count:(tile + 1) * depth_count]
            if tile == 0:
                part = jnp.where(shift_vec < 0, edge[:depth_count], part)
            elif tile == tile_count - 2:
                part = jnp.where(shift_vec >= 2, edge[depth_count:], part)
            elif tile == tile_count - 1:
                part = jnp.where(shift_vec >= 0, edge[depth_count:], part)
            lanes = pl.ds(tile * LANES, LANES)
            out_ref[row, :, lanes] = out_ref[row, :, lanes] + part

    @pl.when(p == pl.num_programs(0) - 1)
    def _():
        out_ref[...] = math.pi / P_SIZE * out_ref[...]


def backproject(shifts, columns, mats):
    count, rows = shifts.shape
    depth_count, column_count = columns.shape[1], columns.shape[2]
    tile_count = column_count // LANES
    return pl.pallas_call(
        backproject_kernel,
        out_shape=jax.ShapeDtypeStruct((rows, depth_count, column_count), jnp.float32),
        grid_spec=pltpu.PrefetchScalarGridSpec(
            num_scalar_prefetch=1,
            grid=(count,),
            in_specs=[
                pl.BlockSpec((1,) + columns.shape[1:], lambda p, s: (p, 0, 0)),
                pl.BlockSpec((1,) + mats.shape[1:], lambda p, s: (p, 0, 0, 0)),
            ],
            out_specs=pl.BlockSpec((rows, depth_count, column_count), lambda p, s: (0, 0, 0)),
            scratch_shapes=[pltpu.VMEM((1, tile_count + 3, depth_count, LANES), jnp.float32)],
        ),
        compiler_params=pltpu.CompilerParams(dimension_semantics=("arbitrary",)),
    )(shifts, columns, mats)


def per_device(filtered, angle_index, band_offset, band_length, foot_block):
    depth_count = filtered.shape[1]
    row_count = foot_block.shape[1]
    extended_band = with_halo(filtered, (("gz", 1),), depth_count // 2)
    axial_weights = axial_table(band_offset[:, 0], band_length[:, 0], depth_count)
    summed_rows = jnp.einsum(
        "pzv,pvu->pzu",
        axial_weights,
        extended_band,
        preferred_element_type=jnp.float32,
    )
    columns = gather_columns(summed_rows.astype(jnp.bfloat16))
    column_count = columns.shape[2]
    row_base = lax.axis_index("gy") * row_count
    depth_base = lax.axis_index("gz") * depth_count
    rows_total = lax.axis_size("gy") * row_count
    depth_total = lax.axis_size("gz") * depth_count
    row_global = (row_base + jnp.arange(row_count)).astype(jnp.float32)
    shifts = foot_block[:, :, 2] - 2
    mats = jax.vmap(footprint_mats, in_axes=(0, None, None))(angle_index, row_global, rows_total)
    backprojection = backproject(shifts, columns, mats)
    current = backprojection
    extended = with_wide_halo(backprojection, ITERS)
    fidelity = extended
    current = extended
    for turn_index in range(ITERS):
        reach = ITERS - turn_index
        current = smooth_update(
            current, fidelity, row_base - reach, depth_base - reach, rows_total, depth_total
        )[1:-1, 1:-1]
        fidelity = fidelity[1:-1, 1:-1]
    return current


def solution(mesh):
    return jax.shard_map(
        per_device,
        mesh=mesh,
        in_specs=(P(None, "gz", "gy"), P(), P(None, "gz"), P(None, "gz"), P(None, "gy", None)),
        out_specs=P("gy", "gz", None),
        check_vma=False,
    )
```

```python
import functools
import math

import jax
import jax.numpy as jnp
from jax import lax
from jax.experimental import pallas as pl
from jax.experimental.pallas import tpu as pltpu
from jax.sharding import PartitionSpec as P

X = 4096
P_SIZE = 16
NANG = 3600
BLOCK = 64
LANES = 128
GATHER_CHUNKS = 2
ITERS = 2


step_length = 0.25
smooth_weight = 0.3
gradient_floor = 0.01
shift_reach = 8.0


def with_halo(cells, sides, width):
    for axis, dim in sides:
        count = lax.axis_size(axis)
        ends = count - 1
        head = lax.slice_in_dim(cells, 0, width, axis=dim)
        tail = lax.slice_in_dim(cells, cells.shape[dim] - width, cells.shape[dim], axis=dim)
        cells = jnp.concatenate(
            [
                lax.ppermute(tail, axis, [(i, (i + 1) % count) for i in range(ends)]),
                cells,
                lax.ppermute(head, axis, [((i + 1) % count, i) for i in range(ends)]),
            ],
            axis=dim,
        )
    return cells


def gather_kernel(count, local_ref, out_ref, send_sem, recv_sem, own_sem):
    ring = count // 2
    forward_steps = ring // 2
    backward_steps = (ring - 1) // 2
    me = lax.axis_index("gy")
    depth_index = lax.axis_index("gz")
    half = me // ring
    place = me % ring
    width = local_ref.shape[2]
    mesh_kind = pl.DeviceIdType.MESH

    def device(half_of, place_of):
        return half_of * ring + lax.rem(place_of + 2 * ring, ring)

    partner = device(1 - half, place)
    right = device(half, place + 1)
    left = device(half, place - 1)

    chunks = GATHER_CHUNKS
    chunk_rows = local_ref.shape[0] // chunks

    def rows_of(chunk):
        return pl.ds(chunk * chunk_rows, chunk_rows)

    def slot(index, chunk):
        columns = pl.ds(pl.multiple_of(index * width, width), width)
        return out_ref.at[rows_of(chunk), :, columns]

    barrier = pltpu.get_barrier_semaphore()
    for peer in (partner, right, left):
        pl.semaphore_signal(barrier, inc=1, device_id=(depth_index, peer), device_id_type=mesh_kind)
    pl.semaphore_wait(barrier, 3)

    own = pltpu.make_async_copy(local_ref, out_ref.at[:, :, pl.ds(pl.multiple_of(me * width, width), width)], own_sem)
    own.start()
    sends = []

    def send(source, index, chunk, peer):
        copy = pltpu.make_async_remote_copy(
            src_ref=source,
            dst_ref=slot(index, chunk),
            send_sem=send_sem.at[len(sends)],
            recv_sem=recv_sem.at[index, chunk],
            device_id=(depth_index, peer),
            device_id_type=mesh_kind,
        )
        copy.start()
        sends.append(copy)

    def arrived(index, chunk):
        pltpu.make_async_remote_copy(
            src_ref=local_ref.at[rows_of(chunk)],
            dst_ref=slot(index, chunk),
            send_sem=send_sem.at[0],
            recv_sem=recv_sem.at[index, chunk],
            device_id=(depth_index, partner),
            device_id_type=mesh_kind,
        ).wait_recv()

    for chunk in range(chunks):
        send(local_ref.at[rows_of(chunk)], me, chunk, partner)
    shared = ring - 1 - 2 * backward_steps

    def carried(direction, step, chunk):
        if step <= backward_steps:
            return True
        if shared and step == backward_steps + 1:
            return chunk == (0 if direction == -1 else chunks - 1)
        return False

    for step in range(1, forward_steps + 1):
        for chunk in range(chunks):
            for direction, peer in ((-1, right), (1, left)):
                if not carried(direction, step, chunk):
                    continue
                if step == 1:
                    send(local_ref.at[rows_of(chunk)], me, chunk, peer)
                    if direction == -1:
                        arrived(partner, chunk)
                    send(slot(partner, chunk), partner, chunk, peer)
                    continue
                for half_of in (0, 1):
                    index = device(half_of, place + direction * (step - 1))
                    arrived(index, chunk)
                    send(slot(index, chunk), index, chunk, peer)
    for direction in (-1, 1):
        for step in range(1, forward_steps + 1):
            for chunk in range(chunks):
                if not carried(direction, step, chunk):
                    continue
                if step < forward_steps and carried(direction, step + 1, chunk):
                    continue
                for half_of in (0, 1):
                    arrived(device(half_of, place + direction * step), chunk)
    own.wait()
    for copy in sends:
        copy.wait_send()


def gather_columns(local):
    count = lax.axis_size("gy")
    rows, depth, width = local.shape
    return pl.pallas_call(
        functools.partial(gather_kernel, count),
        out_shape=jax.ShapeDtypeStruct((rows, depth, width * count), local.dtype),
        in_specs=[pl.BlockSpec(memory_space=pl.ANY)],
        out_specs=pl.BlockSpec(memory_space=pl.ANY),
        scratch_shapes=[
            pltpu.SemaphoreType.DMA((count * GATHER_CHUNKS,)),
            pltpu.SemaphoreType.DMA((count, GATHER_CHUNKS)),
            pltpu.SemaphoreType.DMA(()),
        ],
        compiler_params=pltpu.CompilerParams(collective_id=0, has_side_effects=True),
    )(local)


STEPS = ((1, 1), (1, 0), (1, -1), (0, 1), (0, -1), (-1, 1), (-1, 0), (-1, -1))


def halo_kernel(count, width, cells_ref, *refs):
    pieces = len(STEPS)
    targets = refs[:pieces]
    send_sem, recv_sem = refs[pieces], refs[pieces + 1]
    row_count, depth_count = count
    rows, depth = cells_ref.shape[0], cells_ref.shape[1]
    row_parts = {1: pl.ds(rows - width, width), 0: pl.ds(0, rows), -1: pl.ds(0, width)}
    depth_parts = {1: pl.ds(depth - width, width), 0: pl.ds(0, depth), -1: pl.ds(0, width)}
    row_me = lax.axis_index("gy")
    depth_me = lax.axis_index("gz")
    peers = [
        (lax.rem(depth_me + depth_step + depth_count, depth_count),
         lax.rem(row_me + row_step + row_count, row_count))
        for row_step, depth_step in STEPS
    ]
    barrier = pltpu.get_barrier_semaphore()
    for peer in peers:
        pl.semaphore_signal(barrier, inc=1, device_id=peer, device_id_type=pl.DeviceIdType.MESH)
    pl.semaphore_wait(barrier, pieces)
    copies = []
    for k, peer in enumerate(peers):
        row_step, depth_step = STEPS[k]
        copy = pltpu.make_async_remote_copy(
            src_ref=cells_ref.at[row_parts[row_step], depth_parts[depth_step]],
            dst_ref=targets[k],
            send_sem=send_sem.at[k],
            recv_sem=recv_sem.at[k],
            device_id=peer,
            device_id_type=pl.DeviceIdType.MESH,
        )
        copy.start()
        copies.append(copy)
    for copy in copies:
        copy.wait()


def with_wide_halo(cells, width):
    rows, depth = cells.shape[0], cells.shape[1]
    count = (lax.axis_size("gy"), lax.axis_size("gz"))
    row_parts = {1: slice(rows - width, rows), 0: slice(None), -1: slice(0, width)}
    depth_parts = {1: slice(depth - width, depth), 0: slice(None), -1: slice(0, width)}
    sent = [cells[row_parts[r], depth_parts[d]] for r, d in STEPS]
    received = pl.pallas_call(
        functools.partial(halo_kernel, count, width),
        out_shape=[jax.ShapeDtypeStruct(piece.shape, piece.dtype) for piece in sent],
        in_specs=[pl.BlockSpec(memory_space=pl.ANY)],
        out_specs=[pl.BlockSpec(memory_space=pl.ANY)] * len(STEPS),
        scratch_shapes=[
            pltpu.SemaphoreType.DMA((len(STEPS),)),
            pltpu.SemaphoreType.DMA((len(STEPS),)),
        ],
        compiler_params=pltpu.CompilerParams(collective_id=1, has_side_effects=True),
    )(cells)
    parts = dict(zip(STEPS, received))
    parts[(0, 0)] = cells
    bands = [
        jnp.concatenate([parts[(r, 1)], parts[(r, 0)], parts[(r, -1)]], axis=1) for r in (1, 0, -1)
    ]
    return jnp.concatenate(bands, axis=0)


def geometry(angle_value):
    radians = 2.0 * math.pi * angle_value.astype(jnp.float32) / NANG
    stretch = 0.5 + 0.5 * jnp.abs(jnp.cos(radians))
    spread = 1.0 + jnp.abs(jnp.sin(radians))
    return (radians, stretch, spread)


def footprint(radians, stretch, spread, row_global, rows_total, block_size):
    shifted = shift_reach * jnp.sin(radians + 2.0 * math.pi * row_global / rows_total)
    inside = jnp.arange(block_size).astype(jnp.float32) - 0.5 * (block_size - 1)
    centre = block_size + inside[None, :] * stretch + shifted[:, None]
    places = jnp.arange(2 * block_size).astype(jnp.float32) + 0.5
    weights = (
        jnp.maximum(0.0, 1.0 - jnp.abs(places[None, None, :] - centre[:, :, None]) / spread)
        / spread
    )
    return weights.astype(jnp.bfloat16)


def axial_table(offsets, lengths, depth_count):
    offset_real = offsets.astype(jnp.float32)[..., None]
    length_real = lengths.astype(jnp.float32)[..., None]
    depth_place = jnp.arange(depth_count).astype(jnp.float32) + 0.5
    centre = offset_real + depth_place * length_real / depth_count
    row_number = jnp.arange(2 * depth_count)
    row_place = row_number.astype(jnp.float32) + 0.5
    triangle = jnp.maximum(0.0, 1.0 - jnp.abs(row_place - centre[..., None]))
    inside = (row_number >= offsets[..., None, None]) & (
        row_number < (offsets + lengths)[..., None, None]
    )
    return jnp.where(inside, triangle, 0.0).astype(jnp.bfloat16)


def smooth_update(current, fidelity, row_first, depth_first, rows_total, depth_total):
    row_index = row_first + jnp.arange(current.shape[0])
    depth_index = depth_first + jnp.arange(current.shape[1])
    keep_rows = ((row_index >= 0) & (row_index < rows_total - 1)).astype(jnp.float32)[:, None, None]
    keep_depth = ((depth_index >= 0) & (depth_index < depth_total - 1)).astype(jnp.float32)[
        None, :, None
    ]
    forward_rows = (
        jnp.concatenate([current[1:] - current[:-1], jnp.zeros_like(current[:1])], 0) * keep_rows
    )
    forward_depth = (
        jnp.concatenate([current[:, 1:] - current[:, :-1], jnp.zeros_like(current[:, :1])], 1)
        * keep_depth
    )
    forward_width = jnp.concatenate(
        [current[:, :, 1:] - current[:, :, :-1], jnp.zeros_like(current[:, :, :1])], 2
    )
    inverse = lax.rsqrt(
        forward_rows * forward_rows
        + forward_depth * forward_depth
        + forward_width * forward_width
        + gradient_floor
    )
    normal_rows = forward_rows * inverse
    normal_depth = forward_depth * inverse
    normal_width = forward_width * inverse
    divergence = normal_rows - jnp.concatenate(
        [jnp.zeros_like(normal_rows[:1]), normal_rows[:-1]], 0
    )
    divergence = (
        divergence
        + normal_depth
        - jnp.concatenate([jnp.zeros_like(normal_depth[:, :1]), normal_depth[:, :-1]], 1)
    )
    divergence = (
        divergence
        + normal_width
        - jnp.concatenate([jnp.zeros_like(normal_width[:, :, :1]), normal_width[:, :, :-1]], 2)
    )
    return current + step_length * (smooth_weight * divergence - (current - fidelity))


def footprint_mats(angle_value, row_global, rows_total):
    radians, stretch, spread = geometry(angle_value)
    shifted = shift_reach * jnp.sin(radians + 2.0 * math.pi * row_global / rows_total)
    inside = jnp.arange(BLOCK).astype(jnp.float32) - 0.5 * (BLOCK - 1)
    centre = BLOCK + inside[None, :] * stretch + shifted[:, None]
    centre = jnp.concatenate([centre, centre], axis=1)
    places = jnp.arange(LANES).astype(jnp.float32)[:, None] + 0.5
    weights = (
        jnp.maximum(0.0, 1.0 - jnp.abs(places[None] - centre[:, None, :]) / spread) / spread
    )
    return weights.astype(jnp.bfloat16)


def backproject_kernel(shift_ref, columns_ref, mats_ref, out_ref, tiles_ref):
    p = pl.program_id(0)
    tile_count = out_ref.shape[2] // LANES
    depth_count = out_ref.shape[1]

    @pl.when(p == 0)
    def _():
        out_ref[...] = jnp.zeros_like(out_ref)
        tiles_ref[...] = jnp.zeros_like(tiles_ref)

    for tile in range(tile_count):
        tiles_ref[0, tile + 1] = columns_ref[0, :, tile * LANES:(tile + 1) * LANES].astype(
            jnp.float32
        )

    ends = jnp.concatenate([tiles_ref[0, 1], tiles_ref[0, tile_count]], axis=0).astype(jnp.bfloat16)
    second_half = lax.broadcasted_iota(jnp.int32, (LANES, LANES), 1) >= BLOCK
    empty = jnp.zeros((BLOCK, LANES), jnp.bfloat16)
    for row in range(out_ref.shape[0]):
        shift = shift_ref[p, row]
        start = (shift + 2) // 2
        odd = jnp.full((LANES, LANES), shift - 2 * (start - 1), jnp.int32) == 1
        whole = mats_ref[0, row]
        down = jnp.concatenate([empty, whole[:BLOCK]], axis=0)
        up = jnp.concatenate([whole[BLOCK:], empty], axis=0)
        nothing = jnp.zeros_like(whole)
        first = jnp.where(
            second_half, jnp.where(odd, nothing, down), jnp.where(odd, down, whole)
        )
        second = jnp.where(
            second_half, jnp.where(odd, whole, up), jnp.where(odd, up, nothing)
        )
        low = tiles_ref[0, pl.ds(start, tile_count)].reshape(tile_count * depth_count, LANES)
        high = tiles_ref[0, pl.ds(start + 1, tile_count)].reshape(tile_count * depth_count, LANES)
        taps = jnp.concatenate([low, high], axis=1).astype(jnp.bfloat16)
        result = jnp.dot(
            taps, jnp.concatenate([first, second], axis=0), preferred_element_type=jnp.float32
        )
        edge = jnp.dot(ends, whole, preferred_element_type=jnp.float32)
        shift_vec = jnp.full((depth_count, LANES), shift, jnp.int32)
        for tile in range(tile_count):
            part = result[tile * depth_count:(tile + 1) * depth_count]
            if tile == 0:
                part = jnp.where(shift_vec < 0, edge[:depth_count], part)
            elif tile == tile_count - 2:
                part = jnp.where(shift_vec >= 2, edge[depth_count:], part)
            elif tile == tile_count - 1:
                part = jnp.where(shift_vec >= 0, edge[depth_count:], part)
            lanes = pl.ds(tile * LANES, LANES)
            out_ref[row, :, lanes] = out_ref[row, :, lanes] + part

    @pl.when(p == pl.num_programs(0) - 1)
    def _():
        out_ref[...] = math.pi / P_SIZE * out_ref[...]


def backproject(shifts, columns, mats):
    count, rows = shifts.shape
    depth_count, column_count = columns.shape[1], columns.shape[2]
    tile_count = column_count // LANES
    return pl.pallas_call(
        backproject_kernel,
        out_shape=jax.ShapeDtypeStruct((rows, depth_count, column_count), jnp.float32),
        grid_spec=pltpu.PrefetchScalarGridSpec(
            num_scalar_prefetch=1,
            grid=(count,),
            in_specs=[
                pl.BlockSpec((1,) + columns.shape[1:], lambda p, s: (p, 0, 0)),
                pl.BlockSpec((1,) + mats.shape[1:], lambda p, s: (p, 0, 0, 0)),
            ],
            out_specs=pl.BlockSpec((rows, depth_count, column_count), lambda p, s: (0, 0, 0)),
            scratch_shapes=[pltpu.VMEM((1, tile_count + 3, depth_count, LANES), jnp.float32)],
        ),
        compiler_params=pltpu.CompilerParams(dimension_semantics=("arbitrary",)),
    )(shifts, columns, mats)


def per_device(filtered, angle_index, band_offset, band_length, foot_block):
    depth_count = filtered.shape[1]
    row_count = foot_block.shape[1]
    extended_band = with_halo(filtered, (("gz", 1),), depth_count // 2)
    axial_weights = axial_table(band_offset[:, 0], band_length[:, 0], depth_count)
    summed_rows = jnp.einsum(
        "pzv,pvu->pzu",
        axial_weights,
        extended_band,
        preferred_element_type=jnp.float32,
    )
    columns = gather_columns(summed_rows.astype(jnp.bfloat16))
    column_count = columns.shape[2]
    row_base = lax.axis_index("gy") * row_count
    depth_base = lax.axis_index("gz") * depth_count
    rows_total = lax.axis_size("gy") * row_count
    depth_total = lax.axis_size("gz") * depth_count
    row_global = (row_base + jnp.arange(row_count)).astype(jnp.float32)
    shifts = foot_block[:, :, 2] - 2
    mats = jax.vmap(footprint_mats, in_axes=(0, None, None))(angle_index, row_global, rows_total)
    backprojection = backproject(shifts, columns, mats)
    current = backprojection
    extended = with_wide_halo(backprojection, ITERS)
    fidelity = extended
    current = extended
    for turn_index in range(ITERS):
        reach = ITERS - turn_index
        current = smooth_update(
            current, fidelity, row_base - reach, depth_base - reach, rows_total, depth_total
        )[1:-1, 1:-1]
        fidelity = fidelity[1:-1, 1:-1]
    return current


def solution(mesh):
    return jax.shard_map(
        per_device,
        mesh=mesh,
        in_specs=(P(None, "gz", "gy"), P(), P(None, "gz"), P(None, "gz"), P(None, "gy", None)),
        out_specs=P("gy", "gz", None),
        check_vma=False,
    )
```

```python
import functools
import math

import jax
import jax.numpy as jnp
from jax import lax
from jax.experimental import pallas as pl
from jax.experimental.pallas import tpu as pltpu
from jax.sharding import PartitionSpec as P

X = 4096
P_SIZE = 16
NANG = 3600
BLOCK = 64
LANES = 128
GATHER_CHUNKS = 2
ITERS = 2


step_length = 0.25
smooth_weight = 0.3
gradient_floor = 0.01
shift_reach = 8.0


def with_halo(cells, sides, width):
    for axis, dim in sides:
        count = lax.axis_size(axis)
        ends = count - 1
        head = lax.slice_in_dim(cells, 0, width, axis=dim)
        tail = lax.slice_in_dim(cells, cells.shape[dim] - width, cells.shape[dim], axis=dim)
        cells = jnp.concatenate(
            [
                lax.ppermute(tail, axis, [(i, (i + 1) % count) for i in range(ends)]),
                cells,
                lax.ppermute(head, axis, [((i + 1) % count, i) for i in range(ends)]),
            ],
            axis=dim,
        )
    return cells


def gather_kernel(count, local_ref, out_ref, send_sem, recv_sem, own_sem):
    ring = count // 2
    forward_steps = ring // 2
    backward_steps = ring - 1 - forward_steps
    me = lax.axis_index("gy")
    depth_index = lax.axis_index("gz")
    half = me // ring
    place = me % ring
    width = local_ref.shape[2]
    mesh_kind = pl.DeviceIdType.MESH

    def device(half_of, place_of):
        return half_of * ring + lax.rem(place_of + 2 * ring, ring)

    partner = device(1 - half, place)
    right = device(half, place + 1)
    left = device(half, place - 1)

    chunks = GATHER_CHUNKS
    chunk_rows = local_ref.shape[0] // chunks

    def rows_of(chunk):
        return pl.ds(chunk * chunk_rows, chunk_rows)

    def slot(index, chunk):
        columns = pl.ds(pl.multiple_of(index * width, width), width)
        return out_ref.at[rows_of(chunk), :, columns]

    barrier = pltpu.get_barrier_semaphore()
    for peer in (partner, right, left):
        pl.semaphore_signal(barrier, inc=1, device_id=(depth_index, peer), device_id_type=mesh_kind)
    pl.semaphore_wait(barrier, 3)

    own = pltpu.make_async_copy(local_ref, out_ref.at[:, :, pl.ds(pl.multiple_of(me * width, width), width)], own_sem)
    own.start()
    sends = []

    def send(source, index, chunk, peer):
        copy = pltpu.make_async_remote_copy(
            src_ref=source,
            dst_ref=slot(index, chunk),
            send_sem=send_sem.at[len(sends)],
            recv_sem=recv_sem.at[index, chunk],
            device_id=(depth_index, peer),
            device_id_type=mesh_kind,
        )
        copy.start()
        sends.append(copy)

    def arrived(index, chunk):
        pltpu.make_async_remote_copy(
            src_ref=local_ref.at[rows_of(chunk)],
            dst_ref=slot(index, chunk),
            send_sem=send_sem.at[0],
            recv_sem=recv_sem.at[index, chunk],
            device_id=(depth_index, partner),
            device_id_type=mesh_kind,
        ).wait_recv()

    for chunk in range(chunks):
        send(local_ref.at[rows_of(chunk)], me, chunk, partner)
    for step in range(1, forward_steps + 1):
        for chunk in range(chunks):
            for direction, peer, limit in ((-1, right, forward_steps), (1, left, backward_steps)):
                if step > limit:
                    continue
                if step == 1:
                    send(local_ref.at[rows_of(chunk)], me, chunk, peer)
                    if direction == -1:
                        arrived(partner, chunk)
                    send(slot(partner, chunk), partner, chunk, peer)
                    continue
                for half_of in (0, 1):
                    index = device(half_of, place + direction * (step - 1))
                    arrived(index, chunk)
                    send(slot(index, chunk), index, chunk, peer)
    for direction, steps in ((-1, forward_steps), (1, backward_steps)):
        for half_of in (0, 1):
            for chunk in range(chunks):
                arrived(device(half_of, place + direction * steps), chunk)
    own.wait()
    for copy in sends:
        copy.wait_send()


def gather_columns(local):
    count = lax.axis_size("gy")
    rows, depth, width = local.shape
    return pl.pallas_call(
        functools.partial(gather_kernel, count),
        out_shape=jax.ShapeDtypeStruct((rows, depth, width * count), local.dtype),
        in_specs=[pl.BlockSpec(memory_space=pl.ANY)],
        out_specs=pl.BlockSpec(memory_space=pl.ANY),
        scratch_shapes=[
            pltpu.SemaphoreType.DMA((count * GATHER_CHUNKS,)),
            pltpu.SemaphoreType.DMA((count, GATHER_CHUNKS)),
            pltpu.SemaphoreType.DMA(()),
        ],
        compiler_params=pltpu.CompilerParams(collective_id=0, has_side_effects=True),
    )(local)


STEPS = ((1, 1), (1, 0), (1, -1), (0, 1), (0, -1), (-1, 1), (-1, 0), (-1, -1))


def halo_kernel(count, width, cells_ref, *refs):
    pieces = len(STEPS)
    targets = refs[:pieces]
    send_sem, recv_sem = refs[pieces], refs[pieces + 1]
    row_count, depth_count = count
    rows, depth = cells_ref.shape[0], cells_ref.shape[1]
    row_parts = {1: pl.ds(rows - width, width), 0: pl.ds(0, rows), -1: pl.ds(0, width)}
    depth_parts = {1: pl.ds(depth - width, width), 0: pl.ds(0, depth), -1: pl.ds(0, width)}
    row_me = lax.axis_index("gy")
    depth_me = lax.axis_index("gz")
    peers = [
        (lax.rem(depth_me + depth_step + depth_count, depth_count),
         lax.rem(row_me + row_step + row_count, row_count))
        for row_step, depth_step in STEPS
    ]
    barrier = pltpu.get_barrier_semaphore()
    for peer in peers:
        pl.semaphore_signal(barrier, inc=1, device_id=peer, device_id_type=pl.DeviceIdType.MESH)
    pl.semaphore_wait(barrier, pieces)
    copies = []
    for k, peer in enumerate(peers):
        row_step, depth_step = STEPS[k]
        copy = pltpu.make_async_remote_copy(
            src_ref=cells_ref.at[row_parts[row_step], depth_parts[depth_step]],
            dst_ref=targets[k],
            send_sem=send_sem.at[k],
            recv_sem=recv_sem.at[k],
            device_id=peer,
            device_id_type=pl.DeviceIdType.MESH,
        )
        copy.start()
        copies.append(copy)
    for copy in copies:
        copy.wait()


def with_wide_halo(cells, width):
    rows, depth = cells.shape[0], cells.shape[1]
    count = (lax.axis_size("gy"), lax.axis_size("gz"))
    row_parts = {1: slice(rows - width, rows), 0: slice(None), -1: slice(0, width)}
    depth_parts = {1: slice(depth - width, depth), 0: slice(None), -1: slice(0, width)}
    sent = [cells[row_parts[r], depth_parts[d]] for r, d in STEPS]
    received = pl.pallas_call(
        functools.partial(halo_kernel, count, width),
        out_shape=[jax.ShapeDtypeStruct(piece.shape, piece.dtype) for piece in sent],
        in_specs=[pl.BlockSpec(memory_space=pl.ANY)],
        out_specs=[pl.BlockSpec(memory_space=pl.ANY)] * len(STEPS),
        scratch_shapes=[
            pltpu.SemaphoreType.DMA((len(STEPS),)),
            pltpu.SemaphoreType.DMA((len(STEPS),)),
        ],
        compiler_params=pltpu.CompilerParams(collective_id=1, has_side_effects=True),
    )(cells)
    parts = dict(zip(STEPS, received))
    parts[(0, 0)] = cells
    bands = [
        jnp.concatenate([parts[(r, 1)], parts[(r, 0)], parts[(r, -1)]], axis=1) for r in (1, 0, -1)
    ]
    return jnp.concatenate(bands, axis=0)


def geometry(angle_value):
    radians = 2.0 * math.pi * angle_value.astype(jnp.float32) / NANG
    stretch = 0.5 + 0.5 * jnp.abs(jnp.cos(radians))
    spread = 1.0 + jnp.abs(jnp.sin(radians))
    return (radians, stretch, spread)


def footprint(radians, stretch, spread, row_global, rows_total, block_size):
    shifted = shift_reach * jnp.sin(radians + 2.0 * math.pi * row_global / rows_total)
    inside = jnp.arange(block_size).astype(jnp.float32) - 0.5 * (block_size - 1)
    centre = block_size + inside[None, :] * stretch + shifted[:, None]
    places = jnp.arange(2 * block_size).astype(jnp.float32) + 0.5
    weights = (
        jnp.maximum(0.0, 1.0 - jnp.abs(places[None, None, :] - centre[:, :, None]) / spread)
        / spread
    )
    return weights.astype(jnp.bfloat16)


def axial_table(offsets, lengths, depth_count):
    offset_real = offsets.astype(jnp.float32)[..., None]
    length_real = lengths.astype(jnp.float32)[..., None]
    depth_place = jnp.arange(depth_count).astype(jnp.float32) + 0.5
    centre = offset_real + depth_place * length_real / depth_count
    row_number = jnp.arange(2 * depth_count)
    row_place = row_number.astype(jnp.float32) + 0.5
    triangle = jnp.maximum(0.0, 1.0 - jnp.abs(row_place - centre[..., None]))
    inside = (row_number >= offsets[..., None, None]) & (
        row_number < (offsets + lengths)[..., None, None]
    )
    return jnp.where(inside, triangle, 0.0).astype(jnp.bfloat16)


def smooth_update(current, fidelity, row_first, depth_first, rows_total, depth_total):
    row_index = row_first + jnp.arange(current.shape[0])
    depth_index = depth_first + jnp.arange(current.shape[1])
    keep_rows = ((row_index >= 0) & (row_index < rows_total - 1)).astype(jnp.float32)[:, None, None]
    keep_depth = ((depth_index >= 0) & (depth_index < depth_total - 1)).astype(jnp.float32)[
        None, :, None
    ]
    forward_rows = (
        jnp.concatenate([current[1:] - current[:-1], jnp.zeros_like(current[:1])], 0) * keep_rows
    )
    forward_depth = (
        jnp.concatenate([current[:, 1:] - current[:, :-1], jnp.zeros_like(current[:, :1])], 1)
        * keep_depth
    )
    forward_width = jnp.concatenate(
        [current[:, :, 1:] - current[:, :, :-1], jnp.zeros_like(current[:, :, :1])], 2
    )
    inverse = lax.rsqrt(
        forward_rows * forward_rows
        + forward_depth * forward_depth
        + forward_width * forward_width
        + gradient_floor
    )
    normal_rows = forward_rows * inverse
    normal_depth = forward_depth * inverse
    normal_width = forward_width * inverse
    divergence = normal_rows - jnp.concatenate(
        [jnp.zeros_like(normal_rows[:1]), normal_rows[:-1]], 0
    )
    divergence = (
        divergence
        + normal_depth
        - jnp.concatenate([jnp.zeros_like(normal_depth[:, :1]), normal_depth[:, :-1]], 1)
    )
    divergence = (
        divergence
        + normal_width
        - jnp.concatenate([jnp.zeros_like(normal_width[:, :, :1]), normal_width[:, :, :-1]], 2)
    )
    return current + step_length * (smooth_weight * divergence - (current - fidelity))


def footprint_mats(angle_value, row_global, rows_total):
    radians, stretch, spread = geometry(angle_value)
    shifted = shift_reach * jnp.sin(radians + 2.0 * math.pi * row_global / rows_total)
    inside = jnp.arange(BLOCK).astype(jnp.float32) - 0.5 * (BLOCK - 1)
    centre = BLOCK + inside[None, :] * stretch + shifted[:, None]
    centre = jnp.concatenate([centre, centre], axis=1)
    places = jnp.arange(LANES).astype(jnp.float32)[:, None] + 0.5
    weights = (
        jnp.maximum(0.0, 1.0 - jnp.abs(places[None] - centre[:, None, :]) / spread) / spread
    )
    return weights.astype(jnp.bfloat16)


def backproject_kernel(shift_ref, columns_ref, mats_ref, out_ref, tiles_ref):
    p = pl.program_id(0)
    tile_count = out_ref.shape[2] // LANES
    depth_count = out_ref.shape[1]

    @pl.when(p == 0)
    def _():
        out_ref[...] = jnp.zeros_like(out_ref)
        tiles_ref[...] = jnp.zeros_like(tiles_ref)

    for tile in range(tile_count):
        tiles_ref[0, tile + 1] = columns_ref[0, :, tile * LANES:(tile + 1) * LANES].astype(
            jnp.float32
        )

    ends = jnp.concatenate([tiles_ref[0, 1], tiles_ref[0, tile_count]], axis=0).astype(jnp.bfloat16)
    second_half = lax.broadcasted_iota(jnp.int32, (LANES, LANES), 1) >= BLOCK
    empty = jnp.zeros((BLOCK, LANES), jnp.bfloat16)
    for row in range(out_ref.shape[0]):
        shift = shift_ref[p, row, 2] - 2
        start = (shift + 2) // 2
        odd = jnp.full((LANES, LANES), shift - 2 * (start - 1), jnp.int32) == 1
        whole = mats_ref[0, row]
        down = jnp.concatenate([empty, whole[:BLOCK]], axis=0)
        up = jnp.concatenate([whole[BLOCK:], empty], axis=0)
        nothing = jnp.zeros_like(whole)
        first = jnp.where(
            second_half, jnp.where(odd, nothing, down), jnp.where(odd, down, whole)
        )
        second = jnp.where(
            second_half, jnp.where(odd, whole, up), jnp.where(odd, up, nothing)
        )
        low = tiles_ref[0, pl.ds(start, tile_count)].reshape(tile_count * depth_count, LANES)
        high = tiles_ref[0, pl.ds(start + 1, tile_count)].reshape(tile_count * depth_count, LANES)
        taps = jnp.concatenate([low, high], axis=1).astype(jnp.bfloat16)
        result = jnp.dot(
            taps, jnp.concatenate([first, second], axis=0), preferred_element_type=jnp.float32
        )
        edge = jnp.dot(ends, whole, preferred_element_type=jnp.float32)
        shift_vec = jnp.full((depth_count, LANES), shift, jnp.int32)
        for tile in range(tile_count):
            part = result[tile * depth_count:(tile + 1) * depth_count]
            if tile == 0:
                part = jnp.where(shift_vec < 0, edge[:depth_count], part)
            elif tile == tile_count - 2:
                part = jnp.where(shift_vec >= 2, edge[depth_count:], part)
            elif tile == tile_count - 1:
                part = jnp.where(shift_vec >= 0, edge[depth_count:], part)
            lanes = pl.ds(tile * LANES, LANES)
            out_ref[row, :, lanes] = out_ref[row, :, lanes] + part

    @pl.when(p == pl.num_programs(0) - 1)
    def _():
        out_ref[...] = math.pi / P_SIZE * out_ref[...]


def backproject(shifts, columns, mats):
    count, rows = shifts.shape[0], shifts.shape[1]
    depth_count, column_count = columns.shape[1], columns.shape[2]
    tile_count = column_count // LANES
    return pl.pallas_call(
        backproject_kernel,
        out_shape=jax.ShapeDtypeStruct((rows, depth_count, column_count), jnp.float32),
        grid_spec=pltpu.PrefetchScalarGridSpec(
            num_scalar_prefetch=1,
            grid=(count,),
            in_specs=[
                pl.BlockSpec((1,) + columns.shape[1:], lambda p, s: (p, 0, 0)),
                pl.BlockSpec((1,) + mats.shape[1:], lambda p, s: (p, 0, 0, 0)),
            ],
            out_specs=pl.BlockSpec((rows, depth_count, column_count), lambda p, s: (0, 0, 0)),
            scratch_shapes=[pltpu.VMEM((1, tile_count + 3, depth_count, LANES), jnp.float32)],
        ),
        compiler_params=pltpu.CompilerParams(dimension_semantics=("arbitrary",)),
    )(shifts, columns, mats)


def per_device(filtered, angle_index, band_offset, band_length, foot_block):
    depth_count = filtered.shape[1]
    row_count = foot_block.shape[1]
    extended_band = with_halo(filtered, (("gz", 1),), depth_count // 2)
    axial_weights = axial_table(band_offset[:, 0], band_length[:, 0], depth_count)
    summed_rows = jnp.einsum(
        "pzv,pvu->pzu",
        axial_weights,
        extended_band,
        preferred_element_type=jnp.float32,
    )
    columns = gather_columns(summed_rows.astype(jnp.bfloat16))
    column_count = columns.shape[2]
    row_base = lax.axis_index("gy") * row_count
    depth_base = lax.axis_index("gz") * depth_count
    rows_total = lax.axis_size("gy") * row_count
    depth_total = lax.axis_size("gz") * depth_count
    row_global = (row_base + jnp.arange(row_count)).astype(jnp.float32)
    mats = jax.vmap(footprint_mats, in_axes=(0, None, None))(angle_index, row_global, rows_total)
    backprojection = backproject(foot_block, columns, mats)
    current = backprojection
    extended = with_wide_halo(backprojection, ITERS)
    fidelity = extended
    current = extended
    for turn_index in range(ITERS):
        reach = ITERS - turn_index
        current = smooth_update(
            current, fidelity, row_base - reach, depth_base - reach, rows_total, depth_total
        )[1:-1, 1:-1]
        fidelity = fidelity[1:-1, 1:-1]
    return current


def solution(mesh):
    return jax.shard_map(
        per_device,
        mesh=mesh,
        in_specs=(P(None, "gz", "gy"), P(), P(None, "gz"), P(None, "gz"), P(None, "gy", None)),
        out_specs=P("gy", "gz", None),
        check_vma=False,
    )
```

```python
import functools
import math

import jax
import jax.numpy as jnp
from jax import lax
from jax.experimental import pallas as pl
from jax.experimental.pallas import tpu as pltpu
from jax.sharding import PartitionSpec as P

X = 4096
P_SIZE = 16
NANG = 3600
BLOCK = 64
LANES = 128
GATHER_CHUNKS = 2
ITERS = 2


step_length = 0.25
smooth_weight = 0.3
gradient_floor = 0.01
shift_reach = 8.0


def with_halo(cells, sides, width):
    for axis, dim in sides:
        count = lax.axis_size(axis)
        ends = count - 1
        head = lax.slice_in_dim(cells, 0, width, axis=dim)
        tail = lax.slice_in_dim(cells, cells.shape[dim] - width, cells.shape[dim], axis=dim)
        cells = jnp.concatenate(
            [
                lax.ppermute(tail, axis, [(i, (i + 1) % count) for i in range(ends)]),
                cells,
                lax.ppermute(head, axis, [((i + 1) % count, i) for i in range(ends)]),
            ],
            axis=dim,
        )
    return cells


def gather_kernel(count, local_ref, out_ref, send_sem, recv_sem, own_sem):
    ring = count // 2
    forward_steps = ring // 2
    backward_steps = ring - 1 - forward_steps
    me = lax.axis_index("gy")
    depth_index = lax.axis_index("gz")
    half = me // ring
    place = me % ring
    width = local_ref.shape[2]
    mesh_kind = pl.DeviceIdType.MESH

    def device(half_of, place_of):
        return half_of * ring + lax.rem(place_of + 2 * ring, ring)

    partner = device(1 - half, place)
    right = device(half, place + 1)
    left = device(half, place - 1)

    chunks = GATHER_CHUNKS
    chunk_rows = local_ref.shape[0] // chunks

    def rows_of(chunk):
        return pl.ds(chunk * chunk_rows, chunk_rows)

    def slot(index, chunk):
        columns = pl.ds(pl.multiple_of(index * width, width), width)
        return out_ref.at[rows_of(chunk), :, columns]

    barrier = pltpu.get_barrier_semaphore()
    for peer in (partner, right, left):
        pl.semaphore_signal(barrier, inc=1, device_id=(depth_index, peer), device_id_type=mesh_kind)
    pl.semaphore_wait(barrier, 3)

    own = pltpu.make_async_copy(local_ref, out_ref.at[:, :, pl.ds(pl.multiple_of(me * width, width), width)], own_sem)
    own.start()
    sends = []

    def send(source, index, chunk, peer):
        copy = pltpu.make_async_remote_copy(
            src_ref=source,
            dst_ref=slot(index, chunk),
            send_sem=send_sem.at[len(sends)],
            recv_sem=recv_sem.at[index, chunk],
            device_id=(depth_index, peer),
            device_id_type=mesh_kind,
        )
        copy.start()
        sends.append(copy)

    def arrived(index, chunk):
        pltpu.make_async_remote_copy(
            src_ref=local_ref.at[rows_of(chunk)],
            dst_ref=slot(index, chunk),
            send_sem=send_sem.at[0],
            recv_sem=recv_sem.at[index, chunk],
            device_id=(depth_index, partner),
            device_id_type=mesh_kind,
        ).wait_recv()

    for chunk in range(chunks):
        send(local_ref.at[rows_of(chunk)], me, chunk, partner)
    for step in range(1, forward_steps + 1):
        for chunk in range(chunks):
            for direction, peer, limit in ((-1, right, forward_steps), (1, left, backward_steps)):
                if step > limit:
                    continue
                if step == 1:
                    send(local_ref.at[rows_of(chunk)], me, chunk, peer)
                    if direction == -1:
                        arrived(partner, chunk)
                    send(slot(partner, chunk), partner, chunk, peer)
                    continue
                for half_of in (0, 1):
                    index = device(half_of, place + direction * (step - 1))
                    arrived(index, chunk)
                    send(slot(index, chunk), index, chunk, peer)
    for direction, steps in ((-1, forward_steps), (1, backward_steps)):
        for half_of in (0, 1):
            for chunk in range(chunks):
                arrived(device(half_of, place + direction * steps), chunk)
    own.wait()
    for copy in sends:
        copy.wait_send()


def gather_columns(local):
    count = lax.axis_size("gy")
    rows, depth, width = local.shape
    return pl.pallas_call(
        functools.partial(gather_kernel, count),
        out_shape=jax.ShapeDtypeStruct((rows, depth, width * count), local.dtype),
        in_specs=[pl.BlockSpec(memory_space=pl.ANY)],
        out_specs=pl.BlockSpec(memory_space=pl.ANY),
        scratch_shapes=[
            pltpu.SemaphoreType.DMA((count * GATHER_CHUNKS,)),
            pltpu.SemaphoreType.DMA((count, GATHER_CHUNKS)),
            pltpu.SemaphoreType.DMA(()),
        ],
        compiler_params=pltpu.CompilerParams(collective_id=0, has_side_effects=True),
    )(local)


def band_kernel(count, width, band_ref, before_ref, after_ref, send_sem, recv_sem):
    me = lax.axis_index("gz")
    row_index = lax.axis_index("gy")
    depth = band_ref.shape[1]
    mesh_kind = pl.DeviceIdType.MESH
    below = (lax.rem(me + count - 1, count), row_index)
    above = (lax.rem(me + 1, count), row_index)
    barrier = pltpu.get_barrier_semaphore()
    for peer in (below, above):
        pl.semaphore_signal(barrier, inc=1, device_id=peer, device_id_type=mesh_kind)
    pl.semaphore_wait(barrier, 2)
    up = pltpu.make_async_remote_copy(
        src_ref=band_ref.at[:, pl.ds(depth - width, width)],
        dst_ref=before_ref,
        send_sem=send_sem.at[0],
        recv_sem=recv_sem.at[0],
        device_id=above,
        device_id_type=mesh_kind,
    )
    down = pltpu.make_async_remote_copy(
        src_ref=band_ref.at[:, pl.ds(0, width)],
        dst_ref=after_ref,
        send_sem=send_sem.at[1],
        recv_sem=recv_sem.at[1],
        device_id=below,
        device_id_type=mesh_kind,
    )
    up.start()
    down.start()
    up.wait()
    down.wait()


def with_band_halo(band, width):
    count = lax.axis_size("gz")
    me = lax.axis_index("gz")
    piece = jax.ShapeDtypeStruct((band.shape[0], width, band.shape[2]), band.dtype)
    before, after = pl.pallas_call(
        functools.partial(band_kernel, count, width),
        out_shape=[piece, piece],
        in_specs=[pl.BlockSpec(memory_space=pl.ANY)],
        out_specs=[pl.BlockSpec(memory_space=pl.ANY)] * 2,
        scratch_shapes=[pltpu.SemaphoreType.DMA((2,)), pltpu.SemaphoreType.DMA((2,))],
        compiler_params=pltpu.CompilerParams(collective_id=2, has_side_effects=True),
    )(band)
    before = jnp.where(me > 0, before, jnp.zeros_like(before))
    after = jnp.where(me < count - 1, after, jnp.zeros_like(after))
    return jnp.concatenate([before, band, after], axis=1)


STEPS = ((1, 1), (1, 0), (1, -1), (0, 1), (0, -1), (-1, 1), (-1, 0), (-1, -1))


def halo_kernel(count, width, cells_ref, *refs):
    pieces = len(STEPS)
    targets = refs[:pieces]
    send_sem, recv_sem = refs[pieces], refs[pieces + 1]
    row_count, depth_count = count
    rows, depth = cells_ref.shape[0], cells_ref.shape[1]
    row_parts = {1: pl.ds(rows - width, width), 0: pl.ds(0, rows), -1: pl.ds(0, width)}
    depth_parts = {1: pl.ds(depth - width, width), 0: pl.ds(0, depth), -1: pl.ds(0, width)}
    row_me = lax.axis_index("gy")
    depth_me = lax.axis_index("gz")
    peers = [
        (lax.rem(depth_me + depth_step + depth_count, depth_count),
         lax.rem(row_me + row_step + row_count, row_count))
        for row_step, depth_step in STEPS
    ]
    barrier = pltpu.get_barrier_semaphore()
    for peer in peers:
        pl.semaphore_signal(barrier, inc=1, device_id=peer, device_id_type=pl.DeviceIdType.MESH)
    pl.semaphore_wait(barrier, pieces)
    copies = []
    for k, peer in enumerate(peers):
        row_step, depth_step = STEPS[k]
        copy = pltpu.make_async_remote_copy(
            src_ref=cells_ref.at[row_parts[row_step], depth_parts[depth_step]],
            dst_ref=targets[k],
            send_sem=send_sem.at[k],
            recv_sem=recv_sem.at[k],
            device_id=peer,
            device_id_type=pl.DeviceIdType.MESH,
        )
        copy.start()
        copies.append(copy)
    for copy in copies:
        copy.wait()


def with_wide_halo(cells, width):
    rows, depth = cells.shape[0], cells.shape[1]
    count = (lax.axis_size("gy"), lax.axis_size("gz"))
    row_parts = {1: slice(rows - width, rows), 0: slice(None), -1: slice(0, width)}
    depth_parts = {1: slice(depth - width, depth), 0: slice(None), -1: slice(0, width)}
    sent = [cells[row_parts[r], depth_parts[d]] for r, d in STEPS]
    received = pl.pallas_call(
        functools.partial(halo_kernel, count, width),
        out_shape=[jax.ShapeDtypeStruct(piece.shape, piece.dtype) for piece in sent],
        in_specs=[pl.BlockSpec(memory_space=pl.ANY)],
        out_specs=[pl.BlockSpec(memory_space=pl.ANY)] * len(STEPS),
        scratch_shapes=[
            pltpu.SemaphoreType.DMA((len(STEPS),)),
            pltpu.SemaphoreType.DMA((len(STEPS),)),
        ],
        compiler_params=pltpu.CompilerParams(collective_id=1, has_side_effects=True),
    )(cells)
    parts = dict(zip(STEPS, received))
    parts[(0, 0)] = cells
    bands = [
        jnp.concatenate([parts[(r, 1)], parts[(r, 0)], parts[(r, -1)]], axis=1) for r in (1, 0, -1)
    ]
    return jnp.concatenate(bands, axis=0)


def geometry(angle_value):
    radians = 2.0 * math.pi * angle_value.astype(jnp.float32) / NANG
    stretch = 0.5 + 0.5 * jnp.abs(jnp.cos(radians))
    spread = 1.0 + jnp.abs(jnp.sin(radians))
    return (radians, stretch, spread)


def footprint(radians, stretch, spread, row_global, rows_total, block_size):
    shifted = shift_reach * jnp.sin(radians + 2.0 * math.pi * row_global / rows_total)
    inside = jnp.arange(block_size).astype(jnp.float32) - 0.5 * (block_size - 1)
    centre = block_size + inside[None, :] * stretch + shifted[:, None]
    places = jnp.arange(2 * block_size).astype(jnp.float32) + 0.5
    weights = (
        jnp.maximum(0.0, 1.0 - jnp.abs(places[None, None, :] - centre[:, :, None]) / spread)
        / spread
    )
    return weights.astype(jnp.bfloat16)


def axial_table(offsets, lengths, depth_count):
    offset_real = offsets.astype(jnp.float32)[..., None]
    length_real = lengths.astype(jnp.float32)[..., None]
    depth_place = jnp.arange(depth_count).astype(jnp.float32) + 0.5
    centre = offset_real + depth_place * length_real / depth_count
    row_number = jnp.arange(2 * depth_count)
    row_place = row_number.astype(jnp.float32) + 0.5
    triangle = jnp.maximum(0.0, 1.0 - jnp.abs(row_place - centre[..., None]))
    inside = (row_number >= offsets[..., None, None]) & (
        row_number < (offsets + lengths)[..., None, None]
    )
    return jnp.where(inside, triangle, 0.0).astype(jnp.bfloat16)


def smooth_update(current, fidelity, row_first, depth_first, rows_total, depth_total):
    row_index = row_first + jnp.arange(current.shape[0])
    depth_index = depth_first + jnp.arange(current.shape[1])
    keep_rows = ((row_index >= 0) & (row_index < rows_total - 1)).astype(jnp.float32)[:, None, None]
    keep_depth = ((depth_index >= 0) & (depth_index < depth_total - 1)).astype(jnp.float32)[
        None, :, None
    ]
    forward_rows = (
        jnp.concatenate([current[1:] - current[:-1], jnp.zeros_like(current[:1])], 0) * keep_rows
    )
    forward_depth = (
        jnp.concatenate([current[:, 1:] - current[:, :-1], jnp.zeros_like(current[:, :1])], 1)
        * keep_depth
    )
    forward_width = jnp.concatenate(
        [current[:, :, 1:] - current[:, :, :-1], jnp.zeros_like(current[:, :, :1])], 2
    )
    inverse = lax.rsqrt(
        forward_rows * forward_rows
        + forward_depth * forward_depth
        + forward_width * forward_width
        + gradient_floor
    )
    normal_rows = forward_rows * inverse
    normal_depth = forward_depth * inverse
    normal_width = forward_width * inverse
    divergence = normal_rows - jnp.concatenate(
        [jnp.zeros_like(normal_rows[:1]), normal_rows[:-1]], 0
    )
    divergence = (
        divergence
        + normal_depth
        - jnp.concatenate([jnp.zeros_like(normal_depth[:, :1]), normal_depth[:, :-1]], 1)
    )
    divergence = (
        divergence
        + normal_width
        - jnp.concatenate([jnp.zeros_like(normal_width[:, :, :1]), normal_width[:, :, :-1]], 2)
    )
    return current + step_length * (smooth_weight * divergence - (current - fidelity))


def footprint_mats(angle_value, row_global, rows_total):
    radians, stretch, spread = geometry(angle_value)
    shifted = shift_reach * jnp.sin(radians + 2.0 * math.pi * row_global / rows_total)
    inside = jnp.arange(BLOCK).astype(jnp.float32) - 0.5 * (BLOCK - 1)
    centre = BLOCK + inside[None, :] * stretch + shifted[:, None]
    centre = jnp.concatenate([centre, centre], axis=1)
    places = jnp.arange(LANES).astype(jnp.float32)[:, None] + 0.5
    weights = (
        jnp.maximum(0.0, 1.0 - jnp.abs(places[None] - centre[:, None, :]) / spread) / spread
    )
    return weights.astype(jnp.bfloat16)


def backproject_kernel(shift_ref, columns_ref, mats_ref, out_ref, tiles_ref):
    p = pl.program_id(0)
    tile_count = out_ref.shape[2] // LANES
    depth_count = out_ref.shape[1]

    @pl.when(p == 0)
    def _():
        out_ref[...] = jnp.zeros_like(out_ref)
        tiles_ref[...] = jnp.zeros_like(tiles_ref)

    for tile in range(tile_count):
        tiles_ref[0, tile + 1] = columns_ref[0, :, tile * LANES:(tile + 1) * LANES].astype(
            jnp.float32
        )

    ends = jnp.concatenate([tiles_ref[0, 1], tiles_ref[0, tile_count]], axis=0).astype(jnp.bfloat16)
    second_half = lax.broadcasted_iota(jnp.int32, (LANES, LANES), 1) >= BLOCK
    empty = jnp.zeros((BLOCK, LANES), jnp.bfloat16)
    for row in range(out_ref.shape[0]):
        shift = shift_ref[p, row, 2] - 2
        start = (shift + 2) // 2
        odd = jnp.full((LANES, LANES), shift - 2 * (start - 1), jnp.int32) == 1
        whole = mats_ref[0, row]
        down = jnp.concatenate([empty, whole[:BLOCK]], axis=0)
        up = jnp.concatenate([whole[BLOCK:], empty], axis=0)
        nothing = jnp.zeros_like(whole)
        first = jnp.where(
            second_half, jnp.where(odd, nothing, down), jnp.where(odd, down, whole)
        )
        second = jnp.where(
            second_half, jnp.where(odd, whole, up), jnp.where(odd, up, nothing)
        )
        low = tiles_ref[0, pl.ds(start, tile_count)].reshape(tile_count * depth_count, LANES)
        high = tiles_ref[0, pl.ds(start + 1, tile_count)].reshape(tile_count * depth_count, LANES)
        taps = jnp.concatenate([low, high], axis=1).astype(jnp.bfloat16)
        result = jnp.dot(
            taps, jnp.concatenate([first, second], axis=0), preferred_element_type=jnp.float32
        )
        edge = jnp.dot(ends, whole, preferred_element_type=jnp.float32)
        shift_vec = jnp.full((depth_count, LANES), shift, jnp.int32)
        for tile in range(tile_count):
            part = result[tile * depth_count:(tile + 1) * depth_count]
            if tile == 0:
                part = jnp.where(shift_vec < 0, edge[:depth_count], part)
            elif tile == tile_count - 2:
                part = jnp.where(shift_vec >= 2, edge[depth_count:], part)
            elif tile == tile_count - 1:
                part = jnp.where(shift_vec >= 0, edge[depth_count:], part)
            lanes = pl.ds(tile * LANES, LANES)
            out_ref[row, :, lanes] = out_ref[row, :, lanes] + part

    @pl.when(p == pl.num_programs(0) - 1)
    def _():
        out_ref[...] = math.pi / P_SIZE * out_ref[...]


def backproject(shifts, columns, mats):
    count, rows = shifts.shape[0], shifts.shape[1]
    depth_count, column_count = columns.shape[1], columns.shape[2]
    tile_count = column_count // LANES
    return pl.pallas_call(
        backproject_kernel,
        out_shape=jax.ShapeDtypeStruct((rows, depth_count, column_count), jnp.float32),
        grid_spec=pltpu.PrefetchScalarGridSpec(
            num_scalar_prefetch=1,
            grid=(count,),
            in_specs=[
                pl.BlockSpec((1,) + columns.shape[1:], lambda p, s: (p, 0, 0)),
                pl.BlockSpec((1,) + mats.shape[1:], lambda p, s: (p, 0, 0, 0)),
            ],
            out_specs=pl.BlockSpec((rows, depth_count, column_count), lambda p, s: (0, 0, 0)),
            scratch_shapes=[pltpu.VMEM((1, tile_count + 3, depth_count, LANES), jnp.float32)],
        ),
        compiler_params=pltpu.CompilerParams(dimension_semantics=("arbitrary",)),
    )(shifts, columns, mats)


def per_device(filtered, angle_index, band_offset, band_length, foot_block):
    depth_count = filtered.shape[1]
    row_count = foot_block.shape[1]
    extended_band = with_band_halo(filtered, depth_count // 2)
    axial_weights = axial_table(band_offset[:, 0], band_length[:, 0], depth_count)
    summed_rows = jnp.einsum(
        "pzv,pvu->pzu",
        axial_weights,
        extended_band,
        preferred_element_type=jnp.float32,
    )
    columns = gather_columns(summed_rows.astype(jnp.bfloat16))
    column_count = columns.shape[2]
    row_base = lax.axis_index("gy") * row_count
    depth_base = lax.axis_index("gz") * depth_count
    rows_total = lax.axis_size("gy") * row_count
    depth_total = lax.axis_size("gz") * depth_count
    row_global = (row_base + jnp.arange(row_count)).astype(jnp.float32)
    mats = jax.vmap(footprint_mats, in_axes=(0, None, None))(angle_index, row_global, rows_total)
    backprojection = backproject(foot_block, columns, mats)
    current = backprojection
    extended = with_wide_halo(backprojection, ITERS)
    fidelity = extended
    current = extended
    for turn_index in range(ITERS):
        reach = ITERS - turn_index
        current = smooth_update(
            current, fidelity, row_base - reach, depth_base - reach, rows_total, depth_total
        )[1:-1, 1:-1]
        fidelity = fidelity[1:-1, 1:-1]
    return current


def solution(mesh):
    return jax.shard_map(
        per_device,
        mesh=mesh,
        in_specs=(P(None, "gz", "gy"), P(), P(None, "gz"), P(None, "gz"), P(None, "gy", None)),
        out_specs=P("gy", "gz", None),
        check_vma=False,
    )
```

```python
import functools
import math

import jax
import jax.numpy as jnp
from jax import lax
from jax.experimental import pallas as pl
from jax.experimental.pallas import tpu as pltpu
from jax.sharding import PartitionSpec as P

X = 4096
P_SIZE = 16
NANG = 3600
BLOCK = 64
LANES = 128
GATHER_CHUNKS = 2
ITERS = 2


step_length = 0.25
smooth_weight = 0.3
gradient_floor = 0.01
shift_reach = 8.0


def with_halo(cells, sides, width):
    for axis, dim in sides:
        count = lax.axis_size(axis)
        ends = count - 1
        head = lax.slice_in_dim(cells, 0, width, axis=dim)
        tail = lax.slice_in_dim(cells, cells.shape[dim] - width, cells.shape[dim], axis=dim)
        cells = jnp.concatenate(
            [
                lax.ppermute(tail, axis, [(i, (i + 1) % count) for i in range(ends)]),
                cells,
                lax.ppermute(head, axis, [((i + 1) % count, i) for i in range(ends)]),
            ],
            axis=dim,
        )
    return cells


def gather_kernel(count, local_ref, out_ref, send_sem, recv_sem, own_sem):
    ring = count // 2
    forward_steps = ring // 2
    backward_steps = ring - 1 - forward_steps
    me = lax.axis_index("gy")
    depth_index = lax.axis_index("gz")
    half = me // ring
    place = me % ring
    width = local_ref.shape[2]
    mesh_kind = pl.DeviceIdType.MESH

    def device(half_of, place_of):
        return half_of * ring + lax.rem(place_of + 2 * ring, ring)

    partner = device(1 - half, place)
    right = device(half, place + 1)
    left = device(half, place - 1)

    chunks = GATHER_CHUNKS
    chunk_rows = local_ref.shape[0] // chunks

    def rows_of(chunk):
        return pl.ds(chunk * chunk_rows, chunk_rows)

    def slot(index, chunk):
        columns = pl.ds(pl.multiple_of(index * width, width), width)
        return out_ref.at[rows_of(chunk), :, columns]

    barrier = pltpu.get_barrier_semaphore()
    for peer in (partner, right, left):
        pl.semaphore_signal(barrier, inc=1, device_id=(depth_index, peer), device_id_type=mesh_kind)
    pl.semaphore_wait(barrier, 3)

    own = pltpu.make_async_copy(local_ref, out_ref.at[:, :, pl.ds(pl.multiple_of(me * width, width), width)], own_sem)
    own.start()
    sends = []

    def send(source, index, chunk, peer):
        copy = pltpu.make_async_remote_copy(
            src_ref=source,
            dst_ref=slot(index, chunk),
            send_sem=send_sem.at[len(sends)],
            recv_sem=recv_sem.at[index, chunk],
            device_id=(depth_index, peer),
            device_id_type=mesh_kind,
        )
        copy.start()
        sends.append(copy)

    def arrived(index, chunk):
        pltpu.make_async_remote_copy(
            src_ref=local_ref.at[rows_of(chunk)],
            dst_ref=slot(index, chunk),
            send_sem=send_sem.at[0],
            recv_sem=recv_sem.at[index, chunk],
            device_id=(depth_index, partner),
            device_id_type=mesh_kind,
        ).wait_recv()

    for chunk in range(chunks):
        send(local_ref.at[rows_of(chunk)], me, chunk, partner)
    for step in range(1, forward_steps + 1):
        for chunk in range(chunks):
            for direction, peer, limit in ((-1, right, forward_steps), (1, left, backward_steps)):
                if step > limit:
                    continue
                if step == 1:
                    send(local_ref.at[rows_of(chunk)], me, chunk, peer)
                    if direction == -1:
                        arrived(partner, chunk)
                    send(slot(partner, chunk), partner, chunk, peer)
                    continue
                for half_of in (0, 1):
                    index = device(half_of, place + direction * (step - 1))
                    arrived(index, chunk)
                    send(slot(index, chunk), index, chunk, peer)
    for direction, steps in ((-1, forward_steps), (1, backward_steps)):
        for half_of in (0, 1):
            for chunk in range(chunks):
                arrived(device(half_of, place + direction * steps), chunk)
    own.wait()
    for copy in sends:
        copy.wait_send()


def gather_columns(local):
    count = lax.axis_size("gy")
    rows, depth, width = local.shape
    return pl.pallas_call(
        functools.partial(gather_kernel, count),
        out_shape=jax.ShapeDtypeStruct((rows, depth, width * count), local.dtype),
        in_specs=[pl.BlockSpec(memory_space=pl.ANY)],
        out_specs=pl.BlockSpec(memory_space=pl.ANY),
        scratch_shapes=[
            pltpu.SemaphoreType.DMA((count * GATHER_CHUNKS,)),
            pltpu.SemaphoreType.DMA((count, GATHER_CHUNKS)),
            pltpu.SemaphoreType.DMA(()),
        ],
        compiler_params=pltpu.CompilerParams(collective_id=0, has_side_effects=True),
    )(local)


STEPS = ((1, 1), (1, 0), (1, -1), (0, 1), (0, -1), (-1, 1), (-1, 0), (-1, -1))


def halo_kernel(count, width, cells_ref, *refs):
    pieces = len(STEPS)
    targets = refs[:pieces]
    send_sem, recv_sem = refs[pieces], refs[pieces + 1]
    row_count, depth_count = count
    rows, depth = cells_ref.shape[0], cells_ref.shape[1]
    row_parts = {1: pl.ds(rows - width, width), 0: pl.ds(0, rows), -1: pl.ds(0, width)}
    depth_parts = {1: pl.ds(depth - width, width), 0: pl.ds(0, depth), -1: pl.ds(0, width)}
    row_me = lax.axis_index("gy")
    depth_me = lax.axis_index("gz")
    peers = [
        (lax.rem(depth_me + depth_step + depth_count, depth_count),
         lax.rem(row_me + row_step + row_count, row_count))
        for row_step, depth_step in STEPS
    ]
    barrier = pltpu.get_barrier_semaphore()
    for peer in peers:
        pl.semaphore_signal(barrier, inc=1, device_id=peer, device_id_type=pl.DeviceIdType.MESH)
    pl.semaphore_wait(barrier, pieces)
    copies = []
    for k, peer in enumerate(peers):
        row_step, depth_step = STEPS[k]
        copy = pltpu.make_async_remote_copy(
            src_ref=cells_ref.at[row_parts[row_step], depth_parts[depth_step]],
            dst_ref=targets[k],
            send_sem=send_sem.at[k],
            recv_sem=recv_sem.at[k],
            device_id=peer,
            device_id_type=pl.DeviceIdType.MESH,
        )
        copy.start()
        copies.append(copy)
    for copy in copies:
        copy.wait()


def with_wide_halo(cells, width):
    rows, depth = cells.shape[0], cells.shape[1]
    count = (lax.axis_size("gy"), lax.axis_size("gz"))
    row_parts = {1: slice(rows - width, rows), 0: slice(None), -1: slice(0, width)}
    depth_parts = {1: slice(depth - width, depth), 0: slice(None), -1: slice(0, width)}
    sent = [cells[row_parts[r], depth_parts[d]] for r, d in STEPS]
    received = pl.pallas_call(
        functools.partial(halo_kernel, count, width),
        out_shape=[jax.ShapeDtypeStruct(piece.shape, piece.dtype) for piece in sent],
        in_specs=[pl.BlockSpec(memory_space=pl.ANY)],
        out_specs=[pl.BlockSpec(memory_space=pl.ANY)] * len(STEPS),
        scratch_shapes=[
            pltpu.SemaphoreType.DMA((len(STEPS),)),
            pltpu.SemaphoreType.DMA((len(STEPS),)),
        ],
        compiler_params=pltpu.CompilerParams(collective_id=1, has_side_effects=True),
    )(cells)
    parts = dict(zip(STEPS, received))
    parts[(0, 0)] = cells
    bands = [
        jnp.concatenate([parts[(r, 1)], parts[(r, 0)], parts[(r, -1)]], axis=1) for r in (1, 0, -1)
    ]
    return jnp.concatenate(bands, axis=0)


def geometry(angle_value):
    radians = 2.0 * math.pi * angle_value.astype(jnp.float32) / NANG
    stretch = 0.5 + 0.5 * jnp.abs(jnp.cos(radians))
    spread = 1.0 + jnp.abs(jnp.sin(radians))
    return (radians, stretch, spread)


def footprint(radians, stretch, spread, row_global, rows_total, block_size):
    shifted = shift_reach * jnp.sin(radians + 2.0 * math.pi * row_global / rows_total)
    inside = jnp.arange(block_size).astype(jnp.float32) - 0.5 * (block_size - 1)
    centre = block_size + inside[None, :] * stretch + shifted[:, None]
    places = jnp.arange(2 * block_size).astype(jnp.float32) + 0.5
    weights = (
        jnp.maximum(0.0, 1.0 - jnp.abs(places[None, None, :] - centre[:, :, None]) / spread)
        / spread
    )
    return weights.astype(jnp.bfloat16)


def axial_table(offsets, lengths, depth_count):
    offset_real = offsets.astype(jnp.float32)[..., None]
    length_real = lengths.astype(jnp.float32)[..., None]
    depth_place = jnp.arange(depth_count).astype(jnp.float32) + 0.5
    centre = offset_real + depth_place * length_real / depth_count
    row_number = jnp.arange(2 * depth_count)
    row_place = row_number.astype(jnp.float32) + 0.5
    triangle = jnp.maximum(0.0, 1.0 - jnp.abs(row_place - centre[..., None]))
    inside = (row_number >= offsets[..., None, None]) & (
        row_number < (offsets + lengths)[..., None, None]
    )
    return jnp.where(inside, triangle, 0.0).astype(jnp.bfloat16)


def smooth_update(current, fidelity, row_first, depth_first, rows_total, depth_total):
    row_index = row_first + jnp.arange(current.shape[0])
    depth_index = depth_first + jnp.arange(current.shape[1])
    keep_rows = ((row_index >= 0) & (row_index < rows_total - 1)).astype(jnp.float32)[:, None, None]
    keep_depth = ((depth_index >= 0) & (depth_index < depth_total - 1)).astype(jnp.float32)[
        None, :, None
    ]
    forward_rows = (
        jnp.concatenate([current[1:] - current[:-1], jnp.zeros_like(current[:1])], 0) * keep_rows
    )
    forward_depth = (
        jnp.concatenate([current[:, 1:] - current[:, :-1], jnp.zeros_like(current[:, :1])], 1)
        * keep_depth
    )
    forward_width = jnp.concatenate(
        [current[:, :, 1:] - current[:, :, :-1], jnp.zeros_like(current[:, :, :1])], 2
    )
    inverse = lax.rsqrt(
        forward_rows * forward_rows
        + forward_depth * forward_depth
        + forward_width * forward_width
        + gradient_floor
    )
    normal_rows = forward_rows * inverse
    normal_depth = forward_depth * inverse
    normal_width = forward_width * inverse
    divergence = normal_rows - jnp.concatenate(
        [jnp.zeros_like(normal_rows[:1]), normal_rows[:-1]], 0
    )
    divergence = (
        divergence
        + normal_depth
        - jnp.concatenate([jnp.zeros_like(normal_depth[:, :1]), normal_depth[:, :-1]], 1)
    )
    divergence = (
        divergence
        + normal_width
        - jnp.concatenate([jnp.zeros_like(normal_width[:, :, :1]), normal_width[:, :, :-1]], 2)
    )
    return current + step_length * (smooth_weight * divergence - (current - fidelity))


def footprint_mats(angle_value, row_global, rows_total):
    radians, stretch, spread = geometry(angle_value)
    shifted = shift_reach * jnp.sin(radians + 2.0 * math.pi * row_global / rows_total)
    inside = jnp.arange(BLOCK).astype(jnp.float32) - 0.5 * (BLOCK - 1)
    centre = BLOCK + inside[None, :] * stretch + shifted[:, None]
    centre = jnp.concatenate([centre, centre], axis=1)
    places = jnp.arange(LANES).astype(jnp.float32)[:, None] + 0.5
    weights = (
        jnp.maximum(0.0, 1.0 - jnp.abs(places[None] - centre[:, None, :]) / spread) / spread
    )
    return weights.astype(jnp.bfloat16)


def backproject_kernel(shift_ref, columns_ref, mats_ref, out_ref, tiles_ref):
    p = pl.program_id(0)
    tile_count = out_ref.shape[2] // LANES
    depth_count = out_ref.shape[1]

    @pl.when(p == 0)
    def _():
        out_ref[...] = jnp.zeros_like(out_ref)
        tiles_ref[...] = jnp.zeros_like(tiles_ref)

    for tile in range(tile_count):
        tiles_ref[0, tile + 1] = columns_ref[0, :, tile * LANES:(tile + 1) * LANES].astype(
            jnp.float32
        )

    ends = jnp.concatenate([tiles_ref[0, 1], tiles_ref[0, tile_count]], axis=0).astype(jnp.bfloat16)
    second_half = lax.broadcasted_iota(jnp.int32, (LANES, LANES), 1) >= BLOCK
    empty = jnp.zeros((BLOCK, LANES), jnp.bfloat16)
    for row in range(out_ref.shape[0]):
        shift = shift_ref[p, row, 2] - 2
        start = (shift + 2) // 2
        odd = jnp.full((LANES, LANES), shift - 2 * (start - 1), jnp.int32) == 1
        whole = mats_ref[0, row]
        down = jnp.concatenate([empty, whole[:BLOCK]], axis=0)
        up = jnp.concatenate([whole[BLOCK:], empty], axis=0)
        nothing = jnp.zeros_like(whole)
        first = jnp.where(
            second_half, jnp.where(odd, nothing, down), jnp.where(odd, down, whole)
        )
        second = jnp.where(
            second_half, jnp.where(odd, whole, up), jnp.where(odd, up, nothing)
        )
        low = tiles_ref[0, pl.ds(start, tile_count)].reshape(tile_count * depth_count, LANES)
        high = tiles_ref[0, pl.ds(start + 1, tile_count)].reshape(tile_count * depth_count, LANES)
        taps = jnp.concatenate([low, high], axis=1).astype(jnp.bfloat16)
        result = jnp.dot(
            taps, jnp.concatenate([first, second], axis=0), preferred_element_type=jnp.float32
        )
        edge = jnp.dot(ends, whole, preferred_element_type=jnp.float32)
        shift_vec = jnp.full((depth_count, LANES), shift, jnp.int32)
        for tile in range(tile_count):
            part = result[tile * depth_count:(tile + 1) * depth_count]
            if tile == 0:
                part = jnp.where(shift_vec < 0, edge[:depth_count], part)
            elif tile == tile_count - 2:
                part = jnp.where(shift_vec >= 2, edge[depth_count:], part)
            elif tile == tile_count - 1:
                part = jnp.where(shift_vec >= 0, edge[depth_count:], part)
            lanes = pl.ds(tile * LANES, LANES)
            out_ref[row, :, lanes] = out_ref[row, :, lanes] + part

    @pl.when(p == pl.num_programs(0) - 1)
    def _():
        out_ref[...] = math.pi / P_SIZE * out_ref[...]


def backproject(shifts, columns, mats):
    count, rows = shifts.shape[0], shifts.shape[1]
    depth_count, column_count = columns.shape[1], columns.shape[2]
    tile_count = column_count // LANES
    return pl.pallas_call(
        backproject_kernel,
        out_shape=jax.ShapeDtypeStruct((rows, depth_count, column_count), jnp.float32),
        grid_spec=pltpu.PrefetchScalarGridSpec(
            num_scalar_prefetch=1,
            grid=(count,),
            in_specs=[
                pl.BlockSpec((1,) + columns.shape[1:], lambda p, s: (p, 0, 0)),
                pl.BlockSpec((1,) + mats.shape[1:], lambda p, s: (p, 0, 0, 0)),
            ],
            out_specs=pl.BlockSpec((rows, depth_count, column_count), lambda p, s: (0, 0, 0)),
            scratch_shapes=[pltpu.VMEM((1, tile_count + 3, depth_count, LANES), jnp.float32)],
        ),
        compiler_params=pltpu.CompilerParams(dimension_semantics=("arbitrary",)),
    )(shifts, columns, mats)


def smooth_inner(current, fidelity, row_first, depth_first, rows_total, depth_total):
    row_index = row_first + jnp.arange(current.shape[0])
    depth_index = depth_first + jnp.arange(current.shape[1])
    keep_rows = ((row_index >= 0) & (row_index < rows_total - 1)).astype(jnp.float32)[:, None, None]
    keep_depth = ((depth_index >= 0) & (depth_index < depth_total - 1)).astype(jnp.float32)[
        None, :, None
    ]
    rows_here, rows_before = keep_rows[1:-1], keep_rows[:-2]
    depth_here, depth_before = keep_depth[:, 1:-1], keep_depth[:, :-2]

    def across(cells):
        return jnp.concatenate([cells[:, :, 1:] - cells[:, :, :-1], jnp.zeros_like(cells[:, :, :1])], 2)

    centre = current[1:-1, 1:-1]
    row_next, row_prev = current[2:, 1:-1], current[:-2, 1:-1]
    depth_next, depth_prev = current[1:-1, 2:], current[1:-1, :-2]
    prev_row_next_depth = current[:-2, 2:]
    next_row_prev_depth = current[2:, :-2]

    def inverse(a, b, c):
        return lax.rsqrt(a * a + b * b + c * c + gradient_floor)

    rows_d = (row_next - centre) * rows_here
    depth_d = (depth_next - centre) * depth_here
    width_d = across(centre)
    scale = inverse(rows_d, depth_d, width_d)
    prev_rows_d = (centre - row_prev) * rows_before
    prev_scale = inverse(prev_rows_d, (prev_row_next_depth - row_prev) * depth_here, across(row_prev))
    prev_depth_d = (centre - depth_prev) * depth_before
    low_scale = inverse(
        (next_row_prev_depth - depth_prev) * rows_here, prev_depth_d, across(depth_prev)
    )
    width_n = width_d * scale
    divergence = rows_d * scale - prev_rows_d * prev_scale
    divergence = divergence + depth_d * scale - prev_depth_d * low_scale
    divergence = divergence + width_n - jnp.concatenate(
        [jnp.zeros_like(width_n[:, :, :1]), width_n[:, :, :-1]], 2
    )
    return centre + step_length * (smooth_weight * divergence - (centre - fidelity[1:-1, 1:-1]))


def per_device(filtered, angle_index, band_offset, band_length, foot_block):
    depth_count = filtered.shape[1]
    row_count = foot_block.shape[1]
    extended_band = with_halo(filtered, (("gz", 1),), depth_count // 2)
    axial_weights = axial_table(band_offset[:, 0], band_length[:, 0], depth_count)
    summed_rows = jnp.einsum(
        "pzv,pvu->pzu",
        axial_weights,
        extended_band,
        preferred_element_type=jnp.float32,
    )
    columns = gather_columns(summed_rows.astype(jnp.bfloat16))
    column_count = columns.shape[2]
    row_base = lax.axis_index("gy") * row_count
    depth_base = lax.axis_index("gz") * depth_count
    rows_total = lax.axis_size("gy") * row_count
    depth_total = lax.axis_size("gz") * depth_count
    row_global = (row_base + jnp.arange(row_count)).astype(jnp.float32)
    mats = jax.vmap(footprint_mats, in_axes=(0, None, None))(angle_index, row_global, rows_total)
    backprojection = backproject(foot_block, columns, mats)
    current = backprojection
    extended = with_wide_halo(backprojection, ITERS)
    fidelity = extended
    current = extended
    for turn_index in range(ITERS):
        reach = ITERS - turn_index
        current = smooth_inner(
            current, fidelity, row_base - reach, depth_base - reach, rows_total, depth_total
        )
        fidelity = fidelity[1:-1, 1:-1]
    return current


def solution(mesh):
    return jax.shard_map(
        per_device,
        mesh=mesh,
        in_specs=(P(None, "gz", "gy"), P(), P(None, "gz"), P(None, "gz"), P(None, "gy", None)),
        out_specs=P("gy", "gz", None),
        check_vma=False,
    )
```

```python
import functools
import math

import jax
import jax.numpy as jnp
from jax import lax
from jax.experimental import pallas as pl
from jax.experimental.pallas import tpu as pltpu
from jax.sharding import PartitionSpec as P

X = 4096
P_SIZE = 16
NANG = 3600
BLOCK = 64
LANES = 128
GATHER_CHUNKS = 2
PER_STEP = 2
ITERS = 2


step_length = 0.25
smooth_weight = 0.3
gradient_floor = 0.01
shift_reach = 8.0


def with_halo(cells, sides, width):
    for axis, dim in sides:
        count = lax.axis_size(axis)
        ends = count - 1
        head = lax.slice_in_dim(cells, 0, width, axis=dim)
        tail = lax.slice_in_dim(cells, cells.shape[dim] - width, cells.shape[dim], axis=dim)
        cells = jnp.concatenate(
            [
                lax.ppermute(tail, axis, [(i, (i + 1) % count) for i in range(ends)]),
                cells,
                lax.ppermute(head, axis, [((i + 1) % count, i) for i in range(ends)]),
            ],
            axis=dim,
        )
    return cells


def gather_kernel(count, local_ref, out_ref, send_sem, recv_sem, own_sem):
    ring = count // 2
    forward_steps = ring // 2
    backward_steps = ring - 1 - forward_steps
    me = lax.axis_index("gy")
    depth_index = lax.axis_index("gz")
    half = me // ring
    place = me % ring
    width = local_ref.shape[2]
    mesh_kind = pl.DeviceIdType.MESH

    def device(half_of, place_of):
        return half_of * ring + lax.rem(place_of + 2 * ring, ring)

    partner = device(1 - half, place)
    right = device(half, place + 1)
    left = device(half, place - 1)

    chunks = GATHER_CHUNKS
    chunk_rows = local_ref.shape[0] // chunks

    def rows_of(chunk):
        return pl.ds(chunk * chunk_rows, chunk_rows)

    def slot(index, chunk):
        columns = pl.ds(pl.multiple_of(index * width, width), width)
        return out_ref.at[rows_of(chunk), :, columns]

    barrier = pltpu.get_barrier_semaphore()
    for peer in (partner, right, left):
        pl.semaphore_signal(barrier, inc=1, device_id=(depth_index, peer), device_id_type=mesh_kind)
    pl.semaphore_wait(barrier, 3)

    own = pltpu.make_async_copy(local_ref, out_ref.at[:, :, pl.ds(pl.multiple_of(me * width, width), width)], own_sem)
    own.start()
    sends = []

    def send(source, index, chunk, peer):
        copy = pltpu.make_async_remote_copy(
            src_ref=source,
            dst_ref=slot(index, chunk),
            send_sem=send_sem.at[len(sends)],
            recv_sem=recv_sem.at[index, chunk],
            device_id=(depth_index, peer),
            device_id_type=mesh_kind,
        )
        copy.start()
        sends.append(copy)

    def arrived(index, chunk):
        pltpu.make_async_remote_copy(
            src_ref=local_ref.at[rows_of(chunk)],
            dst_ref=slot(index, chunk),
            send_sem=send_sem.at[0],
            recv_sem=recv_sem.at[index, chunk],
            device_id=(depth_index, partner),
            device_id_type=mesh_kind,
        ).wait_recv()

    for chunk in range(chunks):
        send(local_ref.at[rows_of(chunk)], me, chunk, partner)
    for step in range(1, forward_steps + 1):
        for chunk in range(chunks):
            for direction, peer, limit in ((-1, right, forward_steps), (1, left, backward_steps)):
                if step > limit:
                    continue
                if step == 1:
                    send(local_ref.at[rows_of(chunk)], me, chunk, peer)
                    if direction == -1:
                        arrived(partner, chunk)
                    send(slot(partner, chunk), partner, chunk, peer)
                    continue
                for half_of in (0, 1):
                    index = device(half_of, place + direction * (step - 1))
                    arrived(index, chunk)
                    send(slot(index, chunk), index, chunk, peer)
    for direction, steps in ((-1, forward_steps), (1, backward_steps)):
        for half_of in (0, 1):
            for chunk in range(chunks):
                arrived(device(half_of, place + direction * steps), chunk)
    own.wait()
    for copy in sends:
        copy.wait_send()


def gather_columns(local):
    count = lax.axis_size("gy")
    rows, depth, width = local.shape
    return pl.pallas_call(
        functools.partial(gather_kernel, count),
        out_shape=jax.ShapeDtypeStruct((rows, depth, width * count), local.dtype),
        in_specs=[pl.BlockSpec(memory_space=pl.ANY)],
        out_specs=pl.BlockSpec(memory_space=pl.ANY),
        scratch_shapes=[
            pltpu.SemaphoreType.DMA((count * GATHER_CHUNKS,)),
            pltpu.SemaphoreType.DMA((count, GATHER_CHUNKS)),
            pltpu.SemaphoreType.DMA(()),
        ],
        compiler_params=pltpu.CompilerParams(collective_id=0, has_side_effects=True),
    )(local)


STEPS = ((1, 1), (1, 0), (1, -1), (0, 1), (0, -1), (-1, 1), (-1, 0), (-1, -1))


def halo_kernel(count, width, cells_ref, *refs):
    pieces = len(STEPS)
    targets = refs[:pieces]
    send_sem, recv_sem = refs[pieces], refs[pieces + 1]
    row_count, depth_count = count
    rows, depth = cells_ref.shape[0], cells_ref.shape[1]
    row_parts = {1: pl.ds(rows - width, width), 0: pl.ds(0, rows), -1: pl.ds(0, width)}
    depth_parts = {1: pl.ds(depth - width, width), 0: pl.ds(0, depth), -1: pl.ds(0, width)}
    row_me = lax.axis_index("gy")
    depth_me = lax.axis_index("gz")
    peers = [
        (lax.rem(depth_me + depth_step + depth_count, depth_count),
         lax.rem(row_me + row_step + row_count, row_count))
        for row_step, depth_step in STEPS
    ]
    barrier = pltpu.get_barrier_semaphore()
    for peer in peers:
        pl.semaphore_signal(barrier, inc=1, device_id=peer, device_id_type=pl.DeviceIdType.MESH)
    pl.semaphore_wait(barrier, pieces)
    copies = []
    for k, peer in enumerate(peers):
        row_step, depth_step = STEPS[k]
        copy = pltpu.make_async_remote_copy(
            src_ref=cells_ref.at[row_parts[row_step], depth_parts[depth_step]],
            dst_ref=targets[k],
            send_sem=send_sem.at[k],
            recv_sem=recv_sem.at[k],
            device_id=peer,
            device_id_type=pl.DeviceIdType.MESH,
        )
        copy.start()
        copies.append(copy)
    for copy in copies:
        copy.wait()


def with_wide_halo(cells, width):
    rows, depth = cells.shape[0], cells.shape[1]
    count = (lax.axis_size("gy"), lax.axis_size("gz"))
    row_parts = {1: slice(rows - width, rows), 0: slice(None), -1: slice(0, width)}
    depth_parts = {1: slice(depth - width, depth), 0: slice(None), -1: slice(0, width)}
    sent = [cells[row_parts[r], depth_parts[d]] for r, d in STEPS]
    received = pl.pallas_call(
        functools.partial(halo_kernel, count, width),
        out_shape=[jax.ShapeDtypeStruct(piece.shape, piece.dtype) for piece in sent],
        in_specs=[pl.BlockSpec(memory_space=pl.ANY)],
        out_specs=[pl.BlockSpec(memory_space=pl.ANY)] * len(STEPS),
        scratch_shapes=[
            pltpu.SemaphoreType.DMA((len(STEPS),)),
            pltpu.SemaphoreType.DMA((len(STEPS),)),
        ],
        compiler_params=pltpu.CompilerParams(collective_id=1, has_side_effects=True),
    )(cells)
    parts = dict(zip(STEPS, received))
    parts[(0, 0)] = cells
    bands = [
        jnp.concatenate([parts[(r, 1)], parts[(r, 0)], parts[(r, -1)]], axis=1) for r in (1, 0, -1)
    ]
    return jnp.concatenate(bands, axis=0)


def geometry(angle_value):
    radians = 2.0 * math.pi * angle_value.astype(jnp.float32) / NANG
    stretch = 0.5 + 0.5 * jnp.abs(jnp.cos(radians))
    spread = 1.0 + jnp.abs(jnp.sin(radians))
    return (radians, stretch, spread)


def footprint(radians, stretch, spread, row_global, rows_total, block_size):
    shifted = shift_reach * jnp.sin(radians + 2.0 * math.pi * row_global / rows_total)
    inside = jnp.arange(block_size).astype(jnp.float32) - 0.5 * (block_size - 1)
    centre = block_size + inside[None, :] * stretch + shifted[:, None]
    places = jnp.arange(2 * block_size).astype(jnp.float32) + 0.5
    weights = (
        jnp.maximum(0.0, 1.0 - jnp.abs(places[None, None, :] - centre[:, :, None]) / spread)
        / spread
    )
    return weights.astype(jnp.bfloat16)


def axial_table(offsets, lengths, depth_count):
    offset_real = offsets.astype(jnp.float32)[..., None]
    length_real = lengths.astype(jnp.float32)[..., None]
    depth_place = jnp.arange(depth_count).astype(jnp.float32) + 0.5
    centre = offset_real + depth_place * length_real / depth_count
    row_number = jnp.arange(2 * depth_count)
    row_place = row_number.astype(jnp.float32) + 0.5
    triangle = jnp.maximum(0.0, 1.0 - jnp.abs(row_place - centre[..., None]))
    inside = (row_number >= offsets[..., None, None]) & (
        row_number < (offsets + lengths)[..., None, None]
    )
    return jnp.where(inside, triangle, 0.0).astype(jnp.bfloat16)


def smooth_update(current, fidelity, row_first, depth_first, rows_total, depth_total):
    row_index = row_first + jnp.arange(current.shape[0])
    depth_index = depth_first + jnp.arange(current.shape[1])
    keep_rows = ((row_index >= 0) & (row_index < rows_total - 1)).astype(jnp.float32)[:, None, None]
    keep_depth = ((depth_index >= 0) & (depth_index < depth_total - 1)).astype(jnp.float32)[
        None, :, None
    ]
    forward_rows = (
        jnp.concatenate([current[1:] - current[:-1], jnp.zeros_like(current[:1])], 0) * keep_rows
    )
    forward_depth = (
        jnp.concatenate([current[:, 1:] - current[:, :-1], jnp.zeros_like(current[:, :1])], 1)
        * keep_depth
    )
    forward_width = jnp.concatenate(
        [current[:, :, 1:] - current[:, :, :-1], jnp.zeros_like(current[:, :, :1])], 2
    )
    inverse = lax.rsqrt(
        forward_rows * forward_rows
        + forward_depth * forward_depth
        + forward_width * forward_width
        + gradient_floor
    )
    normal_rows = forward_rows * inverse
    normal_depth = forward_depth * inverse
    normal_width = forward_width * inverse
    divergence = normal_rows - jnp.concatenate(
        [jnp.zeros_like(normal_rows[:1]), normal_rows[:-1]], 0
    )
    divergence = (
        divergence
        + normal_depth
        - jnp.concatenate([jnp.zeros_like(normal_depth[:, :1]), normal_depth[:, :-1]], 1)
    )
    divergence = (
        divergence
        + normal_width
        - jnp.concatenate([jnp.zeros_like(normal_width[:, :, :1]), normal_width[:, :, :-1]], 2)
    )
    return current + step_length * (smooth_weight * divergence - (current - fidelity))


def footprint_mats(angle_value, row_global, rows_total):
    radians, stretch, spread = geometry(angle_value)
    shifted = shift_reach * jnp.sin(radians + 2.0 * math.pi * row_global / rows_total)
    inside = jnp.arange(BLOCK).astype(jnp.float32) - 0.5 * (BLOCK - 1)
    centre = BLOCK + inside[None, :] * stretch + shifted[:, None]
    centre = jnp.concatenate([centre, centre], axis=1)
    places = jnp.arange(LANES).astype(jnp.float32)[:, None] + 0.5
    weights = (
        jnp.maximum(0.0, 1.0 - jnp.abs(places[None] - centre[:, None, :]) / spread) / spread
    )
    return weights.astype(jnp.bfloat16)


def backproject_kernel(shift_ref, columns_ref, mats_ref, out_ref, tiles_ref):
    p = pl.program_id(0)
    tile_count = out_ref.shape[2] // LANES
    depth_count = out_ref.shape[1]

    @pl.when(p == 0)
    def _():
        out_ref[...] = jnp.zeros_like(out_ref)
        tiles_ref[...] = jnp.zeros_like(tiles_ref)

    for step in range(PER_STEP):
        for tile in range(tile_count):
            tiles_ref[0, tile + 1] = columns_ref[step, :, tile * LANES:(tile + 1) * LANES].astype(
                jnp.float32
            )

        ends = jnp.concatenate([tiles_ref[0, 1], tiles_ref[0, tile_count]], axis=0).astype(jnp.bfloat16)
        second_half = lax.broadcasted_iota(jnp.int32, (LANES, LANES), 1) >= BLOCK
        empty = jnp.zeros((BLOCK, LANES), jnp.bfloat16)
        for row in range(out_ref.shape[0]):
            shift = shift_ref[p * PER_STEP + step, row, 2] - 2
            start = (shift + 2) // 2
            odd = jnp.full((LANES, LANES), shift - 2 * (start - 1), jnp.int32) == 1
            whole = mats_ref[step, row]
            down = jnp.concatenate([empty, whole[:BLOCK]], axis=0)
            up = jnp.concatenate([whole[BLOCK:], empty], axis=0)
            nothing = jnp.zeros_like(whole)
            first = jnp.where(
                second_half, jnp.where(odd, nothing, down), jnp.where(odd, down, whole)
            )
            second = jnp.where(
                second_half, jnp.where(odd, whole, up), jnp.where(odd, up, nothing)
            )
            low = tiles_ref[0, pl.ds(start, tile_count)].reshape(tile_count * depth_count, LANES)
            high = tiles_ref[0, pl.ds(start + 1, tile_count)].reshape(tile_count * depth_count, LANES)
            taps = jnp.concatenate([low, high], axis=1).astype(jnp.bfloat16)
            result = jnp.dot(
                taps, jnp.concatenate([first, second], axis=0), preferred_element_type=jnp.float32
            )
            edge = jnp.dot(ends, whole, preferred_element_type=jnp.float32)
            shift_vec = jnp.full((depth_count, LANES), shift, jnp.int32)
            for tile in range(tile_count):
                part = result[tile * depth_count:(tile + 1) * depth_count]
                if tile == 0:
                    part = jnp.where(shift_vec < 0, edge[:depth_count], part)
                elif tile == tile_count - 2:
                    part = jnp.where(shift_vec >= 2, edge[depth_count:], part)
                elif tile == tile_count - 1:
                    part = jnp.where(shift_vec >= 0, edge[depth_count:], part)
                lanes = pl.ds(tile * LANES, LANES)
                out_ref[row, :, lanes] = out_ref[row, :, lanes] + part

    @pl.when(p == pl.num_programs(0) - 1)
    def _():
        out_ref[...] = math.pi / P_SIZE * out_ref[...]


def backproject(shifts, columns, mats):
    count, rows = shifts.shape[0], shifts.shape[1]
    depth_count, column_count = columns.shape[1], columns.shape[2]
    tile_count = column_count // LANES
    return pl.pallas_call(
        backproject_kernel,
        out_shape=jax.ShapeDtypeStruct((rows, depth_count, column_count), jnp.float32),
        grid_spec=pltpu.PrefetchScalarGridSpec(
            num_scalar_prefetch=1,
            grid=(count // PER_STEP,),
            in_specs=[
                pl.BlockSpec((PER_STEP,) + columns.shape[1:], lambda p, s: (p, 0, 0)),
                pl.BlockSpec((PER_STEP,) + mats.shape[1:], lambda p, s: (p, 0, 0, 0)),
            ],
            out_specs=pl.BlockSpec((rows, depth_count, column_count), lambda p, s: (0, 0, 0)),
            scratch_shapes=[pltpu.VMEM((1, tile_count + 3, depth_count, LANES), jnp.float32)],
        ),
        compiler_params=pltpu.CompilerParams(dimension_semantics=("arbitrary",)),
    )(shifts, columns, mats)


def smooth_inner(current, fidelity, row_first, depth_first, rows_total, depth_total):
    row_index = row_first + jnp.arange(current.shape[0])
    depth_index = depth_first + jnp.arange(current.shape[1])
    keep_rows = ((row_index >= 0) & (row_index < rows_total - 1)).astype(jnp.float32)[:, None, None]
    keep_depth = ((depth_index >= 0) & (depth_index < depth_total - 1)).astype(jnp.float32)[
        None, :, None
    ]
    rows_here, rows_before = keep_rows[1:-1], keep_rows[:-2]
    depth_here, depth_before = keep_depth[:, 1:-1], keep_depth[:, :-2]

    def across(cells):
        return jnp.concatenate([cells[:, :, 1:] - cells[:, :, :-1], jnp.zeros_like(cells[:, :, :1])], 2)

    centre = current[1:-1, 1:-1]
    row_next, row_prev = current[2:, 1:-1], current[:-2, 1:-1]
    depth_next, depth_prev = current[1:-1, 2:], current[1:-1, :-2]
    prev_row_next_depth = current[:-2, 2:]
    next_row_prev_depth = current[2:, :-2]

    def inverse(a, b, c):
        return lax.rsqrt(a * a + b * b + c * c + gradient_floor)

    rows_d = (row_next - centre) * rows_here
    depth_d = (depth_next - centre) * depth_here
    width_d = across(centre)
    scale = inverse(rows_d, depth_d, width_d)
    prev_rows_d = (centre - row_prev) * rows_before
    prev_scale = inverse(prev_rows_d, (prev_row_next_depth - row_prev) * depth_here, across(row_prev))
    prev_depth_d = (centre - depth_prev) * depth_before
    low_scale = inverse(
        (next_row_prev_depth - depth_prev) * rows_here, prev_depth_d, across(depth_prev)
    )
    width_n = width_d * scale
    divergence = rows_d * scale - prev_rows_d * prev_scale
    divergence = divergence + depth_d * scale - prev_depth_d * low_scale
    divergence = divergence + width_n - jnp.concatenate(
        [jnp.zeros_like(width_n[:, :, :1]), width_n[:, :, :-1]], 2
    )
    return centre + step_length * (smooth_weight * divergence - (centre - fidelity[1:-1, 1:-1]))


def per_device(filtered, angle_index, band_offset, band_length, foot_block):
    depth_count = filtered.shape[1]
    row_count = foot_block.shape[1]
    extended_band = with_halo(filtered, (("gz", 1),), depth_count // 2)
    axial_weights = axial_table(band_offset[:, 0], band_length[:, 0], depth_count)
    summed_rows = jnp.einsum(
        "pzv,pvu->pzu",
        axial_weights,
        extended_band,
        preferred_element_type=jnp.float32,
    )
    columns = gather_columns(summed_rows.astype(jnp.bfloat16))
    column_count = columns.shape[2]
    row_base = lax.axis_index("gy") * row_count
    depth_base = lax.axis_index("gz") * depth_count
    rows_total = lax.axis_size("gy") * row_count
    depth_total = lax.axis_size("gz") * depth_count
    row_global = (row_base + jnp.arange(row_count)).astype(jnp.float32)
    mats = jax.vmap(footprint_mats, in_axes=(0, None, None))(angle_index, row_global, rows_total)
    backprojection = backproject(foot_block, columns, mats)
    current = backprojection
    extended = with_wide_halo(backprojection, ITERS)
    fidelity = extended
    current = extended
    for turn_index in range(ITERS):
        reach = ITERS - turn_index
        current = smooth_inner(
            current, fidelity, row_base - reach, depth_base - reach, rows_total, depth_total
        )
        fidelity = fidelity[1:-1, 1:-1]
    return current


def solution(mesh):
    return jax.shard_map(
        per_device,
        mesh=mesh,
        in_specs=(P(None, "gz", "gy"), P(), P(None, "gz"), P(None, "gz"), P(None, "gy", None)),
        out_specs=P("gy", "gz", None),
        check_vma=False,
    )
```

```python
import functools
import math

import jax
import jax.numpy as jnp
from jax import lax
from jax.experimental import pallas as pl
from jax.experimental.pallas import tpu as pltpu
from jax.sharding import PartitionSpec as P

X = 4096
P_SIZE = 16
NANG = 3600
BLOCK = 64
LANES = 128
GATHER_CHUNKS = 2
PER_STEP = 4
ITERS = 2


step_length = 0.25
smooth_weight = 0.3
gradient_floor = 0.01
shift_reach = 8.0


def with_halo(cells, sides, width):
    for axis, dim in sides:
        count = lax.axis_size(axis)
        ends = count - 1
        head = lax.slice_in_dim(cells, 0, width, axis=dim)
        tail = lax.slice_in_dim(cells, cells.shape[dim] - width, cells.shape[dim], axis=dim)
        cells = jnp.concatenate(
            [
                lax.ppermute(tail, axis, [(i, (i + 1) % count) for i in range(ends)]),
                cells,
                lax.ppermute(head, axis, [((i + 1) % count, i) for i in range(ends)]),
            ],
            axis=dim,
        )
    return cells


def gather_kernel(count, local_ref, out_ref, send_sem, recv_sem, own_sem):
    ring = count // 2
    forward_steps = ring // 2
    backward_steps = ring - 1 - forward_steps
    me = lax.axis_index("gy")
    depth_index = lax.axis_index("gz")
    half = me // ring
    place = me % ring
    width = local_ref.shape[2]
    mesh_kind = pl.DeviceIdType.MESH

    def device(half_of, place_of):
        return half_of * ring + lax.rem(place_of + 2 * ring, ring)

    partner = device(1 - half, place)
    right = device(half, place + 1)
    left = device(half, place - 1)

    chunks = GATHER_CHUNKS
    chunk_rows = local_ref.shape[0] // chunks

    def rows_of(chunk):
        return pl.ds(chunk * chunk_rows, chunk_rows)

    def slot(index, chunk):
        columns = pl.ds(pl.multiple_of(index * width, width), width)
        return out_ref.at[rows_of(chunk), :, columns]

    barrier = pltpu.get_barrier_semaphore()
    for peer in (partner, right, left):
        pl.semaphore_signal(barrier, inc=1, device_id=(depth_index, peer), device_id_type=mesh_kind)
    pl.semaphore_wait(barrier, 3)

    own = pltpu.make_async_copy(local_ref, out_ref.at[:, :, pl.ds(pl.multiple_of(me * width, width), width)], own_sem)
    own.start()
    sends = []

    def send(source, index, chunk, peer):
        copy = pltpu.make_async_remote_copy(
            src_ref=source,
            dst_ref=slot(index, chunk),
            send_sem=send_sem.at[len(sends)],
            recv_sem=recv_sem.at[index, chunk],
            device_id=(depth_index, peer),
            device_id_type=mesh_kind,
        )
        copy.start()
        sends.append(copy)

    def arrived(index, chunk):
        pltpu.make_async_remote_copy(
            src_ref=local_ref.at[rows_of(chunk)],
            dst_ref=slot(index, chunk),
            send_sem=send_sem.at[0],
            recv_sem=recv_sem.at[index, chunk],
            device_id=(depth_index, partner),
            device_id_type=mesh_kind,
        ).wait_recv()

    for chunk in range(chunks):
        send(local_ref.at[rows_of(chunk)], me, chunk, partner)
    for step in range(1, forward_steps + 1):
        for chunk in range(chunks):
            for direction, peer, limit in ((-1, right, forward_steps), (1, left, backward_steps)):
                if step > limit:
                    continue
                if step == 1:
                    send(local_ref.at[rows_of(chunk)], me, chunk, peer)
                    if direction == -1:
                        arrived(partner, chunk)
                    send(slot(partner, chunk), partner, chunk, peer)
                    continue
                for half_of in (0, 1):
                    index = device(half_of, place + direction * (step - 1))
                    arrived(index, chunk)
                    send(slot(index, chunk), index, chunk, peer)
    for direction, steps in ((-1, forward_steps), (1, backward_steps)):
        for half_of in (0, 1):
            for chunk in range(chunks):
                arrived(device(half_of, place + direction * steps), chunk)
    own.wait()
    for copy in sends:
        copy.wait_send()


def gather_columns(local):
    count = lax.axis_size("gy")
    rows, depth, width = local.shape
    return pl.pallas_call(
        functools.partial(gather_kernel, count),
        out_shape=jax.ShapeDtypeStruct((rows, depth, width * count), local.dtype),
        in_specs=[pl.BlockSpec(memory_space=pl.ANY)],
        out_specs=pl.BlockSpec(memory_space=pl.ANY),
        scratch_shapes=[
            pltpu.SemaphoreType.DMA((count * GATHER_CHUNKS,)),
            pltpu.SemaphoreType.DMA((count, GATHER_CHUNKS)),
            pltpu.SemaphoreType.DMA(()),
        ],
        compiler_params=pltpu.CompilerParams(collective_id=0, has_side_effects=True),
    )(local)


STEPS = ((1, 1), (1, 0), (1, -1), (0, 1), (0, -1), (-1, 1), (-1, 0), (-1, -1))


def halo_kernel(count, width, cells_ref, *refs):
    pieces = len(STEPS)
    targets = refs[:pieces]
    send_sem, recv_sem = refs[pieces], refs[pieces + 1]
    row_count, depth_count = count
    rows, depth = cells_ref.shape[0], cells_ref.shape[1]
    row_parts = {1: pl.ds(rows - width, width), 0: pl.ds(0, rows), -1: pl.ds(0, width)}
    depth_parts = {1: pl.ds(depth - width, width), 0: pl.ds(0, depth), -1: pl.ds(0, width)}
    row_me = lax.axis_index("gy")
    depth_me = lax.axis_index("gz")
    peers = [
        (lax.rem(depth_me + depth_step + depth_count, depth_count),
         lax.rem(row_me + row_step + row_count, row_count))
        for row_step, depth_step in STEPS
    ]
    barrier = pltpu.get_barrier_semaphore()
    for peer in peers:
        pl.semaphore_signal(barrier, inc=1, device_id=peer, device_id_type=pl.DeviceIdType.MESH)
    pl.semaphore_wait(barrier, pieces)
    copies = []
    for k, peer in enumerate(peers):
        row_step, depth_step = STEPS[k]
        copy = pltpu.make_async_remote_copy(
            src_ref=cells_ref.at[row_parts[row_step], depth_parts[depth_step]],
            dst_ref=targets[k],
            send_sem=send_sem.at[k],
            recv_sem=recv_sem.at[k],
            device_id=peer,
            device_id_type=pl.DeviceIdType.MESH,
        )
        copy.start()
        copies.append(copy)
    for copy in copies:
        copy.wait()


def with_wide_halo(cells, width):
    rows, depth = cells.shape[0], cells.shape[1]
    count = (lax.axis_size("gy"), lax.axis_size("gz"))
    row_parts = {1: slice(rows - width, rows), 0: slice(None), -1: slice(0, width)}
    depth_parts = {1: slice(depth - width, depth), 0: slice(None), -1: slice(0, width)}
    sent = [cells[row_parts[r], depth_parts[d]] for r, d in STEPS]
    received = pl.pallas_call(
        functools.partial(halo_kernel, count, width),
        out_shape=[jax.ShapeDtypeStruct(piece.shape, piece.dtype) for piece in sent],
        in_specs=[pl.BlockSpec(memory_space=pl.ANY)],
        out_specs=[pl.BlockSpec(memory_space=pl.ANY)] * len(STEPS),
        scratch_shapes=[
            pltpu.SemaphoreType.DMA((len(STEPS),)),
            pltpu.SemaphoreType.DMA((len(STEPS),)),
        ],
        compiler_params=pltpu.CompilerParams(collective_id=1, has_side_effects=True),
    )(cells)
    parts = dict(zip(STEPS, received))
    parts[(0, 0)] = cells
    bands = [
        jnp.concatenate([parts[(r, 1)], parts[(r, 0)], parts[(r, -1)]], axis=1) for r in (1, 0, -1)
    ]
    return jnp.concatenate(bands, axis=0)


def geometry(angle_value):
    radians = 2.0 * math.pi * angle_value.astype(jnp.float32) / NANG
    stretch = 0.5 + 0.5 * jnp.abs(jnp.cos(radians))
    spread = 1.0 + jnp.abs(jnp.sin(radians))
    return (radians, stretch, spread)


def footprint(radians, stretch, spread, row_global, rows_total, block_size):
    shifted = shift_reach * jnp.sin(radians + 2.0 * math.pi * row_global / rows_total)
    inside = jnp.arange(block_size).astype(jnp.float32) - 0.5 * (block_size - 1)
    centre = block_size + inside[None, :] * stretch + shifted[:, None]
    places = jnp.arange(2 * block_size).astype(jnp.float32) + 0.5
    weights = (
        jnp.maximum(0.0, 1.0 - jnp.abs(places[None, None, :] - centre[:, :, None]) / spread)
        / spread
    )
    return weights.astype(jnp.bfloat16)


def axial_table(offsets, lengths, depth_count):
    offset_real = offsets.astype(jnp.float32)[..., None]
    length_real = lengths.astype(jnp.float32)[..., None]
    depth_place = jnp.arange(depth_count).astype(jnp.float32) + 0.5
    centre = offset_real + depth_place * length_real / depth_count
    row_number = jnp.arange(2 * depth_count)
    row_place = row_number.astype(jnp.float32) + 0.5
    triangle = jnp.maximum(0.0, 1.0 - jnp.abs(row_place - centre[..., None]))
    inside = (row_number >= offsets[..., None, None]) & (
        row_number < (offsets + lengths)[..., None, None]
    )
    return jnp.where(inside, triangle, 0.0).astype(jnp.bfloat16)


def smooth_update(current, fidelity, row_first, depth_first, rows_total, depth_total):
    row_index = row_first + jnp.arange(current.shape[0])
    depth_index = depth_first + jnp.arange(current.shape[1])
    keep_rows = ((row_index >= 0) & (row_index < rows_total - 1)).astype(jnp.float32)[:, None, None]
    keep_depth = ((depth_index >= 0) & (depth_index < depth_total - 1)).astype(jnp.float32)[
        None, :, None
    ]
    forward_rows = (
        jnp.concatenate([current[1:] - current[:-1], jnp.zeros_like(current[:1])], 0) * keep_rows
    )
    forward_depth = (
        jnp.concatenate([current[:, 1:] - current[:, :-1], jnp.zeros_like(current[:, :1])], 1)
        * keep_depth
    )
    forward_width = jnp.concatenate(
        [current[:, :, 1:] - current[:, :, :-1], jnp.zeros_like(current[:, :, :1])], 2
    )
    inverse = lax.rsqrt(
        forward_rows * forward_rows
        + forward_depth * forward_depth
        + forward_width * forward_width
        + gradient_floor
    )
    normal_rows = forward_rows * inverse
    normal_depth = forward_depth * inverse
    normal_width = forward_width * inverse
    divergence = normal_rows - jnp.concatenate(
        [jnp.zeros_like(normal_rows[:1]), normal_rows[:-1]], 0
    )
    divergence = (
        divergence
        + normal_depth
        - jnp.concatenate([jnp.zeros_like(normal_depth[:, :1]), normal_depth[:, :-1]], 1)
    )
    divergence = (
        divergence
        + normal_width
        - jnp.concatenate([jnp.zeros_like(normal_width[:, :, :1]), normal_width[:, :, :-1]], 2)
    )
    return current + step_length * (smooth_weight * divergence - (current - fidelity))


def footprint_mats(angle_value, row_global, rows_total):
    radians, stretch, spread = geometry(angle_value)
    shifted = shift_reach * jnp.sin(radians + 2.0 * math.pi * row_global / rows_total)
    inside = jnp.arange(BLOCK).astype(jnp.float32) - 0.5 * (BLOCK - 1)
    centre = BLOCK + inside[None, :] * stretch + shifted[:, None]
    centre = jnp.concatenate([centre, centre], axis=1)
    places = jnp.arange(LANES).astype(jnp.float32)[:, None] + 0.5
    weights = (
        jnp.maximum(0.0, 1.0 - jnp.abs(places[None] - centre[:, None, :]) / spread) / spread
    )
    return weights.astype(jnp.bfloat16)


def backproject_kernel(shift_ref, columns_ref, mats_ref, out_ref, tiles_ref):
    p = pl.program_id(0)
    tile_count = out_ref.shape[2] // LANES
    depth_count = out_ref.shape[1]

    @pl.when(p == 0)
    def _():
        out_ref[...] = jnp.zeros_like(out_ref)
        tiles_ref[...] = jnp.zeros_like(tiles_ref)

    for step in range(PER_STEP):
        for tile in range(tile_count):
            tiles_ref[0, tile + 1] = columns_ref[step, :, tile * LANES:(tile + 1) * LANES].astype(
                jnp.float32
            )

        ends = jnp.concatenate([tiles_ref[0, 1], tiles_ref[0, tile_count]], axis=0).astype(jnp.bfloat16)
        second_half = lax.broadcasted_iota(jnp.int32, (LANES, LANES), 1) >= BLOCK
        empty = jnp.zeros((BLOCK, LANES), jnp.bfloat16)
        for row in range(out_ref.shape[0]):
            shift = shift_ref[p * PER_STEP + step, row, 2] - 2
            start = (shift + 2) // 2
            odd = jnp.full((LANES, LANES), shift - 2 * (start - 1), jnp.int32) == 1
            whole = mats_ref[step, row]
            down = jnp.concatenate([empty, whole[:BLOCK]], axis=0)
            up = jnp.concatenate([whole[BLOCK:], empty], axis=0)
            nothing = jnp.zeros_like(whole)
            first = jnp.where(
                second_half, jnp.where(odd, nothing, down), jnp.where(odd, down, whole)
            )
            second = jnp.where(
                second_half, jnp.where(odd, whole, up), jnp.where(odd, up, nothing)
            )
            low = tiles_ref[0, pl.ds(start, tile_count)].reshape(tile_count * depth_count, LANES)
            high = tiles_ref[0, pl.ds(start + 1, tile_count)].reshape(tile_count * depth_count, LANES)
            taps = jnp.concatenate([low, high], axis=1).astype(jnp.bfloat16)
            result = jnp.dot(
                taps, jnp.concatenate([first, second], axis=0), preferred_element_type=jnp.float32
            )
            edge = jnp.dot(ends, whole, preferred_element_type=jnp.float32)
            shift_vec = jnp.full((depth_count, LANES), shift, jnp.int32)
            for tile in range(tile_count):
                part = result[tile * depth_count:(tile + 1) * depth_count]
                if tile == 0:
                    part = jnp.where(shift_vec < 0, edge[:depth_count], part)
                elif tile == tile_count - 2:
                    part = jnp.where(shift_vec >= 2, edge[depth_count:], part)
                elif tile == tile_count - 1:
                    part = jnp.where(shift_vec >= 0, edge[depth_count:], part)
                lanes = pl.ds(tile * LANES, LANES)
                out_ref[row, :, lanes] = out_ref[row, :, lanes] + part

    @pl.when(p == pl.num_programs(0) - 1)
    def _():
        out_ref[...] = math.pi / P_SIZE * out_ref[...]


def backproject(shifts, columns, mats):
    count, rows = shifts.shape[0], shifts.shape[1]
    depth_count, column_count = columns.shape[1], columns.shape[2]
    tile_count = column_count // LANES
    return pl.pallas_call(
        backproject_kernel,
        out_shape=jax.ShapeDtypeStruct((rows, depth_count, column_count), jnp.float32),
        grid_spec=pltpu.PrefetchScalarGridSpec(
            num_scalar_prefetch=1,
            grid=(count // PER_STEP,),
            in_specs=[
                pl.BlockSpec((PER_STEP,) + columns.shape[1:], lambda p, s: (p, 0, 0)),
                pl.BlockSpec((PER_STEP,) + mats.shape[1:], lambda p, s: (p, 0, 0, 0)),
            ],
            out_specs=pl.BlockSpec((rows, depth_count, column_count), lambda p, s: (0, 0, 0)),
            scratch_shapes=[pltpu.VMEM((1, tile_count + 3, depth_count, LANES), jnp.float32)],
        ),
        compiler_params=pltpu.CompilerParams(dimension_semantics=("arbitrary",)),
    )(shifts, columns, mats)


def smooth_inner(current, fidelity, row_first, depth_first, rows_total, depth_total):
    row_index = row_first + jnp.arange(current.shape[0])
    depth_index = depth_first + jnp.arange(current.shape[1])
    keep_rows = ((row_index >= 0) & (row_index < rows_total - 1)).astype(jnp.float32)[:, None, None]
    keep_depth = ((depth_index >= 0) & (depth_index < depth_total - 1)).astype(jnp.float32)[
        None, :, None
    ]
    rows_here, rows_before = keep_rows[1:-1], keep_rows[:-2]
    depth_here, depth_before = keep_depth[:, 1:-1], keep_depth[:, :-2]

    def across(cells):
        return jnp.concatenate([cells[:, :, 1:] - cells[:, :, :-1], jnp.zeros_like(cells[:, :, :1])], 2)

    centre = current[1:-1, 1:-1]
    row_next, row_prev = current[2:, 1:-1], current[:-2, 1:-1]
    depth_next, depth_prev = current[1:-1, 2:], current[1:-1, :-2]
    prev_row_next_depth = current[:-2, 2:]
    next_row_prev_depth = current[2:, :-2]

    def inverse(a, b, c):
        return lax.rsqrt(a * a + b * b + c * c + gradient_floor)

    rows_d = (row_next - centre) * rows_here
    depth_d = (depth_next - centre) * depth_here
    width_d = across(centre)
    scale = inverse(rows_d, depth_d, width_d)
    prev_rows_d = (centre - row_prev) * rows_before
    prev_scale = inverse(prev_rows_d, (prev_row_next_depth - row_prev) * depth_here, across(row_prev))
    prev_depth_d = (centre - depth_prev) * depth_before
    low_scale = inverse(
        (next_row_prev_depth - depth_prev) * rows_here, prev_depth_d, across(depth_prev)
    )
    width_n = width_d * scale
    divergence = rows_d * scale - prev_rows_d * prev_scale
    divergence = divergence + depth_d * scale - prev_depth_d * low_scale
    divergence = divergence + width_n - jnp.concatenate(
        [jnp.zeros_like(width_n[:, :, :1]), width_n[:, :, :-1]], 2
    )
    return centre + step_length * (smooth_weight * divergence - (centre - fidelity[1:-1, 1:-1]))


def per_device(filtered, angle_index, band_offset, band_length, foot_block):
    depth_count = filtered.shape[1]
    row_count = foot_block.shape[1]
    extended_band = with_halo(filtered, (("gz", 1),), depth_count // 2)
    axial_weights = axial_table(band_offset[:, 0], band_length[:, 0], depth_count)
    summed_rows = jnp.einsum(
        "pzv,pvu->pzu",
        axial_weights,
        extended_band,
        preferred_element_type=jnp.float32,
    )
    columns = gather_columns(summed_rows.astype(jnp.bfloat16))
    column_count = columns.shape[2]
    row_base = lax.axis_index("gy") * row_count
    depth_base = lax.axis_index("gz") * depth_count
    rows_total = lax.axis_size("gy") * row_count
    depth_total = lax.axis_size("gz") * depth_count
    row_global = (row_base + jnp.arange(row_count)).astype(jnp.float32)
    mats = jax.vmap(footprint_mats, in_axes=(0, None, None))(angle_index, row_global, rows_total)
    backprojection = backproject(foot_block, columns, mats)
    current = backprojection
    extended = with_wide_halo(backprojection, ITERS)
    fidelity = extended
    current = extended
    for turn_index in range(ITERS):
        reach = ITERS - turn_index
        current = smooth_inner(
            current, fidelity, row_base - reach, depth_base - reach, rows_total, depth_total
        )
        fidelity = fidelity[1:-1, 1:-1]
    return current


def solution(mesh):
    return jax.shard_map(
        per_device,
        mesh=mesh,
        in_specs=(P(None, "gz", "gy"), P(), P(None, "gz"), P(None, "gz"), P(None, "gy", None)),
        out_specs=P("gy", "gz", None),
        check_vma=False,
    )
```

```python
import functools
import math

import jax
import jax.numpy as jnp
from jax import lax
from jax.experimental import pallas as pl
from jax.experimental.pallas import tpu as pltpu
from jax.sharding import PartitionSpec as P

X = 4096
P_SIZE = 16
NANG = 3600
BLOCK = 64
LANES = 128
GATHER_CHUNKS = 2
PER_STEP = 8
ITERS = 2


step_length = 0.25
smooth_weight = 0.3
gradient_floor = 0.01
shift_reach = 8.0


def with_halo(cells, sides, width):
    for axis, dim in sides:
        count = lax.axis_size(axis)
        ends = count - 1
        head = lax.slice_in_dim(cells, 0, width, axis=dim)
        tail = lax.slice_in_dim(cells, cells.shape[dim] - width, cells.shape[dim], axis=dim)
        cells = jnp.concatenate(
            [
                lax.ppermute(tail, axis, [(i, (i + 1) % count) for i in range(ends)]),
                cells,
                lax.ppermute(head, axis, [((i + 1) % count, i) for i in range(ends)]),
            ],
            axis=dim,
        )
    return cells


def gather_kernel(count, local_ref, out_ref, send_sem, recv_sem, own_sem):
    ring = count // 2
    forward_steps = ring // 2
    backward_steps = ring - 1 - forward_steps
    me = lax.axis_index("gy")
    depth_index = lax.axis_index("gz")
    half = me // ring
    place = me % ring
    width = local_ref.shape[2]
    mesh_kind = pl.DeviceIdType.MESH

    def device(half_of, place_of):
        return half_of * ring + lax.rem(place_of + 2 * ring, ring)

    partner = device(1 - half, place)
    right = device(half, place + 1)
    left = device(half, place - 1)

    chunks = GATHER_CHUNKS
    chunk_rows = local_ref.shape[0] // chunks

    def rows_of(chunk):
        return pl.ds(chunk * chunk_rows, chunk_rows)

    def slot(index, chunk):
        columns = pl.ds(pl.multiple_of(index * width, width), width)
        return out_ref.at[rows_of(chunk), :, columns]

    barrier = pltpu.get_barrier_semaphore()
    for peer in (partner, right, left):
        pl.semaphore_signal(barrier, inc=1, device_id=(depth_index, peer), device_id_type=mesh_kind)
    pl.semaphore_wait(barrier, 3)

    own = pltpu.make_async_copy(local_ref, out_ref.at[:, :, pl.ds(pl.multiple_of(me * width, width), width)], own_sem)
    own.start()
    sends = []

    def send(source, index, chunk, peer):
        copy = pltpu.make_async_remote_copy(
            src_ref=source,
            dst_ref=slot(index, chunk),
            send_sem=send_sem.at[len(sends)],
            recv_sem=recv_sem.at[index, chunk],
            device_id=(depth_index, peer),
            device_id_type=mesh_kind,
        )
        copy.start()
        sends.append(copy)

    def arrived(index, chunk):
        pltpu.make_async_remote_copy(
            src_ref=local_ref.at[rows_of(chunk)],
            dst_ref=slot(index, chunk),
            send_sem=send_sem.at[0],
            recv_sem=recv_sem.at[index, chunk],
            device_id=(depth_index, partner),
            device_id_type=mesh_kind,
        ).wait_recv()

    for chunk in range(chunks):
        send(local_ref.at[rows_of(chunk)], me, chunk, partner)
    for step in range(1, forward_steps + 1):
        for chunk in range(chunks):
            for direction, peer, limit in ((-1, right, forward_steps), (1, left, backward_steps)):
                if step > limit:
                    continue
                if step == 1:
                    send(local_ref.at[rows_of(chunk)], me, chunk, peer)
                    if direction == -1:
                        arrived(partner, chunk)
                    send(slot(partner, chunk), partner, chunk, peer)
                    continue
                for half_of in (0, 1):
                    index = device(half_of, place + direction * (step - 1))
                    arrived(index, chunk)
                    send(slot(index, chunk), index, chunk, peer)
    for direction, steps in ((-1, forward_steps), (1, backward_steps)):
        for half_of in (0, 1):
            for chunk in range(chunks):
                arrived(device(half_of, place + direction * steps), chunk)
    own.wait()
    for copy in sends:
        copy.wait_send()


def gather_columns(local):
    count = lax.axis_size("gy")
    rows, depth, width = local.shape
    return pl.pallas_call(
        functools.partial(gather_kernel, count),
        out_shape=jax.ShapeDtypeStruct((rows, depth, width * count), local.dtype),
        in_specs=[pl.BlockSpec(memory_space=pl.ANY)],
        out_specs=pl.BlockSpec(memory_space=pl.ANY),
        scratch_shapes=[
            pltpu.SemaphoreType.DMA((count * GATHER_CHUNKS,)),
            pltpu.SemaphoreType.DMA((count, GATHER_CHUNKS)),
            pltpu.SemaphoreType.DMA(()),
        ],
        compiler_params=pltpu.CompilerParams(collective_id=0, has_side_effects=True),
    )(local)


STEPS = ((1, 1), (1, 0), (1, -1), (0, 1), (0, -1), (-1, 1), (-1, 0), (-1, -1))


def halo_kernel(count, width, cells_ref, *refs):
    pieces = len(STEPS)
    targets = refs[:pieces]
    send_sem, recv_sem = refs[pieces], refs[pieces + 1]
    row_count, depth_count = count
    rows, depth = cells_ref.shape[0], cells_ref.shape[1]
    row_parts = {1: pl.ds(rows - width, width), 0: pl.ds(0, rows), -1: pl.ds(0, width)}
    depth_parts = {1: pl.ds(depth - width, width), 0: pl.ds(0, depth), -1: pl.ds(0, width)}
    row_me = lax.axis_index("gy")
    depth_me = lax.axis_index("gz")
    peers = [
        (lax.rem(depth_me + depth_step + depth_count, depth_count),
         lax.rem(row_me + row_step + row_count, row_count))
        for row_step, depth_step in STEPS
    ]
    barrier = pltpu.get_barrier_semaphore()
    for peer in peers:
        pl.semaphore_signal(barrier, inc=1, device_id=peer, device_id_type=pl.DeviceIdType.MESH)
    pl.semaphore_wait(barrier, pieces)
    copies = []
    for k, peer in enumerate(peers):
        row_step, depth_step = STEPS[k]
        copy = pltpu.make_async_remote_copy(
            src_ref=cells_ref.at[row_parts[row_step], depth_parts[depth_step]],
            dst_ref=targets[k],
            send_sem=send_sem.at[k],
            recv_sem=recv_sem.at[k],
            device_id=peer,
            device_id_type=pl.DeviceIdType.MESH,
        )
        copy.start()
        copies.append(copy)
    for copy in copies:
        copy.wait()


def with_wide_halo(cells, width):
    rows, depth = cells.shape[0], cells.shape[1]
    count = (lax.axis_size("gy"), lax.axis_size("gz"))
    row_parts = {1: slice(rows - width, rows), 0: slice(None), -1: slice(0, width)}
    depth_parts = {1: slice(depth - width, depth), 0: slice(None), -1: slice(0, width)}
    sent = [cells[row_parts[r], depth_parts[d]] for r, d in STEPS]
    received = pl.pallas_call(
        functools.partial(halo_kernel, count, width),
        out_shape=[jax.ShapeDtypeStruct(piece.shape, piece.dtype) for piece in sent],
        in_specs=[pl.BlockSpec(memory_space=pl.ANY)],
        out_specs=[pl.BlockSpec(memory_space=pl.ANY)] * len(STEPS),
        scratch_shapes=[
            pltpu.SemaphoreType.DMA((len(STEPS),)),
            pltpu.SemaphoreType.DMA((len(STEPS),)),
        ],
        compiler_params=pltpu.CompilerParams(collective_id=1, has_side_effects=True),
    )(cells)
    parts = dict(zip(STEPS, received))
    parts[(0, 0)] = cells
    bands = [
        jnp.concatenate([parts[(r, 1)], parts[(r, 0)], parts[(r, -1)]], axis=1) for r in (1, 0, -1)
    ]
    return jnp.concatenate(bands, axis=0)


def geometry(angle_value):
    radians = 2.0 * math.pi * angle_value.astype(jnp.float32) / NANG
    stretch = 0.5 + 0.5 * jnp.abs(jnp.cos(radians))
    spread = 1.0 + jnp.abs(jnp.sin(radians))
    return (radians, stretch, spread)


def footprint(radians, stretch, spread, row_global, rows_total, block_size):
    shifted = shift_reach * jnp.sin(radians + 2.0 * math.pi * row_global / rows_total)
    inside = jnp.arange(block_size).astype(jnp.float32) - 0.5 * (block_size - 1)
    centre = block_size + inside[None, :] * stretch + shifted[:, None]
    places = jnp.arange(2 * block_size).astype(jnp.float32) + 0.5
    weights = (
        jnp.maximum(0.0, 1.0 - jnp.abs(places[None, None, :] - centre[:, :, None]) / spread)
        / spread
    )
    return weights.astype(jnp.bfloat16)


def axial_table(offsets, lengths, depth_count):
    offset_real = offsets.astype(jnp.float32)[..., None]
    length_real = lengths.astype(jnp.float32)[..., None]
    depth_place = jnp.arange(depth_count).astype(jnp.float32) + 0.5
    centre = offset_real + depth_place * length_real / depth_count
    row_number = jnp.arange(2 * depth_count)
    row_place = row_number.astype(jnp.float32) + 0.5
    triangle = jnp.maximum(0.0, 1.0 - jnp.abs(row_place - centre[..., None]))
    inside = (row_number >= offsets[..., None, None]) & (
        row_number < (offsets + lengths)[..., None, None]
    )
    return jnp.where(inside, triangle, 0.0).astype(jnp.bfloat16)


def smooth_update(current, fidelity, row_first, depth_first, rows_total, depth_total):
    row_index = row_first + jnp.arange(current.shape[0])
    depth_index = depth_first + jnp.arange(current.shape[1])
    keep_rows = ((row_index >= 0) & (row_index < rows_total - 1)).astype(jnp.float32)[:, None, None]
    keep_depth = ((depth_index >= 0) & (depth_index < depth_total - 1)).astype(jnp.float32)[
        None, :, None
    ]
    forward_rows = (
        jnp.concatenate([current[1:] - current[:-1], jnp.zeros_like(current[:1])], 0) * keep_rows
    )
    forward_depth = (
        jnp.concatenate([current[:, 1:] - current[:, :-1], jnp.zeros_like(current[:, :1])], 1)
        * keep_depth
    )
    forward_width = jnp.concatenate(
        [current[:, :, 1:] - current[:, :, :-1], jnp.zeros_like(current[:, :, :1])], 2
    )
    inverse = lax.rsqrt(
        forward_rows * forward_rows
        + forward_depth * forward_depth
        + forward_width * forward_width
        + gradient_floor
    )
    normal_rows = forward_rows * inverse
    normal_depth = forward_depth * inverse
    normal_width = forward_width * inverse
    divergence = normal_rows - jnp.concatenate(
        [jnp.zeros_like(normal_rows[:1]), normal_rows[:-1]], 0
    )
    divergence = (
        divergence
        + normal_depth
        - jnp.concatenate([jnp.zeros_like(normal_depth[:, :1]), normal_depth[:, :-1]], 1)
    )
    divergence = (
        divergence
        + normal_width
        - jnp.concatenate([jnp.zeros_like(normal_width[:, :, :1]), normal_width[:, :, :-1]], 2)
    )
    return current + step_length * (smooth_weight * divergence - (current - fidelity))


def footprint_mats(angle_value, row_global, rows_total):
    radians, stretch, spread = geometry(angle_value)
    shifted = shift_reach * jnp.sin(radians + 2.0 * math.pi * row_global / rows_total)
    inside = jnp.arange(BLOCK).astype(jnp.float32) - 0.5 * (BLOCK - 1)
    centre = BLOCK + inside[None, :] * stretch + shifted[:, None]
    centre = jnp.concatenate([centre, centre], axis=1)
    places = jnp.arange(LANES).astype(jnp.float32)[:, None] + 0.5
    weights = (
        jnp.maximum(0.0, 1.0 - jnp.abs(places[None] - centre[:, None, :]) / spread) / spread
    )
    return weights.astype(jnp.bfloat16)


def backproject_kernel(shift_ref, columns_ref, mats_ref, out_ref, tiles_ref):
    p = pl.program_id(0)
    tile_count = out_ref.shape[2] // LANES
    depth_count = out_ref.shape[1]

    @pl.when(p == 0)
    def _():
        out_ref[...] = jnp.zeros_like(out_ref)
        tiles_ref[...] = jnp.zeros_like(tiles_ref)

    for step in range(PER_STEP):
        for tile in range(tile_count):
            tiles_ref[0, tile + 1] = columns_ref[step, :, tile * LANES:(tile + 1) * LANES].astype(
                jnp.float32
            )

        ends = jnp.concatenate([tiles_ref[0, 1], tiles_ref[0, tile_count]], axis=0).astype(jnp.bfloat16)
        second_half = lax.broadcasted_iota(jnp.int32, (LANES, LANES), 1) >= BLOCK
        empty = jnp.zeros((BLOCK, LANES), jnp.bfloat16)
        for row in range(out_ref.shape[0]):
            shift = shift_ref[p * PER_STEP + step, row, 2] - 2
            start = (shift + 2) // 2
            odd = jnp.full((LANES, LANES), shift - 2 * (start - 1), jnp.int32) == 1
            whole = mats_ref[step, row]
            down = jnp.concatenate([empty, whole[:BLOCK]], axis=0)
            up = jnp.concatenate([whole[BLOCK:], empty], axis=0)
            nothing = jnp.zeros_like(whole)
            first = jnp.where(
                second_half, jnp.where(odd, nothing, down), jnp.where(odd, down, whole)
            )
            second = jnp.where(
                second_half, jnp.where(odd, whole, up), jnp.where(odd, up, nothing)
            )
            low = tiles_ref[0, pl.ds(start, tile_count)].reshape(tile_count * depth_count, LANES)
            high = tiles_ref[0, pl.ds(start + 1, tile_count)].reshape(tile_count * depth_count, LANES)
            taps = jnp.concatenate([low, high], axis=1).astype(jnp.bfloat16)
            result = jnp.dot(
                taps, jnp.concatenate([first, second], axis=0), preferred_element_type=jnp.float32
            )
            edge = jnp.dot(ends, whole, preferred_element_type=jnp.float32)
            shift_vec = jnp.full((depth_count, LANES), shift, jnp.int32)
            for tile in range(tile_count):
                part = result[tile * depth_count:(tile + 1) * depth_count]
                if tile == 0:
                    part = jnp.where(shift_vec < 0, edge[:depth_count], part)
                elif tile == tile_count - 2:
                    part = jnp.where(shift_vec >= 2, edge[depth_count:], part)
                elif tile == tile_count - 1:
                    part = jnp.where(shift_vec >= 0, edge[depth_count:], part)
                lanes = pl.ds(tile * LANES, LANES)
                out_ref[row, :, lanes] = out_ref[row, :, lanes] + part

    @pl.when(p == pl.num_programs(0) - 1)
    def _():
        out_ref[...] = math.pi / P_SIZE * out_ref[...]


def backproject(shifts, columns, mats):
    count, rows = shifts.shape[0], shifts.shape[1]
    depth_count, column_count = columns.shape[1], columns.shape[2]
    tile_count = column_count // LANES
    return pl.pallas_call(
        backproject_kernel,
        out_shape=jax.ShapeDtypeStruct((rows, depth_count, column_count), jnp.float32),
        grid_spec=pltpu.PrefetchScalarGridSpec(
            num_scalar_prefetch=1,
            grid=(count // PER_STEP,),
            in_specs=[
                pl.BlockSpec((PER_STEP,) + columns.shape[1:], lambda p, s: (p, 0, 0)),
                pl.BlockSpec((PER_STEP,) + mats.shape[1:], lambda p, s: (p, 0, 0, 0)),
            ],
            out_specs=pl.BlockSpec((rows, depth_count, column_count), lambda p, s: (0, 0, 0)),
            scratch_shapes=[pltpu.VMEM((1, tile_count + 3, depth_count, LANES), jnp.float32)],
        ),
        compiler_params=pltpu.CompilerParams(dimension_semantics=("arbitrary",)),
    )(shifts, columns, mats)


def smooth_inner(current, fidelity, row_first, depth_first, rows_total, depth_total):
    row_index = row_first + jnp.arange(current.shape[0])
    depth_index = depth_first + jnp.arange(current.shape[1])
    keep_rows = ((row_index >= 0) & (row_index < rows_total - 1)).astype(jnp.float32)[:, None, None]
    keep_depth = ((depth_index >= 0) & (depth_index < depth_total - 1)).astype(jnp.float32)[
        None, :, None
    ]
    rows_here, rows_before = keep_rows[1:-1], keep_rows[:-2]
    depth_here, depth_before = keep_depth[:, 1:-1], keep_depth[:, :-2]

    def across(cells):
        return jnp.concatenate([cells[:, :, 1:] - cells[:, :, :-1], jnp.zeros_like(cells[:, :, :1])], 2)

    centre = current[1:-1, 1:-1]
    row_next, row_prev = current[2:, 1:-1], current[:-2, 1:-1]
    depth_next, depth_prev = current[1:-1, 2:], current[1:-1, :-2]
    prev_row_next_depth = current[:-2, 2:]
    next_row_prev_depth = current[2:, :-2]

    def inverse(a, b, c):
        return lax.rsqrt(a * a + b * b + c * c + gradient_floor)

    rows_d = (row_next - centre) * rows_here
    depth_d = (depth_next - centre) * depth_here
    width_d = across(centre)
    scale = inverse(rows_d, depth_d, width_d)
    prev_rows_d = (centre - row_prev) * rows_before
    prev_scale = inverse(prev_rows_d, (prev_row_next_depth - row_prev) * depth_here, across(row_prev))
    prev_depth_d = (centre - depth_prev) * depth_before
    low_scale = inverse(
        (next_row_prev_depth - depth_prev) * rows_here, prev_depth_d, across(depth_prev)
    )
    width_n = width_d * scale
    divergence = rows_d * scale - prev_rows_d * prev_scale
    divergence = divergence + depth_d * scale - prev_depth_d * low_scale
    divergence = divergence + width_n - jnp.concatenate(
        [jnp.zeros_like(width_n[:, :, :1]), width_n[:, :, :-1]], 2
    )
    return centre + step_length * (smooth_weight * divergence - (centre - fidelity[1:-1, 1:-1]))


def per_device(filtered, angle_index, band_offset, band_length, foot_block):
    depth_count = filtered.shape[1]
    row_count = foot_block.shape[1]
    extended_band = with_halo(filtered, (("gz", 1),), depth_count // 2)
    axial_weights = axial_table(band_offset[:, 0], band_length[:, 0], depth_count)
    summed_rows = jnp.einsum(
        "pzv,pvu->pzu",
        axial_weights,
        extended_band,
        preferred_element_type=jnp.float32,
    )
    columns = gather_columns(summed_rows.astype(jnp.bfloat16))
    column_count = columns.shape[2]
    row_base = lax.axis_index("gy") * row_count
    depth_base = lax.axis_index("gz") * depth_count
    rows_total = lax.axis_size("gy") * row_count
    depth_total = lax.axis_size("gz") * depth_count
    row_global = (row_base + jnp.arange(row_count)).astype(jnp.float32)
    mats = jax.vmap(footprint_mats, in_axes=(0, None, None))(angle_index, row_global, rows_total)
    backprojection = backproject(foot_block, columns, mats)
    current = backprojection
    extended = with_wide_halo(backprojection, ITERS)
    fidelity = extended
    current = extended
    for turn_index in range(ITERS):
        reach = ITERS - turn_index
        current = smooth_inner(
            current, fidelity, row_base - reach, depth_base - reach, rows_total, depth_total
        )
        fidelity = fidelity[1:-1, 1:-1]
    return current


def solution(mesh):
    return jax.shard_map(
        per_device,
        mesh=mesh,
        in_specs=(P(None, "gz", "gy"), P(), P(None, "gz"), P(None, "gz"), P(None, "gy", None)),
        out_specs=P("gy", "gz", None),
        check_vma=False,
    )
```

```python
import functools
import math

import jax
import jax.numpy as jnp
from jax import lax
from jax.experimental import pallas as pl
from jax.experimental.pallas import tpu as pltpu
from jax.sharding import PartitionSpec as P

X = 4096
P_SIZE = 16
NANG = 3600
BLOCK = 64
LANES = 128
GATHER_CHUNKS = 2
PER_STEP = 16
ITERS = 2


step_length = 0.25
smooth_weight = 0.3
gradient_floor = 0.01
shift_reach = 8.0


def with_halo(cells, sides, width):
    for axis, dim in sides:
        count = lax.axis_size(axis)
        ends = count - 1
        head = lax.slice_in_dim(cells, 0, width, axis=dim)
        tail = lax.slice_in_dim(cells, cells.shape[dim] - width, cells.shape[dim], axis=dim)
        cells = jnp.concatenate(
            [
                lax.ppermute(tail, axis, [(i, (i + 1) % count) for i in range(ends)]),
                cells,
                lax.ppermute(head, axis, [((i + 1) % count, i) for i in range(ends)]),
            ],
            axis=dim,
        )
    return cells


def gather_kernel(count, local_ref, out_ref, send_sem, recv_sem, own_sem):
    ring = count // 2
    forward_steps = ring // 2
    backward_steps = ring - 1 - forward_steps
    me = lax.axis_index("gy")
    depth_index = lax.axis_index("gz")
    half = me // ring
    place = me % ring
    width = local_ref.shape[2]
    mesh_kind = pl.DeviceIdType.MESH

    def device(half_of, place_of):
        return half_of * ring + lax.rem(place_of + 2 * ring, ring)

    partner = device(1 - half, place)
    right = device(half, place + 1)
    left = device(half, place - 1)

    chunks = GATHER_CHUNKS
    chunk_rows = local_ref.shape[0] // chunks

    def rows_of(chunk):
        return pl.ds(chunk * chunk_rows, chunk_rows)

    def slot(index, chunk):
        columns = pl.ds(pl.multiple_of(index * width, width), width)
        return out_ref.at[rows_of(chunk), :, columns]

    barrier = pltpu.get_barrier_semaphore()
    for peer in (partner, right, left):
        pl.semaphore_signal(barrier, inc=1, device_id=(depth_index, peer), device_id_type=mesh_kind)
    pl.semaphore_wait(barrier, 3)

    own = pltpu.make_async_copy(local_ref, out_ref.at[:, :, pl.ds(pl.multiple_of(me * width, width), width)], own_sem)
    own.start()
    sends = []

    def send(source, index, chunk, peer):
        copy = pltpu.make_async_remote_copy(
            src_ref=source,
            dst_ref=slot(index, chunk),
            send_sem=send_sem.at[len(sends)],
            recv_sem=recv_sem.at[index, chunk],
            device_id=(depth_index, peer),
            device_id_type=mesh_kind,
        )
        copy.start()
        sends.append(copy)

    def arrived(index, chunk):
        pltpu.make_async_remote_copy(
            src_ref=local_ref.at[rows_of(chunk)],
            dst_ref=slot(index, chunk),
            send_sem=send_sem.at[0],
            recv_sem=recv_sem.at[index, chunk],
            device_id=(depth_index, partner),
            device_id_type=mesh_kind,
        ).wait_recv()

    for chunk in range(chunks):
        send(local_ref.at[rows_of(chunk)], me, chunk, partner)
    for step in range(1, forward_steps + 1):
        for chunk in range(chunks):
            for direction, peer, limit in ((-1, right, forward_steps), (1, left, backward_steps)):
                if step > limit:
                    continue
                if step == 1:
                    send(local_ref.at[rows_of(chunk)], me, chunk, peer)
                    if direction == -1:
                        arrived(partner, chunk)
                    send(slot(partner, chunk), partner, chunk, peer)
                    continue
                for half_of in (0, 1):
                    index = device(half_of, place + direction * (step - 1))
                    arrived(index, chunk)
                    send(slot(index, chunk), index, chunk, peer)
    for direction, steps in ((-1, forward_steps), (1, backward_steps)):
        for half_of in (0, 1):
            for chunk in range(chunks):
                arrived(device(half_of, place + direction * steps), chunk)
    own.wait()
    for copy in sends:
        copy.wait_send()


def gather_columns(local):
    count = lax.axis_size("gy")
    rows, depth, width = local.shape
    return pl.pallas_call(
        functools.partial(gather_kernel, count),
        out_shape=jax.ShapeDtypeStruct((rows, depth, width * count), local.dtype),
        in_specs=[pl.BlockSpec(memory_space=pl.ANY)],
        out_specs=pl.BlockSpec(memory_space=pl.ANY),
        scratch_shapes=[
            pltpu.SemaphoreType.DMA((count * GATHER_CHUNKS,)),
            pltpu.SemaphoreType.DMA((count, GATHER_CHUNKS)),
            pltpu.SemaphoreType.DMA(()),
        ],
        compiler_params=pltpu.CompilerParams(collective_id=0, has_side_effects=True),
    )(local)


STEPS = ((1, 1), (1, 0), (1, -1), (0, 1), (0, -1), (-1, 1), (-1, 0), (-1, -1))


def halo_kernel(count, width, cells_ref, *refs):
    pieces = len(STEPS)
    targets = refs[:pieces]
    send_sem, recv_sem = refs[pieces], refs[pieces + 1]
    row_count, depth_count = count
    rows, depth = cells_ref.shape[0], cells_ref.shape[1]
    row_parts = {1: pl.ds(rows - width, width), 0: pl.ds(0, rows), -1: pl.ds(0, width)}
    depth_parts = {1: pl.ds(depth - width, width), 0: pl.ds(0, depth), -1: pl.ds(0, width)}
    row_me = lax.axis_index("gy")
    depth_me = lax.axis_index("gz")
    peers = [
        (lax.rem(depth_me + depth_step + depth_count, depth_count),
         lax.rem(row_me + row_step + row_count, row_count))
        for row_step, depth_step in STEPS
    ]
    barrier = pltpu.get_barrier_semaphore()
    for peer in peers:
        pl.semaphore_signal(barrier, inc=1, device_id=peer, device_id_type=pl.DeviceIdType.MESH)
    pl.semaphore_wait(barrier, pieces)
    copies = []
    for k, peer in enumerate(peers):
        row_step, depth_step = STEPS[k]
        copy = pltpu.make_async_remote_copy(
            src_ref=cells_ref.at[row_parts[row_step], depth_parts[depth_step]],
            dst_ref=targets[k],
            send_sem=send_sem.at[k],
            recv_sem=recv_sem.at[k],
            device_id=peer,
            device_id_type=pl.DeviceIdType.MESH,
        )
        copy.start()
        copies.append(copy)
    for copy in copies:
        copy.wait()


def with_wide_halo(cells, width):
    rows, depth = cells.shape[0], cells.shape[1]
    count = (lax.axis_size("gy"), lax.axis_size("gz"))
    row_parts = {1: slice(rows - width, rows), 0: slice(None), -1: slice(0, width)}
    depth_parts = {1: slice(depth - width, depth), 0: slice(None), -1: slice(0, width)}
    sent = [cells[row_parts[r], depth_parts[d]] for r, d in STEPS]
    received = pl.pallas_call(
        functools.partial(halo_kernel, count, width),
        out_shape=[jax.ShapeDtypeStruct(piece.shape, piece.dtype) for piece in sent],
        in_specs=[pl.BlockSpec(memory_space=pl.ANY)],
        out_specs=[pl.BlockSpec(memory_space=pl.ANY)] * len(STEPS),
        scratch_shapes=[
            pltpu.SemaphoreType.DMA((len(STEPS),)),
            pltpu.SemaphoreType.DMA((len(STEPS),)),
        ],
        compiler_params=pltpu.CompilerParams(collective_id=1, has_side_effects=True),
    )(cells)
    parts = dict(zip(STEPS, received))
    parts[(0, 0)] = cells
    bands = [
        jnp.concatenate([parts[(r, 1)], parts[(r, 0)], parts[(r, -1)]], axis=1) for r in (1, 0, -1)
    ]
    return jnp.concatenate(bands, axis=0)


def geometry(angle_value):
    radians = 2.0 * math.pi * angle_value.astype(jnp.float32) / NANG
    stretch = 0.5 + 0.5 * jnp.abs(jnp.cos(radians))
    spread = 1.0 + jnp.abs(jnp.sin(radians))
    return (radians, stretch, spread)


def footprint(radians, stretch, spread, row_global, rows_total, block_size):
    shifted = shift_reach * jnp.sin(radians + 2.0 * math.pi * row_global / rows_total)
    inside = jnp.arange(block_size).astype(jnp.float32) - 0.5 * (block_size - 1)
    centre = block_size + inside[None, :] * stretch + shifted[:, None]
    places = jnp.arange(2 * block_size).astype(jnp.float32) + 0.5
    weights = (
        jnp.maximum(0.0, 1.0 - jnp.abs(places[None, None, :] - centre[:, :, None]) / spread)
        / spread
    )
    return weights.astype(jnp.bfloat16)


def axial_table(offsets, lengths, depth_count):
    offset_real = offsets.astype(jnp.float32)[..., None]
    length_real = lengths.astype(jnp.float32)[..., None]
    depth_place = jnp.arange(depth_count).astype(jnp.float32) + 0.5
    centre = offset_real + depth_place * length_real / depth_count
    row_number = jnp.arange(2 * depth_count)
    row_place = row_number.astype(jnp.float32) + 0.5
    triangle = jnp.maximum(0.0, 1.0 - jnp.abs(row_place - centre[..., None]))
    inside = (row_number >= offsets[..., None, None]) & (
        row_number < (offsets + lengths)[..., None, None]
    )
    return jnp.where(inside, triangle, 0.0).astype(jnp.bfloat16)


def smooth_update(current, fidelity, row_first, depth_first, rows_total, depth_total):
    row_index = row_first + jnp.arange(current.shape[0])
    depth_index = depth_first + jnp.arange(current.shape[1])
    keep_rows = ((row_index >= 0) & (row_index < rows_total - 1)).astype(jnp.float32)[:, None, None]
    keep_depth = ((depth_index >= 0) & (depth_index < depth_total - 1)).astype(jnp.float32)[
        None, :, None
    ]
    forward_rows = (
        jnp.concatenate([current[1:] - current[:-1], jnp.zeros_like(current[:1])], 0) * keep_rows
    )
    forward_depth = (
        jnp.concatenate([current[:, 1:] - current[:, :-1], jnp.zeros_like(current[:, :1])], 1)
        * keep_depth
    )
    forward_width = jnp.concatenate(
        [current[:, :, 1:] - current[:, :, :-1], jnp.zeros_like(current[:, :, :1])], 2
    )
    inverse = lax.rsqrt(
        forward_rows * forward_rows
        + forward_depth * forward_depth
        + forward_width * forward_width
        + gradient_floor
    )
    normal_rows = forward_rows * inverse
    normal_depth = forward_depth * inverse
    normal_width = forward_width * inverse
    divergence = normal_rows - jnp.concatenate(
        [jnp.zeros_like(normal_rows[:1]), normal_rows[:-1]], 0
    )
    divergence = (
        divergence
        + normal_depth
        - jnp.concatenate([jnp.zeros_like(normal_depth[:, :1]), normal_depth[:, :-1]], 1)
    )
    divergence = (
        divergence
        + normal_width
        - jnp.concatenate([jnp.zeros_like(normal_width[:, :, :1]), normal_width[:, :, :-1]], 2)
    )
    return current + step_length * (smooth_weight * divergence - (current - fidelity))


def footprint_mats(angle_value, row_global, rows_total):
    radians, stretch, spread = geometry(angle_value)
    shifted = shift_reach * jnp.sin(radians + 2.0 * math.pi * row_global / rows_total)
    inside = jnp.arange(BLOCK).astype(jnp.float32) - 0.5 * (BLOCK - 1)
    centre = BLOCK + inside[None, :] * stretch + shifted[:, None]
    centre = jnp.concatenate([centre, centre], axis=1)
    places = jnp.arange(LANES).astype(jnp.float32)[:, None] + 0.5
    weights = (
        jnp.maximum(0.0, 1.0 - jnp.abs(places[None] - centre[:, None, :]) / spread) / spread
    )
    return weights.astype(jnp.bfloat16)


def backproject_kernel(shift_ref, columns_ref, mats_ref, out_ref, tiles_ref):
    p = pl.program_id(0)
    tile_count = out_ref.shape[2] // LANES
    depth_count = out_ref.shape[1]

    @pl.when(p == 0)
    def _():
        out_ref[...] = jnp.zeros_like(out_ref)
        tiles_ref[...] = jnp.zeros_like(tiles_ref)

    for step in range(PER_STEP):
        for tile in range(tile_count):
            tiles_ref[0, tile + 1] = columns_ref[step, :, tile * LANES:(tile + 1) * LANES].astype(
                jnp.float32
            )

        ends = jnp.concatenate([tiles_ref[0, 1], tiles_ref[0, tile_count]], axis=0).astype(jnp.bfloat16)
        second_half = lax.broadcasted_iota(jnp.int32, (LANES, LANES), 1) >= BLOCK
        empty = jnp.zeros((BLOCK, LANES), jnp.bfloat16)
        for row in range(out_ref.shape[0]):
            shift = shift_ref[p * PER_STEP + step, row, 2] - 2
            start = (shift + 2) // 2
            odd = jnp.full((LANES, LANES), shift - 2 * (start - 1), jnp.int32) == 1
            whole = mats_ref[step, row]
            down = jnp.concatenate([empty, whole[:BLOCK]], axis=0)
            up = jnp.concatenate([whole[BLOCK:], empty], axis=0)
            nothing = jnp.zeros_like(whole)
            first = jnp.where(
                second_half, jnp.where(odd, nothing, down), jnp.where(odd, down, whole)
            )
            second = jnp.where(
                second_half, jnp.where(odd, whole, up), jnp.where(odd, up, nothing)
            )
            low = tiles_ref[0, pl.ds(start, tile_count)].reshape(tile_count * depth_count, LANES)
            high = tiles_ref[0, pl.ds(start + 1, tile_count)].reshape(tile_count * depth_count, LANES)
            taps = jnp.concatenate([low, high], axis=1).astype(jnp.bfloat16)
            result = jnp.dot(
                taps, jnp.concatenate([first, second], axis=0), preferred_element_type=jnp.float32
            )
            edge = jnp.dot(ends, whole, preferred_element_type=jnp.float32)
            shift_vec = jnp.full((depth_count, LANES), shift, jnp.int32)
            for tile in range(tile_count):
                part = result[tile * depth_count:(tile + 1) * depth_count]
                if tile == 0:
                    part = jnp.where(shift_vec < 0, edge[:depth_count], part)
                elif tile == tile_count - 2:
                    part = jnp.where(shift_vec >= 2, edge[depth_count:], part)
                elif tile == tile_count - 1:
                    part = jnp.where(shift_vec >= 0, edge[depth_count:], part)
                lanes = pl.ds(tile * LANES, LANES)
                out_ref[row, :, lanes] = out_ref[row, :, lanes] + part

    @pl.when(p == pl.num_programs(0) - 1)
    def _():
        out_ref[...] = math.pi / P_SIZE * out_ref[...]


def backproject(shifts, columns, mats):
    count, rows = shifts.shape[0], shifts.shape[1]
    depth_count, column_count = columns.shape[1], columns.shape[2]
    tile_count = column_count // LANES
    return pl.pallas_call(
        backproject_kernel,
        out_shape=jax.ShapeDtypeStruct((rows, depth_count, column_count), jnp.float32),
        grid_spec=pltpu.PrefetchScalarGridSpec(
            num_scalar_prefetch=1,
            grid=(count // PER_STEP,),
            in_specs=[
                pl.BlockSpec((PER_STEP,) + columns.shape[1:], lambda p, s: (p, 0, 0)),
                pl.BlockSpec((PER_STEP,) + mats.shape[1:], lambda p, s: (p, 0, 0, 0)),
            ],
            out_specs=pl.BlockSpec((rows, depth_count, column_count), lambda p, s: (0, 0, 0)),
            scratch_shapes=[pltpu.VMEM((1, tile_count + 3, depth_count, LANES), jnp.float32)],
        ),
        compiler_params=pltpu.CompilerParams(dimension_semantics=("arbitrary",)),
    )(shifts, columns, mats)


def smooth_inner(current, fidelity, row_first, depth_first, rows_total, depth_total):
    row_index = row_first + jnp.arange(current.shape[0])
    depth_index = depth_first + jnp.arange(current.shape[1])
    keep_rows = ((row_index >= 0) & (row_index < rows_total - 1)).astype(jnp.float32)[:, None, None]
    keep_depth = ((depth_index >= 0) & (depth_index < depth_total - 1)).astype(jnp.float32)[
        None, :, None
    ]
    rows_here, rows_before = keep_rows[1:-1], keep_rows[:-2]
    depth_here, depth_before = keep_depth[:, 1:-1], keep_depth[:, :-2]

    def across(cells):
        return jnp.concatenate([cells[:, :, 1:] - cells[:, :, :-1], jnp.zeros_like(cells[:, :, :1])], 2)

    centre = current[1:-1, 1:-1]
    row_next, row_prev = current[2:, 1:-1], current[:-2, 1:-1]
    depth_next, depth_prev = current[1:-1, 2:], current[1:-1, :-2]
    prev_row_next_depth = current[:-2, 2:]
    next_row_prev_depth = current[2:, :-2]

    def inverse(a, b, c):
        return lax.rsqrt(a * a + b * b + c * c + gradient_floor)

    rows_d = (row_next - centre) * rows_here
    depth_d = (depth_next - centre) * depth_here
    width_d = across(centre)
    scale = inverse(rows_d, depth_d, width_d)
    prev_rows_d = (centre - row_prev) * rows_before
    prev_scale = inverse(prev_rows_d, (prev_row_next_depth - row_prev) * depth_here, across(row_prev))
    prev_depth_d = (centre - depth_prev) * depth_before
    low_scale = inverse(
        (next_row_prev_depth - depth_prev) * rows_here, prev_depth_d, across(depth_prev)
    )
    width_n = width_d * scale
    divergence = rows_d * scale - prev_rows_d * prev_scale
    divergence = divergence + depth_d * scale - prev_depth_d * low_scale
    divergence = divergence + width_n - jnp.concatenate(
        [jnp.zeros_like(width_n[:, :, :1]), width_n[:, :, :-1]], 2
    )
    return centre + step_length * (smooth_weight * divergence - (centre - fidelity[1:-1, 1:-1]))


def per_device(filtered, angle_index, band_offset, band_length, foot_block):
    depth_count = filtered.shape[1]
    row_count = foot_block.shape[1]
    extended_band = with_halo(filtered, (("gz", 1),), depth_count // 2)
    axial_weights = axial_table(band_offset[:, 0], band_length[:, 0], depth_count)
    summed_rows = jnp.einsum(
        "pzv,pvu->pzu",
        axial_weights,
        extended_band,
        preferred_element_type=jnp.float32,
    )
    columns = gather_columns(summed_rows.astype(jnp.bfloat16))
    column_count = columns.shape[2]
    row_base = lax.axis_index("gy") * row_count
    depth_base = lax.axis_index("gz") * depth_count
    rows_total = lax.axis_size("gy") * row_count
    depth_total = lax.axis_size("gz") * depth_count
    row_global = (row_base + jnp.arange(row_count)).astype(jnp.float32)
    mats = jax.vmap(footprint_mats, in_axes=(0, None, None))(angle_index, row_global, rows_total)
    backprojection = backproject(foot_block, columns, mats)
    current = backprojection
    extended = with_wide_halo(backprojection, ITERS)
    fidelity = extended
    current = extended
    for turn_index in range(ITERS):
        reach = ITERS - turn_index
        current = smooth_inner(
            current, fidelity, row_base - reach, depth_base - reach, rows_total, depth_total
        )
        fidelity = fidelity[1:-1, 1:-1]
    return current


def solution(mesh):
    return jax.shard_map(
        per_device,
        mesh=mesh,
        in_specs=(P(None, "gz", "gy"), P(), P(None, "gz"), P(None, "gz"), P(None, "gy", None)),
        out_specs=P("gy", "gz", None),
        check_vma=False,
    )
```
